32 devices in a mesh: dp: 8 (over y, x, core), tensor: 4 (over z).
Axes of the slice: x: 2, y: 2, z: 4, core: 2. Of those that a mesh axis runs over, the one named last changes fastest.
Arguments:
- tokens: bfloat16 [8192, 2048], P(('dp', 'tensor')), may hold values from -6 to 6
- cotangent: bfloat16 [8192, 2048], P(('dp', 'tensor')), may hold values from -6 to 6
- routes: int32 [8192, 2], P('dp'), may hold values from 0 to 7, all different within a row
- block_ids: int32 [8, 1024], P('dp'), may hold values from 0 to 7, never falling along the last dimension, each value on 1 to 256 neighbouring positions
- attn_gain: bfloat16 [2048], P('dp'), may hold values from 0.25 to 1.75
- q_gain: bfloat16 [2048], P('dp'), may hold values from 0.25 to 1.75
- k_gain: bfloat16 [2048], P('dp'), may hold values from 0.25 to 1.75
- w_query: bfloat16 [2048, 2048], P('dp', 'tensor'), may hold values from -0.125 to 0.125
- w_key: bfloat16 [2048, 2048], P('dp', 'tensor'), may hold values from -0.125 to 0.125
- w_value: bfloat16 [2048, 2048], P('dp', 'tensor'), may hold values from -0.125 to 0.125
- w_out: bfloat16 [2048, 2048], P('tensor', 'dp'), may hold values from -1.5 to 1.5
- ffn_gain: bfloat16 [2048], P('dp'), may hold values from 0.25 to 1.75
- w_router: bfloat16 [2048, 8], P('dp'), may hold values from -0.25 to 0.25
- w_gate: bfloat16 [8, 2048, 1024], P(None, 'dp', 'tensor'), may hold values from -0.125 to 0.125
- w_up: bfloat16 [8, 2048, 1024], P(None, 'dp', 'tensor'), may hold values from -0.125 to 0.125
- w_down: bfloat16 [8, 1024, 2048], P(None, 'tensor', 'dp'), may hold values from -1.5 to 1.5
Outputs:
- output: bfloat16 [8192, 2048], P(('dp', 'tensor'))
- grad_tokens: float32 [8192, 2048], P(('dp', 'tensor'))
- grad_attn_gain: float32 [2048], P(('dp', 'tensor'))
- grad_q_gain: float32 [2048], P(('dp', 'tensor'))
- grad_k_gain: float32 [2048], P(('dp', 'tensor'))
- grad_query: float32 [2048, 2048], P('dp', 'tensor')
- grad_key: float32 [2048, 2048], P('dp', 'tensor')
- grad_value: float32 [2048, 2048], P('dp', 'tensor')
- grad_out: float32 [2048, 2048], P('tensor', 'dp')
- grad_ffn_gain: float32 [2048], P(('dp', 'tensor'))
- grad_router: float32 [2048, 8], P('dp')
- grad_gate: float32 [8, 2048, 1024], P(None, 'dp', 'tensor')
- grad_up: float32 [8, 2048, 1024], P(None, 'dp', 'tensor')
- grad_down: float32 [8, 1024, 2048], P(None, 'tensor', 'dp')
The draws below stay inside these ranges and needn't reach their ends.
Inputs may be any that keep to these rules, and one draw needn't show every extreme that they name: `routes`: each row names 2 different experts, and every expert is named by some row. `block_ids`: along each sequence the block ids start at 0, never fall and rise by one at a time; a block holds 1 to 256 positions and one block holds exactly 256.
All inputs are finite; a program needn't handle non-finite values.
Results may differ from the reference program's by a relative error of at most 0.03.
Values may be sent and summed in bfloat16 or wider, within the bound.
A program may use at most 320 MiB of HBM per device.

```python
import math
import jax
import jax.numpy as jnp
import numpy as np
from jax import lax

D = 2048
HEADS = 16
HEAD_DIM = 128
FF = 1024
EXPERTS = 8
TOPK = 2
SEQ = 1024
QROWS = 512
BLOCK = 256
SEQS = 8
TOKENS = 8192
CAP = 320


def levels(stream_key, extent, cuts, least, top_value):
    level, own = 1.0, jax.random.fold_in(stream_key, 6)
    for dim, parts in cuts:
        heights = jnp.exp(jax.random.uniform(jax.random.fold_in(own, dim), (parts,), jnp.float32, least / len(cuts), top_value / len(cuts)))
        level = level * jnp.repeat(heights, extent[dim] // parts).reshape([-1 if axis == dim else 1 for axis in range(len(extent))])
    return level


def distinct(own_key, rows, number_of, top, lift):
    sequence = jax.random.permutation(jax.random.fold_in(own_key, 1), number_of)
    boost = sequence
    for power in range(3):
        boost = boost * boost // number_of
    boost = boost * lift // number_of
    chance = jax.random.randint(jax.random.fold_in(own_key, 2), (rows, number_of), 0, 4096) + boost
    fixed_rows = jax.random.permutation(jax.random.fold_in(own_key, 3), rows)[jnp.arange(number_of) % rows]
    chance = jnp.where(jnp.arange(rows)[:, None] == fixed_rows[None, :], 1 << 14, chance)
    merit = chance * number_of + jnp.arange(number_of)
    return lax.top_k(merit.astype(jnp.int32), top)[1].astype(jnp.int32)


def split_up(count, total, bound, slope):
    loads = [(1 << 20) // math.isqrt(standing ** slope) + 1 for standing in range(2, count + 1)]
    spare, counts = total - bound - (count - 1), [1] * (count - 1)
    while spare > 0:
        free = [i for i in range(count - 1) if counts[i] < bound]
        mass, left = sum([loads[i] for i in free]), spare
        for i in free:
            addition = min(bound - counts[i], max(1, left * loads[i] // mass), spare)
            counts[i] = counts[i] + addition
            spare = spare - addition
    return np.array([bound] + counts)


def uneven(stream_key, number_of, total, reach, lean):
    if number_of == 2:
        one = jax.random.randint(stream_key, (), max(1, total - reach), min(reach, total - 1) + 1)
        return jnp.stack([one, total - one])
    tallies = jnp.asarray(split_up(number_of, total, reach, lean), jnp.int32)
    pairs = (number_of - 1) // 2
    giver, receiver = tallies[1:1 + 2 * pairs:2], tallies[2:2 + 2 * pairs:2]
    room = jnp.minimum(giver - 1, reach - receiver)
    moved = jax.random.randint(jax.random.fold_in(stream_key, 1), (pairs,), 0, 1 << 20) % (room + 1)
    tallies = tallies.at[1:1 + 2 * pairs:2].set(giver - moved).at[2:2 + 2 * pairs:2].set(receiver + moved)
    return tallies[jax.random.permutation(jax.random.fold_in(stream_key, 2), number_of)]


def noise(stream_key, extent, spread, reach, shards=(), kind=jnp.bfloat16):
    values = jax.random.normal(stream_key, extent, jnp.float32) * spread
    if len(shards) > 0:
        values = levels(stream_key, extent, shards, -0.22, 0.18) * values
    return jnp.clip(values, min=-reach, max=reach).astype(kind)


def setup_inputs(seed: int = 0) -> dict:
    splits = jax.random.split(jax.random.key(seed), 17)
    return {
        "tokens": noise(splits[0], (TOKENS, D), 1.0, 6.0, ((0, 32),)),
        "cotangent": noise(splits[1], (TOKENS, D), 1.0, 6.0, ((0, 32),)),
        "routes": distinct(splits[2], TOKENS, EXPERTS, TOPK, 2048),
        "block_ids": jax.vmap(lambda own: jnp.searchsorted(jnp.cumsum(uneven(own, 2 * SEQ // BLOCK, SEQ, BLOCK, 0)), jnp.arange(SEQ), side="right"))(jax.random.split(splits[3], SEQS)).reshape((SEQS, SEQ)).astype(jnp.int32),
        "attn_gain": jnp.clip(1.0 + 0.15 * jax.random.normal(splits[4], (D,), jnp.float32), 0.25, 1.75).astype(jnp.bfloat16),
        "q_gain": jnp.clip(1.0 + 0.15 * jax.random.normal(splits[5], (D,), jnp.float32), 0.25, 1.75).astype(jnp.bfloat16),
        "k_gain": jnp.clip(1.0 + 0.15 * jax.random.normal(splits[6], (D,), jnp.float32), 0.25, 1.75).astype(jnp.bfloat16),
        "w_query": noise(splits[7], (D, D), D ** -0.5, 0.125, ((0, 8), (1, 4))),
        "w_key": noise(splits[8], (D, D), D ** -0.5, 0.125, ((0, 8), (1, 4))),
        "w_value": noise(splits[9], (D, D), D ** -0.5, 0.125, ((0, 8), (1, 4))),
        "w_out": noise(splits[10], (D, D), (D // 128) ** -0.5, 1.5, ((0, 4), (1, 8))),
        "ffn_gain": jnp.clip(1.0 + 0.15 * jax.random.normal(splits[11], (D,), jnp.float32), 0.25, 1.75).astype(jnp.bfloat16),
        "w_router": noise(splits[12], (D, EXPERTS), (D // 4) ** -0.5, 0.25, ((0, 8),)),
        "w_gate": noise(splits[13], (EXPERTS, D, FF), D ** -0.5, 0.125, ((1, 8), (2, 4))),
        "w_up": noise(splits[14], (EXPERTS, D, FF), D ** -0.5, 0.125, ((1, 8), (2, 4))),
        "w_down": noise(splits[15], (EXPERTS, FF, D), (FF // 64) ** -0.5, 1.5, ((1, 4), (2, 8))),
    }


@jax.custom_vjp
def low(v):
    return lax.optimization_barrier(v.astype(jnp.bfloat16)).astype(jnp.float32)

@jax.custom_vjp
def low_back(v):
    return v

def low_keep(v):
    return (low(v), None)

def low_pass(kept, grad):
    return (grad,)

def back_keep(v):
    return (v, None)

def back_low(kept, grad):
    return (low(grad),)
low.defvjp(low_keep, low_pass)
low_back.defvjp(back_keep, back_low)
EPSILON = 1e-05
MASKED = -1e+30
HIGHEST = lax.Precision.HIGHEST

def matmul(left_side, right_side):
    return jnp.dot(left_side, right_side, precision=HIGHEST, preferred_element_type=jnp.float32)

def rms_scale(source):
    return source * lax.rsqrt(lax.optimization_barrier(jnp.mean(source * source, axis=-1, keepdims=True)) + EPSILON)

def rope_tables(seq_len, head_dim):
    half_dim = head_dim // 2
    frequency = jnp.exp(-math.log(10000.0) * 2.0 * jnp.arange(half_dim, dtype=jnp.float32) / head_dim)
    angles = jnp.arange(seq_len, dtype=jnp.float32)[:, None] * frequency[None, :]
    return (jnp.concatenate([jnp.cos(angles)] * 2, axis=1), jnp.concatenate([jnp.sin(angles)] * 2, axis=1))

def rotate(heads_in, cosine_table, sine_table):
    half_dim = heads_in.shape[-1] // 2
    turned = jnp.concatenate([-heads_in[..., half_dim:], heads_in[..., :half_dim]], axis=-1)
    return heads_in * cosine_table[:, None, :] + turned * sine_table[:, None, :]

def claim_slots(route_rows):
    seq_len = route_rows.shape[0]
    flat_routes = route_rows.reshape(-1)
    pair_count = flat_routes.shape[0]
    onehot = (flat_routes[:, None] == jnp.arange(EXPERTS, dtype=jnp.int32)[None, :]).astype(jnp.int32)
    earlier = jnp.cumsum(onehot, axis=0) - onehot
    place_index = lax.optimization_barrier(jnp.sum(earlier * onehot, axis=1))
    kept_pair = place_index < CAP
    slot_index = jnp.where(kept_pair, flat_routes * CAP + place_index, EXPERTS * CAP).astype(jnp.int32)
    pair_index = jnp.arange(pair_count, dtype=jnp.int32)
    filler = jnp.full((EXPERTS * CAP + 1,), pair_count, jnp.int32).at[slot_index].set(pair_index)
    slot_pair = filler[:EXPERTS * CAP]
    slot_owner = jnp.where(slot_pair < pair_count, slot_pair // TOPK, seq_len).astype(jnp.int32)
    return (slot_index, slot_pair, slot_owner)

def attention(q_rot, k_rot, value_heads, block_row):
    seq_len = q_rot.shape[0]
    blocks = seq_len // QROWS
    score_scale = HEAD_DIM ** (-0.5)
    q_blocks = q_rot.reshape(blocks, QROWS, HEADS, HEAD_DIM)
    id_blocks = block_row.reshape(blocks, QROWS)

    def attend_block(block_item):
        q_block, id_block = block_item
        scores = jnp.einsum('qhd,khd->hqk', q_block, k_rot, precision=HIGHEST) * score_scale
        allowed = block_row[None, None, :] <= id_block[None, :, None]
        scores = low_back(jnp.where(allowed, scores, MASKED))
        weights = jax.nn.softmax(scores, axis=-1)
        mixed_block = jnp.einsum('hqk,khd->qhd', low(weights), value_heads, precision=HIGHEST)
        return mixed_block.reshape(QROWS, HEADS * HEAD_DIM)
    return lax.map(jax.checkpoint(attend_block), (q_blocks, id_blocks)).reshape(seq_len, HEADS * HEAD_DIM)

def sequence_layer(params, source, route_row, block_row, cosine_table, sine_table):
    attn_gain, q_gain, k_gain, w_query, w_key, w_value, w_out, ffn_gain, w_router, w_gate, w_up, w_down = params
    seq_len = source.shape[0]
    model_width = source.shape[1]
    slots = claim_slots(route_row)
    slot_pair = slots[1]
    slot_owner = slots[2]
    normed = low(rms_scale(source) * attn_gain)
    query_proj = low_back(matmul(normed, w_query))
    key_proj = low_back(matmul(normed, w_key))
    value_proj = low_back(low(matmul(normed, w_value)))
    query_normed = rms_scale(query_proj) * q_gain
    key_normed = rms_scale(key_proj) * k_gain
    q_rot = low(rotate(query_normed.reshape(seq_len, HEADS, HEAD_DIM), cosine_table, sine_table))
    k_rot = low(rotate(key_normed.reshape(seq_len, HEADS, HEAD_DIM), cosine_table, sine_table))
    mixed_heads = low_back(low(attention(q_rot, k_rot, value_proj.reshape(seq_len, HEADS, HEAD_DIM), block_row)))
    attn_branch = low_back(matmul(mixed_heads, w_out))
    middle = source + attn_branch
    normed_two = low(rms_scale(middle) * ffn_gain)
    logits = low_back(matmul(normed_two, w_router))
    router_probs = jax.nn.softmax(logits, axis=-1)
    chosen = jnp.take_along_axis(router_probs, route_row, axis=1)
    gate_slot = jnp.concatenate([chosen.reshape(-1), jnp.zeros((1,), chosen.dtype)])[slot_pair]
    padded = jnp.concatenate([normed_two, jnp.zeros((1, model_width), normed_two.dtype)])
    dispatched = padded[slot_owner].reshape(EXPERTS, CAP, model_width)
    gate_part = low_back(jnp.einsum('ecd,edf->ecf', dispatched, w_gate, precision=HIGHEST))
    up_part = low_back(jnp.einsum('ecd,edf->ecf', dispatched, w_up, precision=HIGHEST))
    hidden = low(jax.nn.silu(gate_part) * up_part)
    expert_out = low_back(jnp.einsum('ecf,efd->ecd', hidden, w_down, precision=HIGHEST))
    weighted = expert_out.reshape(EXPERTS * CAP, model_width) * gate_slot[:, None]
    combined = jax.ops.segment_sum(weighted, slot_owner, num_segments=seq_len + 1)[:seq_len]
    return middle + combined

def reference(tokens, cotangent, routes, block_ids, attn_gain, q_gain, k_gain, w_query, w_key, w_value, w_out, ffn_gain, w_router, w_gate, w_up, w_down):
    params = tuple((weight.astype(jnp.float32) for weight in (attn_gain, q_gain, k_gain, w_query, w_key, w_value, w_out, ffn_gain, w_router, w_gate, w_up, w_down)))
    model_width = tokens.shape[1]
    source = tokens.astype(jnp.float32).reshape(SEQS, SEQ, model_width)
    route_rows = routes.reshape(SEQS, SEQ, TOPK)
    cosine_table, sine_table = rope_tables(SEQ, HEAD_DIM)

    def forward(source_all, weights_all):

        def per_sequence(scan_carry, seq_item):
            return (scan_carry, sequence_layer(weights_all, seq_item[0], seq_item[1], seq_item[2], cosine_table, sine_table))
        carry_out, result = lax.scan(jax.checkpoint(per_sequence), jnp.zeros((), jnp.float32), (source_all, route_rows, block_ids))
        return result
    result, pullback = jax.vjp(forward, source, params)
    grad_source, grad_params = pullback(cotangent.astype(jnp.float32).reshape(SEQS, SEQ, model_width))
    return (result.reshape(TOKENS, model_width).astype(jnp.bfloat16), grad_source.reshape(TOKENS, model_width), grad_params[0], grad_params[1], grad_params[2], grad_params[3], grad_params[4], grad_params[5], grad_params[6], grad_params[7], grad_params[8], grad_params[9], grad_params[10], grad_params[11])
```

```python
import math

import jax
import jax.numpy as jnp
from jax import lax
from jax.sharding import PartitionSpec as P

HEAD_DIM = 128
EXPERTS = 8
TOPK = 2
QROWS = 512
CAP = 320


EPSILON = 1e-05
MASKED = -1e30


def rms_scale(source):
    return source * lax.rsqrt(jnp.mean(source * source, axis=-1, keepdims=True) + EPSILON)


def norm_back(source, gain_vec, grad_out):
    inverse = lax.rsqrt(jnp.mean(source * source, axis=-1, keepdims=True) + EPSILON)
    normed = source * inverse
    grad_gain = jnp.sum(grad_out * normed, axis=0)
    scaled = grad_out * gain_vec
    grad_in = inverse * (scaled - normed * jnp.mean(scaled * normed, axis=-1, keepdims=True))
    return (grad_in, grad_gain)


def rope_tables(seq_len, head_dim):
    half_dim = head_dim // 2
    frequency = jnp.exp(
        -math.log(10000.0) * 2.0 * jnp.arange(half_dim, dtype=jnp.float32) / head_dim
    )
    angles = jnp.arange(seq_len, dtype=jnp.float32)[:, None] * frequency[None, :]
    return (
        jnp.concatenate([jnp.cos(angles)] * 2, axis=1),
        jnp.concatenate([jnp.sin(angles)] * 2, axis=1),
    )


def rotate(heads_in, cosine_table, sine_table):
    half_dim = heads_in.shape[-1] // 2
    turned = jnp.concatenate([-heads_in[..., half_dim:], heads_in[..., :half_dim]], axis=-1)
    return heads_in * cosine_table[:, None, :] + turned * sine_table[:, None, :]


def rotate_back(grad_in, cosine_table, sine_table):
    half_dim = grad_in.shape[-1] // 2
    sined = grad_in * sine_table[:, None, :]
    turned = jnp.concatenate([sined[..., half_dim:], -sined[..., :half_dim]], axis=-1)
    return grad_in * cosine_table[:, None, :] + turned


def attend(q_rot, k_rot, value_heads, block_row):
    seq_len, heads_here, head_dim = q_rot.shape
    blocks = seq_len // QROWS
    score_scale = head_dim ** (-0.5)
    q_blocks = q_rot.reshape(blocks, QROWS, heads_here, head_dim)
    id_blocks = block_row.reshape(blocks, QROWS)

    def per_block(block_item):
        q_block, id_block = block_item
        scores = (
            jnp.einsum("qhd,khd->hqk", q_block, k_rot, preferred_element_type=jnp.float32)
            * score_scale
        )
        allowed = block_row[None, None, :] <= id_block[None, :, None]
        scores = jnp.where(allowed, scores, MASKED)
        row_top = jnp.max(scores, axis=-1, keepdims=True)
        row_sum = jnp.sum(jnp.exp(scores - row_top), axis=-1, keepdims=True)
        log_total = row_top + jnp.log(row_sum)
        weights_low = jnp.exp(scores - log_total).astype(jnp.bfloat16)
        mixed_block = jnp.einsum(
            "hqk,khd->qhd", weights_low, value_heads, preferred_element_type=jnp.float32
        )
        return (mixed_block.reshape(QROWS, heads_here * head_dim), log_total[..., 0])

    mixed_blocks, log_totals = lax.map(per_block, (q_blocks, id_blocks))
    return (mixed_blocks.reshape(seq_len, heads_here * head_dim), log_totals)


def attend_back(q_rot, k_rot, value_heads, block_row, log_totals, grad_mixed):
    seq_len, heads_here, head_dim = q_rot.shape
    blocks = seq_len // QROWS
    score_scale = head_dim ** (-0.5)
    q_blocks = q_rot.reshape(blocks, QROWS, heads_here, head_dim)
    g_blocks = grad_mixed.reshape(blocks, QROWS, heads_here, head_dim)
    id_blocks = block_row.reshape(blocks, QROWS)

    def back_block(running, block_item):
        q_block, g_block, id_block, log_block = block_item
        scores = (
            jnp.einsum("qhd,khd->hqk", q_block, k_rot, preferred_element_type=jnp.float32)
            * score_scale
        )
        allowed = block_row[None, None, :] <= id_block[None, :, None]
        scores = jnp.where(allowed, scores, MASKED)
        weights = jnp.exp(scores - log_block[..., None])
        weights_low = weights.astype(jnp.bfloat16)
        grad_weights = jnp.einsum(
            "qhd,khd->hqk", g_block, value_heads, preferred_element_type=jnp.float32
        )
        grad_scores = weights * (
            grad_weights - jnp.sum(weights * grad_weights, axis=-1, keepdims=True)
        )
        grad_low = grad_scores.astype(jnp.bfloat16)
        grad_query = (
            jnp.einsum("hqk,khd->qhd", grad_low, k_rot, preferred_element_type=jnp.float32)
            * score_scale
        )
        grad_key = (
            running[0]
            + jnp.einsum("hqk,qhd->khd", grad_low, q_block, preferred_element_type=jnp.float32)
            * score_scale
        )
        grad_value = running[1] + jnp.einsum(
            "hqk,qhd->khd", weights_low, g_block, preferred_element_type=jnp.float32
        )
        return ((grad_key, grad_value), grad_query)

    zero_heads = jnp.zeros(k_rot.shape, jnp.float32)
    sums_out, grad_query = lax.scan(
        back_block, (zero_heads, zero_heads), (q_blocks, g_blocks, id_blocks, log_totals)
    )
    return (grad_query.reshape(seq_len, heads_here, head_dim), sums_out[0], sums_out[1])


def kept_mask(route_rows):
    expert_ids = jnp.arange(EXPERTS, dtype=jnp.int32)
    first = (route_rows[:, 0:1] == expert_ids[None, :]).astype(jnp.int32)
    second = (route_rows[:, 1:2] == expert_ids[None, :]).astype(jnp.int32)
    both = first + second
    earlier = jnp.cumsum(both, axis=0) - both
    return jnp.where((both > 0) & (earlier < CAP), 1.0, 0.0).astype(jnp.float32)


def local(
    tokens,
    cotangent,
    routes,
    block_ids,
    attn_gain,
    q_gain,
    k_gain,
    w_query,
    w_key,
    w_value,
    w_out,
    ffn_gain,
    w_router,
    w_gate,
    w_up,
    w_down,
):
    shard_width = w_query.shape[0]
    head_cols = w_query.shape[1]
    ff_here = w_gate.shape[2]
    hidden_cols = EXPERTS * ff_here
    small = jnp.concatenate(
        [attn_gain[:, None], q_gain[:, None], k_gain[:, None], ffn_gain[:, None], w_router], axis=1
    )
    small = lax.all_gather(small, "dp", axis=0, tiled=True)
    w_qkv = lax.all_gather(
        jnp.concatenate([w_query, w_key, w_value], axis=1), "dp", axis=0, tiled=True
    )
    w_o_t = lax.all_gather(w_out.T, "dp", axis=0, tiled=True)
    gate_local = w_gate.transpose(1, 0, 2).reshape(shard_width, hidden_cols)
    up_local = w_up.transpose(1, 0, 2).reshape(shard_width, hidden_cols)
    down_local = w_down.transpose(2, 0, 1).reshape(shard_width, hidden_cols)
    full_gate = lax.all_gather(gate_local, "dp", axis=0, tiled=True)
    full_up = lax.all_gather(up_local, "dp", axis=0, tiled=True)
    full_down = lax.all_gather(down_local, "dp", axis=0, tiled=True)
    full_router = small[:, 4:]
    model_width = tokens.shape[1]
    local_rows = tokens.shape[0]
    tensor_rank = lax.axis_index("tensor")
    heads_here = head_cols // HEAD_DIM
    col_start = tensor_rank * head_cols
    gains = small[:, :4].astype(jnp.float32).T
    attn_scale = gains[0]
    query_scale = lax.dynamic_slice_in_dim(gains[1], col_start, head_cols)
    key_scale = lax.dynamic_slice_in_dim(gains[2], col_start, head_cols)
    ffn_scale = gains[3]
    source = tokens.astype(jnp.float32)
    normed_local = (rms_scale(source) * attn_scale).astype(jnp.bfloat16)
    normed = lax.all_gather(normed_local, "tensor", axis=0, tiled=True)
    seq_len = normed.shape[0]
    block_row = block_ids[0]
    cosine_table, sine_table = rope_tables(seq_len, HEAD_DIM)
    projected = jnp.dot(normed, w_qkv, preferred_element_type=jnp.float32)
    query_proj = projected[:, :head_cols]
    key_proj = projected[:, head_cols : 2 * head_cols]
    value_low = projected[:, 2 * head_cols :].astype(jnp.bfloat16)
    query_sq, key_sq = lax.psum(
        (jnp.sum(query_proj * query_proj, axis=1), jnp.sum(key_proj * key_proj, axis=1)), "tensor"
    )
    query_inv = lax.rsqrt(query_sq / model_width + EPSILON)[:, None]
    key_inv = lax.rsqrt(key_sq / model_width + EPSILON)[:, None]
    query_normed = query_proj * query_inv
    key_normed = key_proj * key_inv
    q_rot = rotate(
        (query_normed * query_scale).reshape(seq_len, heads_here, HEAD_DIM),
        cosine_table,
        sine_table,
    ).astype(jnp.bfloat16)
    k_rot = rotate(
        (key_normed * key_scale).reshape(seq_len, heads_here, HEAD_DIM), cosine_table, sine_table
    ).astype(jnp.bfloat16)
    value_heads = value_low.reshape(seq_len, heads_here, HEAD_DIM)
    mixed, log_totals = attend(q_rot, k_rot, value_heads, block_row)
    mixed_low = mixed.astype(jnp.bfloat16)
    attn_branch = lax.psum_scatter(
        jnp.einsum("sf,df->sd", mixed_low, w_o_t, preferred_element_type=jnp.float32).astype(
            jnp.bfloat16
        ),
        "tensor",
        scatter_dimension=0,
        tiled=True,
    ).astype(jnp.float32)
    middle = source + attn_branch
    normed_two_local = (rms_scale(middle) * ffn_scale).astype(jnp.bfloat16)
    normed_two = lax.all_gather(normed_two_local, "tensor", axis=0, tiled=True)
    grad_rows = lax.all_gather(cotangent, "tensor", axis=0, tiled=True)
    logits = jnp.dot(normed_two, full_router, preferred_element_type=jnp.float32)
    router_probs = jax.nn.softmax(logits, axis=-1)
    kept = kept_mask(routes)
    gate_values = router_probs * kept
    gates = jnp.repeat(gate_values, ff_here, axis=1)

    gate_part = jnp.dot(normed_two, full_gate, preferred_element_type=jnp.float32)
    up_part = jnp.dot(normed_two, full_up, preferred_element_type=jnp.float32)
    sigmoid_gate = jax.nn.sigmoid(gate_part)
    silu_gate = gate_part * sigmoid_gate
    hidden = silu_gate * up_part
    hidden_gated = (hidden * gates).astype(jnp.bfloat16)
    combined = jnp.einsum(
        "sk,dk->sd", hidden_gated, full_down, preferred_element_type=jnp.float32
    ).astype(jnp.bfloat16)
    back_hidden = jnp.dot(grad_rows, full_down, preferred_element_type=jnp.float32)
    gate_dot = jnp.sum((hidden * back_hidden).reshape(seq_len, EXPERTS, ff_here), axis=2)
    grad_hidden = back_hidden * gates
    grad_gate_part = (
        grad_hidden * up_part * sigmoid_gate * (1.0 + gate_part * (1.0 - sigmoid_gate))
    ).astype(jnp.bfloat16)
    grad_up_part = (grad_hidden * silu_gate).astype(jnp.bfloat16)
    grad_two_part = (
        jnp.einsum("sk,dk->sd", grad_gate_part, full_gate, preferred_element_type=jnp.float32)
        + jnp.einsum("sk,dk->sd", grad_up_part, full_up, preferred_element_type=jnp.float32)
    ).astype(jnp.bfloat16)
    grad_gate_w = jnp.einsum(
        "sd,sk->dk", normed_two, grad_gate_part, preferred_element_type=jnp.float32
    ).astype(jnp.bfloat16)
    grad_up_w = jnp.einsum(
        "sd,sk->dk", normed_two, grad_up_part, preferred_element_type=jnp.float32
    ).astype(jnp.bfloat16)
    grad_down_w = jnp.einsum(
        "sd,sk->dk", grad_rows, hidden_gated, preferred_element_type=jnp.float32
    ).astype(jnp.bfloat16)
    ffn_branch = lax.psum_scatter(
        combined, "tensor", scatter_dimension=0, tiled=True
    ).astype(jnp.float32)
    output = (middle + ffn_branch).astype(jnp.bfloat16)
    grad_probs = lax.psum(gate_dot * kept, "tensor")
    grad_logits = router_probs * (
        grad_probs - jnp.sum(router_probs * grad_probs, axis=1, keepdims=True)
    )
    logits_low = grad_logits.astype(jnp.bfloat16)
    grad_router = jnp.einsum(
        "sd,se->de", normed_two, logits_low, preferred_element_type=jnp.float32
    )
    own_logits = lax.dynamic_slice_in_dim(logits_low, tensor_rank * local_rows, local_rows)
    grad_two = lax.psum_scatter(
        grad_two_part, "tensor", scatter_dimension=0, tiled=True
    ).astype(jnp.float32) + jnp.einsum(
        "se,de->sd", own_logits, full_router, preferred_element_type=jnp.float32
    )
    grad_middle_norm, grad_ffn_gain = norm_back(middle, ffn_scale, grad_two)
    grad_middle = cotangent.astype(jnp.float32) + grad_middle_norm
    grad_attn_rows = lax.all_gather(grad_middle.astype(jnp.bfloat16), "tensor", axis=0, tiled=True)
    grad_out_w = jnp.einsum(
        "sf,sd->df", mixed_low, grad_attn_rows, preferred_element_type=jnp.float32
    ).astype(jnp.bfloat16)
    grad_mixed = jnp.dot(grad_attn_rows, w_o_t, preferred_element_type=jnp.float32).astype(
        jnp.bfloat16
    )
    grad_q_rot, grad_k_rot, grad_v = attend_back(
        q_rot,
        k_rot,
        value_heads,
        block_row,
        log_totals,
        grad_mixed.reshape(seq_len, heads_here, HEAD_DIM),
    )
    grad_query_normed = rotate_back(grad_q_rot, cosine_table, sine_table).reshape(
        seq_len, head_cols
    )
    grad_key_normed = rotate_back(grad_k_rot, cosine_table, sine_table).reshape(seq_len, head_cols)
    grad_query_gain = jnp.sum(grad_query_normed * query_normed, axis=0)
    grad_key_gain = jnp.sum(grad_key_normed * key_normed, axis=0)
    query_scaled = grad_query_normed * query_scale
    key_scaled = grad_key_normed * key_scale
    query_dot, key_dot = lax.psum(
        (jnp.sum(query_scaled * query_normed, axis=1), jnp.sum(key_scaled * key_normed, axis=1)),
        "tensor",
    )
    grad_query_proj = (
        query_inv * (query_scaled - query_normed * (query_dot / model_width)[:, None])
    ).astype(jnp.bfloat16)
    grad_key_proj = (key_inv * (key_scaled - key_normed * (key_dot / model_width)[:, None])).astype(
        jnp.bfloat16
    )
    grad_value_low = grad_v.reshape(seq_len, head_cols).astype(jnp.bfloat16)
    grad_qkv = jnp.concatenate([grad_query_proj, grad_key_proj, grad_value_low], axis=1)
    grad_qkv_w = jnp.einsum(
        "sd,sf->df", normed, grad_qkv, preferred_element_type=jnp.float32
    ).astype(jnp.bfloat16)
    grad_normed_part = jnp.einsum(
        "sf,df->sd", grad_qkv, w_qkv, preferred_element_type=jnp.float32
    ).astype(jnp.bfloat16)
    grad_normed = lax.psum_scatter(
        grad_normed_part, "tensor", scatter_dimension=0, tiled=True
    ).astype(jnp.float32)
    grad_source_norm, grad_attn_gain = norm_back(source, attn_scale, grad_normed)
    grad_source = grad_middle + grad_source_norm
    zero_cols = jnp.zeros((model_width,), jnp.float32)
    query_gain_full = lax.dynamic_update_slice_in_dim(zero_cols, grad_query_gain, col_start, 0)
    key_gain_full = lax.dynamic_update_slice_in_dim(zero_cols, grad_key_gain, col_start, 0)
    gain_sums = lax.psum_scatter(
        jnp.stack([grad_attn_gain, query_gain_full, key_gain_full, grad_ffn_gain], axis=1),
        ("dp", "tensor"),
        scatter_dimension=0,
        tiled=True,
    )
    sum_gate = lax.psum_scatter(grad_gate_w, "dp", scatter_dimension=0, tiled=True)
    sum_up = lax.psum_scatter(grad_up_w, "dp", scatter_dimension=0, tiled=True)
    sum_down = lax.psum_scatter(grad_down_w, "dp", scatter_dimension=0, tiled=True)
    sum_out = lax.psum_scatter(grad_out_w, "dp", scatter_dimension=0, tiled=True)
    sum_qkv = lax.psum_scatter(grad_qkv_w, "dp", scatter_dimension=0, tiled=True).astype(
        jnp.float32
    )
    sum_router = lax.psum_scatter(grad_router, "dp", scatter_dimension=0, tiled=True)
    grad_gate = sum_gate.reshape(shard_width, EXPERTS, ff_here).transpose(1, 0, 2)
    grad_up = sum_up.reshape(shard_width, EXPERTS, ff_here).transpose(1, 0, 2)
    grad_down = sum_down.reshape(shard_width, EXPERTS, ff_here).transpose(1, 2, 0)
    return (
        output,
        grad_source,
        gain_sums[:, 0],
        gain_sums[:, 1],
        gain_sums[:, 2],
        sum_qkv[:, :head_cols],
        sum_qkv[:, head_cols : 2 * head_cols],
        sum_qkv[:, 2 * head_cols :],
        sum_out.T.astype(jnp.float32),
        gain_sums[:, 3],
        sum_router,
        grad_gate.astype(jnp.float32),
        grad_up.astype(jnp.float32),
        grad_down.astype(jnp.float32),
    )


def solution(mesh):
    placed = (
        P(("dp", "tensor"), None),
        P(("dp", "tensor"), None),
        P("dp", None),
        P("dp", None),
        P("dp"),
        P("dp"),
        P("dp"),
        P("dp", "tensor"),
        P("dp", "tensor"),
        P("dp", "tensor"),
        P("tensor", "dp"),
        P("dp"),
        P("dp", None),
        P(None, "dp", "tensor"),
        P(None, "dp", "tensor"),
        P(None, "tensor", "dp"),
    )
    return jax.shard_map(
        local,
        mesh=mesh,
        in_specs=placed,
        out_specs=(
            P(("dp", "tensor"), None),
            P(("dp", "tensor"), None),
            P(("dp", "tensor")),
            P(("dp", "tensor")),
            P(("dp", "tensor")),
            P("dp", "tensor"),
            P("dp", "tensor"),
            P("dp", "tensor"),
            P("tensor", "dp"),
            P(("dp", "tensor")),
            P("dp", None),
            P(None, "dp", "tensor"),
            P(None, "dp", "tensor"),
            P(None, "tensor", "dp"),
        ),
        check_vma=False,
    )
```

```python
import math

import jax
import jax.numpy as jnp
from jax import lax
from jax.experimental import pallas as pl
from jax.experimental.pallas import tpu as pltpu
from jax.sharding import PartitionSpec as P

HEAD_DIM = 128
EXPERTS = 8
TOPK = 2
QROWS = 512
CAP = 320


EPSILON = 1e-05
MASKED = -1e30
MESH = pl.DeviceIdType.MESH
CHUNKS = 8


def rms_scale(source):
    return source * lax.rsqrt(jnp.mean(source * source, axis=-1, keepdims=True) + EPSILON)


def norm_back(source, gain_vec, grad_out):
    inverse = lax.rsqrt(jnp.mean(source * source, axis=-1, keepdims=True) + EPSILON)
    normed = source * inverse
    grad_gain = jnp.sum(grad_out * normed, axis=0)
    scaled = grad_out * gain_vec
    grad_in = inverse * (scaled - normed * jnp.mean(scaled * normed, axis=-1, keepdims=True))
    return (grad_in, grad_gain)


def rope_tables(seq_len, head_dim):
    half_dim = head_dim // 2
    frequency = jnp.exp(
        -math.log(10000.0) * 2.0 * jnp.arange(half_dim, dtype=jnp.float32) / head_dim
    )
    angles = jnp.arange(seq_len, dtype=jnp.float32)[:, None] * frequency[None, :]
    return (
        jnp.concatenate([jnp.cos(angles)] * 2, axis=1),
        jnp.concatenate([jnp.sin(angles)] * 2, axis=1),
    )


def rotate(heads_in, cosine_table, sine_table):
    half_dim = heads_in.shape[-1] // 2
    turned = jnp.concatenate([-heads_in[..., half_dim:], heads_in[..., :half_dim]], axis=-1)
    return heads_in * cosine_table[:, None, :] + turned * sine_table[:, None, :]


def rotate_back(grad_in, cosine_table, sine_table):
    half_dim = grad_in.shape[-1] // 2
    sined = grad_in * sine_table[:, None, :]
    turned = jnp.concatenate([sined[..., half_dim:], -sined[..., :half_dim]], axis=-1)
    return grad_in * cosine_table[:, None, :] + turned


def attend(q_rot, k_rot, value_heads, block_row):
    seq_len, heads_here, head_dim = q_rot.shape
    blocks = seq_len // QROWS
    score_scale = head_dim ** (-0.5)
    q_blocks = q_rot.reshape(blocks, QROWS, heads_here, head_dim)
    id_blocks = block_row.reshape(blocks, QROWS)

    def per_block(block_item):
        q_block, id_block = block_item
        scores = (
            jnp.einsum("qhd,khd->hqk", q_block, k_rot, preferred_element_type=jnp.float32)
            * score_scale
        )
        allowed = block_row[None, None, :] <= id_block[None, :, None]
        scores = jnp.where(allowed, scores, MASKED)
        row_top = jnp.max(scores, axis=-1, keepdims=True)
        row_sum = jnp.sum(jnp.exp(scores - row_top), axis=-1, keepdims=True)
        log_total = row_top + jnp.log(row_sum)
        weights_low = jnp.exp(scores - log_total).astype(jnp.bfloat16)
        mixed_block = jnp.einsum(
            "hqk,khd->qhd", weights_low, value_heads, preferred_element_type=jnp.float32
        )
        return (mixed_block.reshape(QROWS, heads_here * head_dim), log_total[..., 0])

    mixed_blocks, log_totals = lax.map(per_block, (q_blocks, id_blocks))
    return (mixed_blocks.reshape(seq_len, heads_here * head_dim), log_totals)


def attend_back(q_rot, k_rot, value_heads, block_row, log_totals, grad_mixed):
    seq_len, heads_here, head_dim = q_rot.shape
    blocks = seq_len // QROWS
    score_scale = head_dim ** (-0.5)
    q_blocks = q_rot.reshape(blocks, QROWS, heads_here, head_dim)
    g_blocks = grad_mixed.reshape(blocks, QROWS, heads_here, head_dim)
    id_blocks = block_row.reshape(blocks, QROWS)

    def back_block(running, block_item):
        q_block, g_block, id_block, log_block = block_item
        scores = (
            jnp.einsum("qhd,khd->hqk", q_block, k_rot, preferred_element_type=jnp.float32)
            * score_scale
        )
        allowed = block_row[None, None, :] <= id_block[None, :, None]
        scores = jnp.where(allowed, scores, MASKED)
        weights = jnp.exp(scores - log_block[..., None])
        weights_low = weights.astype(jnp.bfloat16)
        grad_weights = jnp.einsum(
            "qhd,khd->hqk", g_block, value_heads, preferred_element_type=jnp.float32
        )
        grad_scores = weights * (
            grad_weights - jnp.sum(weights * grad_weights, axis=-1, keepdims=True)
        )
        grad_low = grad_scores.astype(jnp.bfloat16)
        grad_query = (
            jnp.einsum("hqk,khd->qhd", grad_low, k_rot, preferred_element_type=jnp.float32)
            * score_scale
        )
        grad_key = (
            running[0]
            + jnp.einsum("hqk,qhd->khd", grad_low, q_block, preferred_element_type=jnp.float32)
            * score_scale
        )
        grad_value = running[1] + jnp.einsum(
            "hqk,qhd->khd", weights_low, g_block, preferred_element_type=jnp.float32
        )
        return ((grad_key, grad_value), grad_query)

    zero_heads = jnp.zeros(k_rot.shape, jnp.float32)
    sums_out, grad_query = lax.scan(
        back_block, (zero_heads, zero_heads), (q_blocks, g_blocks, id_blocks, log_totals)
    )
    return (grad_query.reshape(seq_len, heads_here, head_dim), sums_out[0], sums_out[1])


def kept_mask(route_rows):
    expert_ids = jnp.arange(EXPERTS, dtype=jnp.int32)
    first = (route_rows[:, 0:1] == expert_ids[None, :]).astype(jnp.int32)
    second = (route_rows[:, 1:2] == expert_ids[None, :]).astype(jnp.int32)
    both = first + second
    earlier = jnp.cumsum(both, axis=0) - both
    return jnp.where((both > 0) & (earlier < CAP), 1.0, 0.0).astype(jnp.float32)


def neighbour_barrier(me, count):
    barrier = pltpu.get_barrier_semaphore()

    @pl.when(me > 0)
    def _():
        pl.semaphore_signal(barrier, inc=1, device_id={"tensor": me - 1}, device_id_type=MESH)

    @pl.when(me < count - 1)
    def _():
        pl.semaphore_signal(barrier, inc=1, device_id={"tensor": me + 1}, device_id_type=MESH)

    pl.semaphore_wait(
        barrier, jnp.minimum(me, 1).astype(jnp.int32) + jnp.minimum(count - 1 - me, 1)
    )


def line_exchange(
    count, chunks, rows, width, part, extras, out_shapes, epilogue, gather, collective_id, prologue=None
):
    reduce = part is not None
    n_extra = len(extras)
    n_out = len(out_shapes)
    last = count - 1
    back_lag = 2 if reduce else 0
    pass_lag = (back_lag + 1) if reduce else chunks

    def kernel(*refs):
        refs = list(refs)
        part_ref = refs.pop(0) if reduce else None
        extra_refs = [refs.pop(0) for _ in range(n_extra)]
        full_ref = refs.pop(0) if gather else None
        out_refs = [refs.pop(0) for _ in range(n_out)]
        if reduce:
            sum_right, sum_left, acc = refs.pop(0), refs.pop(0), refs.pop(0)
            rs_send_r, rs_recv_r, rs_send_l, rs_recv_l = [refs.pop(0) for _ in range(4)]
        if gather:
            ag_send_r, ag_recv_r, ag_send_l, ag_recv_l = [refs.pop(0) for _ in range(4)]
        me = lax.axis_index("tensor")
        right, left = jnp.minimum(me + 1, last), jnp.maximum(me - 1, 0)

        def remote(source, target, send_sem, recv_sem, device):
            return pltpu.make_async_remote_copy(
                src_ref=source,
                dst_ref=target,
                send_sem=send_sem,
                recv_sem=recv_sem,
                device_id={"tensor": device},
                device_id_type=MESH,
            )

        def rs_right(block, chunk, source=None):
            here = sum_right.at[block, chunk]
            return remote(
                here if source is None else source,
                here,
                rs_send_r.at[block, chunk],
                rs_recv_r.at[block, chunk],
                right,
            )

        def rs_left(block, chunk, source=None):
            here = sum_left.at[block, chunk]
            return remote(
                here if source is None else source,
                here,
                rs_send_l.at[block, chunk],
                rs_recv_l.at[block, chunk],
                left,
            )

        def ag_right(block, chunk):
            here = full_ref.at[block, chunk]
            return remote(
                here, here, ag_send_r.at[block, chunk], ag_recv_r.at[block, chunk], right
            )

        def ag_left(block, chunk):
            here = full_ref.at[block, chunk]
            return remote(here, here, ag_send_l.at[block, chunk], ag_recv_l.at[block, chunk], left)

        neighbour_barrier(me, count)
        if prologue is not None:
            prologue(extra_refs, out_refs)

        def send_sums(chunk):
            for step in range(last):
                far = last - step

                @pl.when(jnp.logical_and(me < far, me == 0))
                def _():
                    rs_right(far, chunk, part_ref.at[far, chunk]).start()

                @pl.when(jnp.logical_and(me < far, me > 0))
                def _():
                    rs_right(far, chunk).wait_recv()
                    sum_right[far, chunk] = sum_right[far, chunk] + part_ref[far, chunk]
                    rs_right(far, chunk).start()

                @pl.when(jnp.logical_and(me > step, me == last))
                def _():
                    rs_left(step, chunk, part_ref.at[step, chunk]).start()

                @pl.when(jnp.logical_and(me > step, me < last))
                def _():
                    rs_left(step, chunk).wait_recv()
                    sum_left[step, chunk] = sum_left[step, chunk] + part_ref[step, chunk]
                    rs_left(step, chunk).start()

        def finish(chunk):
            if reduce:
                acc[...] = part_ref[me, chunk].astype(jnp.float32)

                @pl.when(me > 0)
                def _():
                    rs_right(me, chunk).wait_recv()
                    acc[...] = acc[...] + sum_right[me, chunk].astype(jnp.float32)

                @pl.when(me < last)
                def _():
                    rs_left(me, chunk).wait_recv()
                    acc[...] = acc[...] + sum_left[me, chunk].astype(jnp.float32)

                made = epilogue(chunk, acc[...], extra_refs, out_refs)
            else:
                made = epilogue(chunk, None, extra_refs, out_refs)
            if gather:
                full_ref[me, chunk] = made

                @pl.when(me < last)
                def _():
                    ag_right(me, chunk).start()

                @pl.when(me > 0)
                def _():
                    ag_left(me, chunk).start()

        def forward(chunk):
            for step in range(1, count):

                @pl.when(me - step >= 0)
                def _():
                    ag_right(jnp.maximum(me - step, 0), chunk).wait_recv()

                @pl.when(jnp.logical_and(me - step >= 0, me < last))
                def _():
                    ag_right(jnp.maximum(me - step, 0), chunk).start()

                @pl.when(me + step <= last)
                def _():
                    ag_left(jnp.minimum(me + step, last), chunk).wait_recv()

                @pl.when(jnp.logical_and(me + step <= last, me > 0))
                def _():
                    ag_left(jnp.minimum(me + step, last), chunk).start()

        def tick(time, carry):
            if reduce:

                @pl.when(time < chunks)
                def _():
                    send_sums(time)

            @pl.when(jnp.logical_and(time >= back_lag, time < back_lag + chunks))
            def _():
                finish(time - back_lag)

            if gather:

                @pl.when(time >= pass_lag)
                def _():
                    forward(time - pass_lag)

            return carry

        ticks = chunks + (pass_lag if gather else back_lag)
        lax.fori_loop(0, ticks, tick, 0)

        def drain(chunk, carry):
            for block in range(count):
                if reduce:

                    @pl.when(me < block)
                    def _():
                        rs_right(block, chunk).wait_send()

                    @pl.when(me > block)
                    def _():
                        rs_left(block, chunk).wait_send()

                if gather:

                    @pl.when(jnp.logical_and(block <= me, me < last))
                    def _():
                        ag_right(block, chunk).wait_send()

                    @pl.when(jnp.logical_and(block >= me, me > 0))
                    def _():
                        ag_left(block, chunk).wait_send()

            return carry

        lax.fori_loop(0, chunks, drain, 0)

    block = (count, chunks, rows, width)
    shapes = []
    if gather:
        shapes.append(jax.ShapeDtypeStruct(block, jnp.bfloat16))
    shapes.extend(out_shapes)
    scratch = []
    if reduce:
        scratch += [
            pltpu.VMEM(block, jnp.bfloat16),
            pltpu.VMEM(block, jnp.bfloat16),
            pltpu.VMEM((rows, width), jnp.float32),
        ]
        scratch += [pltpu.SemaphoreType.DMA((count, chunks))] * 4
    if gather:
        scratch += [pltpu.SemaphoreType.DMA((count, chunks))] * 4
    operands = ([part] if reduce else []) + list(extras)
    block_bytes = count * chunks * rows * width * 2
    results = pl.pallas_call(
        kernel,
        out_shape=tuple(shapes),
        in_specs=[pl.BlockSpec(memory_space=pltpu.VMEM)] * len(operands),
        out_specs=tuple([pl.BlockSpec(memory_space=pltpu.VMEM)] * len(shapes)),
        scratch_shapes=scratch,
        compiler_params=pltpu.CompilerParams(
            collective_id=collective_id, has_side_effects=True, vmem_limit_bytes=56 * 1024 * 1024
        ),
        cost_estimate=pl.CostEstimate(
            flops=0,
            bytes_accessed=block_bytes * (60 if reduce and gather else 45),
            transcendentals=0,
        ),
    )(*operands)
    return results


def small_sum(count, values, collective_id):
    def kernel(in_ref, out_ref, slots, send_sems, recv_sems):
        me = lax.axis_index("tensor")
        barrier = pltpu.get_barrier_semaphore()
        for offset in range(1, count):
            peer = lax.rem(me + offset, count)
            pl.semaphore_signal(barrier, inc=1, device_id={"tensor": peer}, device_id_type=MESH)
        pl.semaphore_wait(barrier, count - 1)

        def send(offset):
            return pltpu.make_async_remote_copy(
                src_ref=in_ref,
                dst_ref=slots.at[offset - 1],
                send_sem=send_sems.at[offset - 1],
                recv_sem=recv_sems.at[offset - 1],
                device_id={"tensor": lax.rem(me + offset, count)},
                device_id_type=MESH,
            )

        for offset in range(1, count):
            send(offset).start()
        total = in_ref[...]
        for offset in range(1, count):
            send(offset).wait_recv()
            total = total + slots[offset - 1]
        out_ref[...] = total
        for offset in range(1, count):
            send(offset).wait_send()

    return pl.pallas_call(
        kernel,
        out_shape=jax.ShapeDtypeStruct(values.shape, jnp.float32),
        in_specs=[pl.BlockSpec(memory_space=pltpu.VMEM)],
        out_specs=pl.BlockSpec(memory_space=pltpu.VMEM),
        scratch_shapes=[
            pltpu.VMEM((count - 1,) + values.shape, jnp.float32),
            pltpu.SemaphoreType.DMA((count - 1,)),
            pltpu.SemaphoreType.DMA((count - 1,)),
        ],
        compiler_params=pltpu.CompilerParams(collective_id=collective_id, has_side_effects=True),
    )(values)


def start_gather(count, tokens, gain_row):
    rows, width = tokens.shape
    step = rows // CHUNKS

    def epilogue(chunk, total, extra_refs, out_refs):
        value = extra_refs[0][chunk].astype(jnp.float32)
        return (rms_scale(value) * extra_refs[1][...]).astype(jnp.bfloat16)

    (full,) = line_exchange(
        count,
        CHUNKS,
        step,
        width,
        None,
        [tokens.reshape(CHUNKS, step, width), gain_row],
        [],
        epilogue,
        True,
        1,
    )
    return full.reshape(count * rows, width)


def middle_exchange(count, branch_part, tokens, gain_row):
    rows, width = tokens.shape
    step = rows // CHUNKS

    def epilogue(chunk, total, extra_refs, out_refs):
        value = extra_refs[0][chunk].astype(jnp.float32) + total
        out_refs[0][chunk] = value
        return (rms_scale(value) * extra_refs[1][...]).astype(jnp.bfloat16)

    full, middle = line_exchange(
        count,
        CHUNKS,
        step,
        width,
        branch_part.reshape(count, CHUNKS, step, width),
        [tokens.reshape(CHUNKS, step, width), gain_row],
        [jax.ShapeDtypeStruct((CHUNKS, step, width), jnp.float32)],
        epilogue,
        True,
        2,
    )
    return full.reshape(count * rows, width), middle.reshape(rows, width)


def norm_back_rows(value, gain_row, grad_out):
    inverse = lax.rsqrt(jnp.mean(value * value, axis=-1, keepdims=True) + EPSILON)
    normed = value * inverse
    scaled = grad_out * gain_row
    grad_in = inverse * (scaled - normed * jnp.mean(scaled * normed, axis=-1, keepdims=True))
    return grad_in, jnp.sum(grad_out * normed, axis=0, keepdims=True)


def zero_gain(extra_refs, out_refs):
    out_refs[1][...] = jnp.zeros_like(out_refs[1])


def middle_back_exchange(count, grad_part, router_part, middle, cotangent, gain_row):
    rows, width = middle.shape
    step = rows // CHUNKS

    def epilogue(chunk, total, extra_refs, out_refs):
        grad_out = total + extra_refs[0][chunk]
        grad_in, grad_gain = norm_back_rows(extra_refs[1][chunk], extra_refs[3][...], grad_out)
        out_refs[1][...] = out_refs[1][...] + grad_gain
        grad_middle = extra_refs[2][chunk].astype(jnp.float32) + grad_in
        out_refs[0][chunk] = grad_middle
        return grad_middle.astype(jnp.bfloat16)

    full, grad_middle, grad_gain = line_exchange(
        count,
        CHUNKS,
        step,
        width,
        grad_part.reshape(count, CHUNKS, step, width),
        [
            router_part.reshape(CHUNKS, step, width),
            middle.reshape(CHUNKS, step, width),
            cotangent.reshape(CHUNKS, step, width),
            gain_row,
        ],
        [
            jax.ShapeDtypeStruct((CHUNKS, step, width), jnp.float32),
            jax.ShapeDtypeStruct((1, width), jnp.float32),
        ],
        epilogue,
        True,
        3,
        zero_gain,
    )
    return full.reshape(count * rows, width), grad_middle.reshape(rows, width), grad_gain[0]


def end_exchange(count, grad_part, grad_middle, tokens, gain_row):
    rows, width = tokens.shape
    step = rows // CHUNKS

    def epilogue(chunk, total, extra_refs, out_refs):
        value = extra_refs[1][chunk].astype(jnp.float32)
        grad_in, grad_gain = norm_back_rows(value, extra_refs[2][...], total)
        out_refs[1][...] = out_refs[1][...] + grad_gain
        out_refs[0][chunk] = extra_refs[0][chunk] + grad_in

    grad_source, grad_gain = line_exchange(
        count,
        CHUNKS,
        step,
        width,
        grad_part.reshape(count, CHUNKS, step, width),
        [
            grad_middle.reshape(CHUNKS, step, width),
            tokens.reshape(CHUNKS, step, width),
            gain_row,
        ],
        [
            jax.ShapeDtypeStruct((CHUNKS, step, width), jnp.float32),
            jax.ShapeDtypeStruct((1, width), jnp.float32),
        ],
        epilogue,
        False,
        4,
        zero_gain,
    )
    return grad_source.reshape(rows, width), grad_gain[0]


def local(
    tokens,
    cotangent,
    routes,
    block_ids,
    attn_gain,
    q_gain,
    k_gain,
    w_query,
    w_key,
    w_value,
    w_out,
    ffn_gain,
    w_router,
    w_gate,
    w_up,
    w_down,
):
    shard_width = w_query.shape[0]
    head_cols = w_query.shape[1]
    ff_here = w_gate.shape[2]
    hidden_cols = EXPERTS * ff_here
    small = jnp.concatenate(
        [attn_gain[:, None], q_gain[:, None], k_gain[:, None], ffn_gain[:, None], w_router], axis=1
    )
    small = lax.all_gather(small, "dp", axis=0, tiled=True)
    w_qkv = lax.all_gather(
        jnp.concatenate([w_query, w_key, w_value], axis=1), "dp", axis=0, tiled=True
    )
    w_o_t = lax.all_gather(w_out.T, "dp", axis=0, tiled=True)
    gate_local = w_gate.transpose(1, 0, 2).reshape(shard_width, hidden_cols)
    up_local = w_up.transpose(1, 0, 2).reshape(shard_width, hidden_cols)
    down_local = w_down.transpose(2, 0, 1).reshape(shard_width, hidden_cols)
    full_gate = lax.all_gather(gate_local, "dp", axis=0, tiled=True)
    full_up = lax.all_gather(up_local, "dp", axis=0, tiled=True)
    full_down = lax.all_gather(down_local, "dp", axis=0, tiled=True)
    full_router = small[:, 4:]
    model_width = tokens.shape[1]
    local_rows = tokens.shape[0]
    tensor_rank = lax.axis_index("tensor")
    heads_here = head_cols // HEAD_DIM
    col_start = tensor_rank * head_cols
    gains = small[:, :4].astype(jnp.float32).T
    attn_scale = gains[0]
    query_scale = lax.dynamic_slice_in_dim(gains[1], col_start, head_cols)
    key_scale = lax.dynamic_slice_in_dim(gains[2], col_start, head_cols)
    ffn_scale = gains[3]
    count = lax.axis_size("tensor")
    normed = start_gather(count, tokens, attn_scale[None, :])
    seq_len = normed.shape[0]
    block_row = block_ids[0]
    cosine_table, sine_table = rope_tables(seq_len, HEAD_DIM)
    projected = jnp.dot(normed, w_qkv, preferred_element_type=jnp.float32)
    query_proj = projected[:, :head_cols]
    key_proj = projected[:, head_cols : 2 * head_cols]
    value_low = projected[:, 2 * head_cols :].astype(jnp.bfloat16)
    squares = jnp.stack(
        [jnp.sum(query_proj * query_proj, axis=1), jnp.sum(key_proj * key_proj, axis=1)]
    )
    query_sq, key_sq = small_sum(count, squares, 5)
    query_inv = lax.rsqrt(query_sq / model_width + EPSILON)[:, None]
    key_inv = lax.rsqrt(key_sq / model_width + EPSILON)[:, None]
    query_normed = query_proj * query_inv
    key_normed = key_proj * key_inv
    q_rot = rotate(
        (query_normed * query_scale).reshape(seq_len, heads_here, HEAD_DIM),
        cosine_table,
        sine_table,
    ).astype(jnp.bfloat16)
    k_rot = rotate(
        (key_normed * key_scale).reshape(seq_len, heads_here, HEAD_DIM), cosine_table, sine_table
    ).astype(jnp.bfloat16)
    value_heads = value_low.reshape(seq_len, heads_here, HEAD_DIM)
    mixed, log_totals = attend(q_rot, k_rot, value_heads, block_row)
    mixed_low = mixed.astype(jnp.bfloat16)
    branch_part = jnp.einsum(
        "sf,df->sd", mixed_low, w_o_t, preferred_element_type=jnp.float32
    ).astype(jnp.bfloat16)
    normed_two, middle = middle_exchange(count, branch_part, tokens, ffn_scale[None, :])
    grad_rows = lax.all_gather(cotangent, "tensor", axis=0, tiled=True)
    logits = jnp.dot(normed_two, full_router, preferred_element_type=jnp.float32)
    router_probs = jax.nn.softmax(logits, axis=-1)
    kept = kept_mask(routes)
    gate_values = router_probs * kept
    gates = jnp.repeat(gate_values, ff_here, axis=1)

    gate_part = jnp.dot(normed_two, full_gate, preferred_element_type=jnp.float32)
    up_part = jnp.dot(normed_two, full_up, preferred_element_type=jnp.float32)
    sigmoid_gate = jax.nn.sigmoid(gate_part)
    silu_gate = gate_part * sigmoid_gate
    hidden = silu_gate * up_part
    hidden_gated = (hidden * gates).astype(jnp.bfloat16)
    combined = jnp.einsum(
        "sk,dk->sd", hidden_gated, full_down, preferred_element_type=jnp.float32
    ).astype(jnp.bfloat16)
    back_hidden = jnp.dot(grad_rows, full_down, preferred_element_type=jnp.float32)
    gate_dot = jnp.sum((hidden * back_hidden).reshape(seq_len, EXPERTS, ff_here), axis=2)
    grad_hidden = back_hidden * gates
    grad_gate_part = (
        grad_hidden * up_part * sigmoid_gate * (1.0 + gate_part * (1.0 - sigmoid_gate))
    ).astype(jnp.bfloat16)
    grad_up_part = (grad_hidden * silu_gate).astype(jnp.bfloat16)
    grad_two_part = (
        jnp.einsum("sk,dk->sd", grad_gate_part, full_gate, preferred_element_type=jnp.float32)
        + jnp.einsum("sk,dk->sd", grad_up_part, full_up, preferred_element_type=jnp.float32)
    ).astype(jnp.bfloat16)
    grad_gate_w = jnp.einsum(
        "sd,sk->dk", normed_two, grad_gate_part, preferred_element_type=jnp.float32
    ).astype(jnp.bfloat16)
    grad_up_w = jnp.einsum(
        "sd,sk->dk", normed_two, grad_up_part, preferred_element_type=jnp.float32
    ).astype(jnp.bfloat16)
    grad_down_w = jnp.einsum(
        "sd,sk->dk", grad_rows, hidden_gated, preferred_element_type=jnp.float32
    ).astype(jnp.bfloat16)
    ffn_branch = lax.psum_scatter(
        combined, "tensor", scatter_dimension=0, tiled=True
    ).astype(jnp.float32)
    output = (middle + ffn_branch).astype(jnp.bfloat16)
    grad_probs = small_sum(count, (gate_dot * kept).T, 6).T
    grad_logits = router_probs * (
        grad_probs - jnp.sum(router_probs * grad_probs, axis=1, keepdims=True)
    )
    logits_low = grad_logits.astype(jnp.bfloat16)
    grad_router = jnp.einsum(
        "sd,se->de", normed_two, logits_low, preferred_element_type=jnp.float32
    )
    own_logits = lax.dynamic_slice_in_dim(logits_low, tensor_rank * local_rows, local_rows)
    router_part = jnp.einsum(
        "se,de->sd", own_logits, full_router, preferred_element_type=jnp.float32
    )
    grad_attn_rows, grad_middle, grad_ffn_gain = middle_back_exchange(
        count, grad_two_part, router_part, middle, cotangent, ffn_scale[None, :]
    )
    grad_out_w = jnp.einsum(
        "sf,sd->df", mixed_low, grad_attn_rows, preferred_element_type=jnp.float32
    ).astype(jnp.bfloat16)
    grad_mixed = jnp.dot(grad_attn_rows, w_o_t, preferred_element_type=jnp.float32).astype(
        jnp.bfloat16
    )
    grad_q_rot, grad_k_rot, grad_v = attend_back(
        q_rot,
        k_rot,
        value_heads,
        block_row,
        log_totals,
        grad_mixed.reshape(seq_len, heads_here, HEAD_DIM),
    )
    grad_query_normed = rotate_back(grad_q_rot, cosine_table, sine_table).reshape(
        seq_len, head_cols
    )
    grad_key_normed = rotate_back(grad_k_rot, cosine_table, sine_table).reshape(seq_len, head_cols)
    grad_query_gain = jnp.sum(grad_query_normed * query_normed, axis=0)
    grad_key_gain = jnp.sum(grad_key_normed * key_normed, axis=0)
    query_scaled = grad_query_normed * query_scale
    key_scaled = grad_key_normed * key_scale
    dots = jnp.stack(
        [jnp.sum(query_scaled * query_normed, axis=1), jnp.sum(key_scaled * key_normed, axis=1)]
    )
    query_dot, key_dot = small_sum(count, dots, 7)
    grad_query_proj = (
        query_inv * (query_scaled - query_normed * (query_dot / model_width)[:, None])
    ).astype(jnp.bfloat16)
    grad_key_proj = (key_inv * (key_scaled - key_normed * (key_dot / model_width)[:, None])).astype(
        jnp.bfloat16
    )
    grad_value_low = grad_v.reshape(seq_len, head_cols).astype(jnp.bfloat16)
    grad_qkv = jnp.concatenate([grad_query_proj, grad_key_proj, grad_value_low], axis=1)
    grad_qkv_w = jnp.einsum(
        "sd,sf->df", normed, grad_qkv, preferred_element_type=jnp.float32
    ).astype(jnp.bfloat16)
    grad_normed_part = jnp.einsum(
        "sf,df->sd", grad_qkv, w_qkv, preferred_element_type=jnp.float32
    ).astype(jnp.bfloat16)
    grad_source, grad_attn_gain = end_exchange(
        count, grad_normed_part, grad_middle, tokens, attn_scale[None, :]
    )
    zero_cols = jnp.zeros((model_width,), jnp.float32)
    query_gain_full = lax.dynamic_update_slice_in_dim(zero_cols, grad_query_gain, col_start, 0)
    key_gain_full = lax.dynamic_update_slice_in_dim(zero_cols, grad_key_gain, col_start, 0)
    gain_rows = lax.psum(
        jnp.stack([grad_attn_gain, query_gain_full, key_gain_full, grad_ffn_gain]),
        ("dp", "tensor"),
    )
    dp_rank = lax.axis_index("dp")
    gain_width = model_width // (lax.axis_size("dp") * count)
    gain_sums = lax.dynamic_slice_in_dim(
        gain_rows, (dp_rank * count + tensor_rank) * gain_width, gain_width, 1
    )
    sum_gate = lax.psum_scatter(grad_gate_w, "dp", scatter_dimension=0, tiled=True)
    sum_up = lax.psum_scatter(grad_up_w, "dp", scatter_dimension=0, tiled=True)
    sum_down = lax.psum_scatter(grad_down_w, "dp", scatter_dimension=0, tiled=True)
    sum_out = lax.psum_scatter(grad_out_w, "dp", scatter_dimension=0, tiled=True)
    sum_qkv = lax.psum_scatter(grad_qkv_w, "dp", scatter_dimension=0, tiled=True).astype(
        jnp.float32
    )
    router_rows = lax.psum(grad_router.T, "dp")
    sum_router = lax.dynamic_slice_in_dim(
        router_rows, dp_rank * shard_width, shard_width, 1
    ).T
    grad_gate = sum_gate.reshape(shard_width, EXPERTS, ff_here).transpose(1, 0, 2)
    grad_up = sum_up.reshape(shard_width, EXPERTS, ff_here).transpose(1, 0, 2)
    grad_down = sum_down.reshape(shard_width, EXPERTS, ff_here).transpose(1, 2, 0)
    return (
        output,
        grad_source,
        gain_sums[0],
        gain_sums[1],
        gain_sums[2],
        sum_qkv[:, :head_cols],
        sum_qkv[:, head_cols : 2 * head_cols],
        sum_qkv[:, 2 * head_cols :],
        sum_out.T.astype(jnp.float32),
        gain_sums[3],
        sum_router,
        grad_gate.astype(jnp.float32),
        grad_up.astype(jnp.float32),
        grad_down.astype(jnp.float32),
    )


def solution(mesh):
    placed = (
        P(("dp", "tensor"), None),
        P(("dp", "tensor"), None),
        P("dp", None),
        P("dp", None),
        P("dp"),
        P("dp"),
        P("dp"),
        P("dp", "tensor"),
        P("dp", "tensor"),
        P("dp", "tensor"),
        P("tensor", "dp"),
        P("dp"),
        P("dp", None),
        P(None, "dp", "tensor"),
        P(None, "dp", "tensor"),
        P(None, "tensor", "dp"),
    )
    return jax.shard_map(
        local,
        mesh=mesh,
        in_specs=placed,
        out_specs=(
            P(("dp", "tensor"), None),
            P(("dp", "tensor"), None),
            P(("dp", "tensor")),
            P(("dp", "tensor")),
            P(("dp", "tensor")),
            P("dp", "tensor"),
            P("dp", "tensor"),
            P("dp", "tensor"),
            P("tensor", "dp"),
            P(("dp", "tensor")),
            P("dp", None),
            P(None, "dp", "tensor"),
            P(None, "dp", "tensor"),
            P(None, "tensor", "dp"),
        ),
        check_vma=False,
    )
```

```python
import math

import jax
import jax.numpy as jnp
from jax import lax
from jax.experimental import pallas as pl
from jax.experimental.pallas import tpu as pltpu
from jax.sharding import PartitionSpec as P

HEAD_DIM = 128
EXPERTS = 8
TOPK = 2
QROWS = 512
CAP = 320


EPSILON = 1e-05
MASKED = -1e30
MESH = pl.DeviceIdType.MESH
CHUNK_ROWS = 16


def rms_scale(source):
    return source * lax.rsqrt(jnp.mean(source * source, axis=-1, keepdims=True) + EPSILON)


def norm_back(source, gain_vec, grad_out):
    inverse = lax.rsqrt(jnp.mean(source * source, axis=-1, keepdims=True) + EPSILON)
    normed = source * inverse
    grad_gain = jnp.sum(grad_out * normed, axis=0)
    scaled = grad_out * gain_vec
    grad_in = inverse * (scaled - normed * jnp.mean(scaled * normed, axis=-1, keepdims=True))
    return (grad_in, grad_gain)


def rope_tables(seq_len, head_dim):
    half_dim = head_dim // 2
    frequency = jnp.exp(
        -math.log(10000.0) * 2.0 * jnp.arange(half_dim, dtype=jnp.float32) / head_dim
    )
    angles = jnp.arange(seq_len, dtype=jnp.float32)[:, None] * frequency[None, :]
    return (
        jnp.concatenate([jnp.cos(angles)] * 2, axis=1),
        jnp.concatenate([jnp.sin(angles)] * 2, axis=1),
    )


def rotate(heads_in, cosine_table, sine_table):
    half_dim = heads_in.shape[-1] // 2
    turned = jnp.concatenate([-heads_in[..., half_dim:], heads_in[..., :half_dim]], axis=-1)
    return heads_in * cosine_table[:, None, :] + turned * sine_table[:, None, :]


def rotate_back(grad_in, cosine_table, sine_table):
    half_dim = grad_in.shape[-1] // 2
    sined = grad_in * sine_table[:, None, :]
    turned = jnp.concatenate([sined[..., half_dim:], -sined[..., :half_dim]], axis=-1)
    return grad_in * cosine_table[:, None, :] + turned


def attend(q_rot, k_rot, value_heads, block_row):
    seq_len, heads_here, head_dim = q_rot.shape
    blocks = seq_len // QROWS
    score_scale = head_dim ** (-0.5)
    q_blocks = q_rot.reshape(blocks, QROWS, heads_here, head_dim)
    id_blocks = block_row.reshape(blocks, QROWS)

    def per_block(block_item):
        q_block, id_block = block_item
        scores = (
            jnp.einsum("qhd,khd->hqk", q_block, k_rot, preferred_element_type=jnp.float32)
            * score_scale
        )
        allowed = block_row[None, None, :] <= id_block[None, :, None]
        scores = jnp.where(allowed, scores, MASKED)
        row_top = jnp.max(scores, axis=-1, keepdims=True)
        row_sum = jnp.sum(jnp.exp(scores - row_top), axis=-1, keepdims=True)
        log_total = row_top + jnp.log(row_sum)
        weights_low = jnp.exp(scores - log_total).astype(jnp.bfloat16)
        mixed_block = jnp.einsum(
            "hqk,khd->qhd", weights_low, value_heads, preferred_element_type=jnp.float32
        )
        return (mixed_block.reshape(QROWS, heads_here * head_dim), log_total[..., 0])

    mixed_blocks, log_totals = lax.map(per_block, (q_blocks, id_blocks))
    return (mixed_blocks.reshape(seq_len, heads_here * head_dim), log_totals)


def attend_back(q_rot, k_rot, value_heads, block_row, log_totals, grad_mixed):
    seq_len, heads_here, head_dim = q_rot.shape
    blocks = seq_len // QROWS
    score_scale = head_dim ** (-0.5)
    q_blocks = q_rot.reshape(blocks, QROWS, heads_here, head_dim)
    g_blocks = grad_mixed.reshape(blocks, QROWS, heads_here, head_dim)
    id_blocks = block_row.reshape(blocks, QROWS)

    def back_block(running, block_item):
        q_block, g_block, id_block, log_block = block_item
        scores = (
            jnp.einsum("qhd,khd->hqk", q_block, k_rot, preferred_element_type=jnp.float32)
            * score_scale
        )
        allowed = block_row[None, None, :] <= id_block[None, :, None]
        scores = jnp.where(allowed, scores, MASKED)
        weights = jnp.exp(scores - log_block[..., None])
        weights_low = weights.astype(jnp.bfloat16)
        grad_weights = jnp.einsum(
            "qhd,khd->hqk", g_block, value_heads, preferred_element_type=jnp.float32
        )
        grad_scores = weights * (
            grad_weights - jnp.sum(weights * grad_weights, axis=-1, keepdims=True)
        )
        grad_low = grad_scores.astype(jnp.bfloat16)
        grad_query = (
            jnp.einsum("hqk,khd->qhd", grad_low, k_rot, preferred_element_type=jnp.float32)
            * score_scale
        )
        grad_key = (
            running[0]
            + jnp.einsum("hqk,qhd->khd", grad_low, q_block, preferred_element_type=jnp.float32)
            * score_scale
        )
        grad_value = running[1] + jnp.einsum(
            "hqk,qhd->khd", weights_low, g_block, preferred_element_type=jnp.float32
        )
        return ((grad_key, grad_value), grad_query)

    zero_heads = jnp.zeros(k_rot.shape, jnp.float32)
    sums_out, grad_query = lax.scan(
        back_block, (zero_heads, zero_heads), (q_blocks, g_blocks, id_blocks, log_totals)
    )
    return (grad_query.reshape(seq_len, heads_here, head_dim), sums_out[0], sums_out[1])


def kept_mask(route_rows):
    expert_ids = jnp.arange(EXPERTS, dtype=jnp.int32)
    first = (route_rows[:, 0:1] == expert_ids[None, :]).astype(jnp.int32)
    second = (route_rows[:, 1:2] == expert_ids[None, :]).astype(jnp.int32)
    both = first + second
    earlier = jnp.cumsum(both, axis=0) - both
    return jnp.where((both > 0) & (earlier < CAP), 1.0, 0.0).astype(jnp.float32)


def neighbour_barrier(me, count):
    barrier = pltpu.get_barrier_semaphore()

    @pl.when(me > 0)
    def _():
        pl.semaphore_signal(barrier, inc=1, device_id={"tensor": me - 1}, device_id_type=MESH)

    @pl.when(me < count - 1)
    def _():
        pl.semaphore_signal(barrier, inc=1, device_id={"tensor": me + 1}, device_id_type=MESH)

    pl.semaphore_wait(
        barrier, jnp.minimum(me, 1).astype(jnp.int32) + jnp.minimum(count - 1 - me, 1)
    )


def line_exchange(
    count, chunks, rows, width, part, extras, out_shapes, epilogue, gather, collective_id, prologue=None
):
    reduce = part is not None
    n_extra = len(extras)
    n_out = len(out_shapes)
    last = count - 1
    back_lag = last if reduce else 0
    pass_lag = back_lag if reduce else chunks

    def kernel(*refs):
        refs = list(refs)
        part_ref = refs.pop(0) if reduce else None
        extra_refs = [refs.pop(0) for _ in range(n_extra)]
        full_ref = refs.pop(0) if gather else None
        out_refs = [refs.pop(0) for _ in range(n_out)]
        if reduce:
            sum_right, sum_left, acc = refs.pop(0), refs.pop(0), refs.pop(0)
            rs_send_r, rs_recv_r, rs_send_l, rs_recv_l = [refs.pop(0) for _ in range(4)]
        if gather:
            ag_send_r, ag_recv_r, ag_send_l, ag_recv_l = [refs.pop(0) for _ in range(4)]
        me = lax.axis_index("tensor")
        right, left = jnp.minimum(me + 1, last), jnp.maximum(me - 1, 0)

        def remote(source, target, send_sem, recv_sem, device):
            return pltpu.make_async_remote_copy(
                src_ref=source,
                dst_ref=target,
                send_sem=send_sem,
                recv_sem=recv_sem,
                device_id={"tensor": device},
                device_id_type=MESH,
            )

        def rs_right(block, chunk, source=None):
            here = sum_right.at[block, chunk]
            return remote(
                here if source is None else source,
                here,
                rs_send_r.at[block, chunk],
                rs_recv_r.at[block, chunk],
                right,
            )

        def rs_left(block, chunk, source=None):
            here = sum_left.at[block, chunk]
            return remote(
                here if source is None else source,
                here,
                rs_send_l.at[block, chunk],
                rs_recv_l.at[block, chunk],
                left,
            )

        def ag_right(block, chunk):
            here = full_ref.at[block, chunk]
            return remote(
                here, here, ag_send_r.at[block, chunk], ag_recv_r.at[block, chunk], right
            )

        def ag_left(block, chunk):
            here = full_ref.at[block, chunk]
            return remote(here, here, ag_send_l.at[block, chunk], ag_recv_l.at[block, chunk], left)

        neighbour_barrier(me, count)
        if prologue is not None:
            prologue(extra_refs, out_refs)

        def send_right(chunk):
            for step in range(last):
                far = last - step

                @pl.when(jnp.logical_and(me < far, me == 0))
                def _():
                    rs_right(far, chunk, part_ref.at[far, chunk]).start()

                @pl.when(jnp.logical_and(me < far, me > 0))
                def _():
                    rs_right(far, chunk).wait_recv()
                    sum_right[far, chunk] = sum_right[far, chunk] + part_ref[far, chunk]
                    rs_right(far, chunk).start()

        def send_left(chunk):
            for step in range(last):

                @pl.when(jnp.logical_and(me > step, me == last))
                def _():
                    rs_left(step, chunk, part_ref.at[step, chunk]).start()

                @pl.when(jnp.logical_and(me > step, me < last))
                def _():
                    rs_left(step, chunk).wait_recv()
                    sum_left[step, chunk] = sum_left[step, chunk] + part_ref[step, chunk]
                    rs_left(step, chunk).start()

        def finish(chunk):
            if reduce:
                acc[...] = part_ref[me, chunk].astype(jnp.float32)

                @pl.when(me > 0)
                def _():
                    rs_right(me, chunk).wait_recv()
                    acc[...] = acc[...] + sum_right[me, chunk].astype(jnp.float32)

                @pl.when(me < last)
                def _():
                    rs_left(me, chunk).wait_recv()
                    acc[...] = acc[...] + sum_left[me, chunk].astype(jnp.float32)

                made = epilogue(chunk, acc[...], extra_refs, out_refs)
            else:
                made = epilogue(chunk, None, extra_refs, out_refs)
            if gather:
                full_ref[me, chunk] = made

                @pl.when(me < last)
                def _():
                    ag_right(me, chunk).start()

                @pl.when(me > 0)
                def _():
                    ag_left(me, chunk).start()

        def forward(chunk, step):
            @pl.when(me - step >= 0)
            def _():
                ag_right(jnp.maximum(me - step, 0), chunk).wait_recv()

            @pl.when(jnp.logical_and(me - step >= 0, me < last))
            def _():
                ag_right(jnp.maximum(me - step, 0), chunk).start()

            @pl.when(me + step <= last)
            def _():
                ag_left(jnp.minimum(me + step, last), chunk).wait_recv()

            @pl.when(jnp.logical_and(me + step <= last, me > 0))
            def _():
                ag_left(jnp.minimum(me + step, last), chunk).start()

        def at_chunk(chunk, work):
            @pl.when(jnp.logical_and(chunk >= 0, chunk < chunks))
            def _():
                work(jnp.clip(chunk, 0, chunks - 1))

        def tick(time, carry):
            if reduce:
                at_chunk(time - me, send_right)
                at_chunk(time - (last - me), send_left)
            at_chunk(time - back_lag, finish)
            if gather:
                for step in range(1, count):
                    at_chunk(time - pass_lag - step, lambda chunk: forward(chunk, step))
            return carry

        ticks = chunks + (pass_lag + last if gather else back_lag)
        lax.fori_loop(0, ticks, tick, 0)

        def drain(chunk, carry):
            for block in range(count):
                if reduce:

                    @pl.when(me < block)
                    def _():
                        rs_right(block, chunk).wait_send()

                    @pl.when(me > block)
                    def _():
                        rs_left(block, chunk).wait_send()

                if gather:

                    @pl.when(jnp.logical_and(block <= me, me < last))
                    def _():
                        ag_right(block, chunk).wait_send()

                    @pl.when(jnp.logical_and(block >= me, me > 0))
                    def _():
                        ag_left(block, chunk).wait_send()

            return carry

        lax.fori_loop(0, chunks, drain, 0)

    block = (count, chunks, rows, width)
    shapes = []
    if gather:
        shapes.append(jax.ShapeDtypeStruct(block, jnp.bfloat16))
    shapes.extend(out_shapes)
    scratch = []
    if reduce:
        scratch += [
            pltpu.VMEM(block, jnp.bfloat16),
            pltpu.VMEM(block, jnp.bfloat16),
            pltpu.VMEM((rows, width), jnp.float32),
        ]
        scratch += [pltpu.SemaphoreType.DMA((count, chunks))] * 4
    if gather:
        scratch += [pltpu.SemaphoreType.DMA((count, chunks))] * 4
    operands = ([part] if reduce else []) + list(extras)
    block_bytes = count * chunks * rows * width * 2
    results = pl.pallas_call(
        kernel,
        out_shape=tuple(shapes),
        in_specs=[pl.BlockSpec(memory_space=pltpu.VMEM)] * len(operands),
        out_specs=tuple([pl.BlockSpec(memory_space=pltpu.VMEM)] * len(shapes)),
        scratch_shapes=scratch,
        compiler_params=pltpu.CompilerParams(
            collective_id=collective_id, has_side_effects=True, vmem_limit_bytes=56 * 1024 * 1024
        ),
        cost_estimate=pl.CostEstimate(
            flops=0,
            bytes_accessed=block_bytes * (60 if reduce and gather else 45),
            transcendentals=0,
        ),
    )(*operands)
    return results


def small_sum(count, values, collective_id):
    def kernel(in_ref, out_ref, slots, send_sems, recv_sems):
        me = lax.axis_index("tensor")
        barrier = pltpu.get_barrier_semaphore()
        for offset in range(1, count):
            peer = lax.rem(me + offset, count)
            pl.semaphore_signal(barrier, inc=1, device_id={"tensor": peer}, device_id_type=MESH)
        pl.semaphore_wait(barrier, count - 1)

        def send(offset):
            return pltpu.make_async_remote_copy(
                src_ref=in_ref,
                dst_ref=slots.at[offset - 1],
                send_sem=send_sems.at[offset - 1],
                recv_sem=recv_sems.at[offset - 1],
                device_id={"tensor": lax.rem(me + offset, count)},
                device_id_type=MESH,
            )

        for offset in range(1, count):
            send(offset).start()
        total = in_ref[...]
        for offset in range(1, count):
            send(offset).wait_recv()
            total = total + slots[offset - 1]
        out_ref[...] = total
        for offset in range(1, count):
            send(offset).wait_send()

    return pl.pallas_call(
        kernel,
        out_shape=jax.ShapeDtypeStruct(values.shape, jnp.float32),
        in_specs=[pl.BlockSpec(memory_space=pltpu.VMEM)],
        out_specs=pl.BlockSpec(memory_space=pltpu.VMEM),
        scratch_shapes=[
            pltpu.VMEM((count - 1,) + values.shape, jnp.float32),
            pltpu.SemaphoreType.DMA((count - 1,)),
            pltpu.SemaphoreType.DMA((count - 1,)),
        ],
        compiler_params=pltpu.CompilerParams(collective_id=collective_id, has_side_effects=True),
    )(values)


def start_gather(count, tokens, gain_row):
    rows, width = tokens.shape
    step, chunks = CHUNK_ROWS, rows // CHUNK_ROWS

    def epilogue(chunk, total, extra_refs, out_refs):
        value = extra_refs[0][chunk].astype(jnp.float32)
        return (rms_scale(value) * extra_refs[1][...]).astype(jnp.bfloat16)

    (full,) = line_exchange(
        count,
        chunks,
        step,
        width,
        None,
        [tokens.reshape(chunks, step, width), gain_row],
        [],
        epilogue,
        True,
        1,
    )
    return full.reshape(count * rows, width)


def middle_exchange(count, branch_part, tokens, gain_row):
    rows, width = tokens.shape
    step, chunks = CHUNK_ROWS, rows // CHUNK_ROWS

    def epilogue(chunk, total, extra_refs, out_refs):
        value = extra_refs[0][chunk].astype(jnp.float32) + total
        out_refs[0][chunk] = value
        return (rms_scale(value) * extra_refs[1][...]).astype(jnp.bfloat16)

    full, middle = line_exchange(
        count,
        chunks,
        step,
        width,
        branch_part.reshape(count, chunks, step, width),
        [tokens.reshape(chunks, step, width), gain_row],
        [jax.ShapeDtypeStruct((chunks, step, width), jnp.float32)],
        epilogue,
        True,
        2,
    )
    return full.reshape(count * rows, width), middle.reshape(rows, width)


def norm_back_rows(value, gain_row, grad_out):
    inverse = lax.rsqrt(jnp.mean(value * value, axis=-1, keepdims=True) + EPSILON)
    normed = value * inverse
    scaled = grad_out * gain_row
    grad_in = inverse * (scaled - normed * jnp.mean(scaled * normed, axis=-1, keepdims=True))
    return grad_in, jnp.sum(grad_out * normed, axis=0, keepdims=True)


def zero_gain(extra_refs, out_refs):
    out_refs[1][...] = jnp.zeros_like(out_refs[1])


def middle_back_exchange(count, grad_part, router_part, middle, cotangent, gain_row):
    rows, width = middle.shape
    step, chunks = CHUNK_ROWS, rows // CHUNK_ROWS

    def epilogue(chunk, total, extra_refs, out_refs):
        grad_out = total + extra_refs[0][chunk]
        grad_in, grad_gain = norm_back_rows(extra_refs[1][chunk], extra_refs[3][...], grad_out)
        out_refs[1][...] = out_refs[1][...] + grad_gain
        grad_middle = extra_refs[2][chunk].astype(jnp.float32) + grad_in
        out_refs[0][chunk] = grad_middle
        return grad_middle.astype(jnp.bfloat16)

    full, grad_middle, grad_gain = line_exchange(
        count,
        chunks,
        step,
        width,
        grad_part.reshape(count, chunks, step, width),
        [
            router_part.reshape(chunks, step, width),
            middle.reshape(chunks, step, width),
            cotangent.reshape(chunks, step, width),
            gain_row,
        ],
        [
            jax.ShapeDtypeStruct((chunks, step, width), jnp.float32),
            jax.ShapeDtypeStruct((1, width), jnp.float32),
        ],
        epilogue,
        True,
        3,
        zero_gain,
    )
    return full.reshape(count * rows, width), grad_middle.reshape(rows, width), grad_gain[0]


def end_exchange(count, grad_part, grad_middle, tokens, gain_row):
    rows, width = tokens.shape
    step, chunks = CHUNK_ROWS, rows // CHUNK_ROWS

    def epilogue(chunk, total, extra_refs, out_refs):
        value = extra_refs[1][chunk].astype(jnp.float32)
        grad_in, grad_gain = norm_back_rows(value, extra_refs[2][...], total)
        out_refs[1][...] = out_refs[1][...] + grad_gain
        out_refs[0][chunk] = extra_refs[0][chunk] + grad_in

    grad_source, grad_gain = line_exchange(
        count,
        chunks,
        step,
        width,
        grad_part.reshape(count, chunks, step, width),
        [
            grad_middle.reshape(chunks, step, width),
            tokens.reshape(chunks, step, width),
            gain_row,
        ],
        [
            jax.ShapeDtypeStruct((chunks, step, width), jnp.float32),
            jax.ShapeDtypeStruct((1, width), jnp.float32),
        ],
        epilogue,
        False,
        4,
        zero_gain,
    )
    return grad_source.reshape(rows, width), grad_gain[0]


def after(value, *others):
    zero = sum(other[0, 0].astype(jnp.float32) * 0.0 for other in others)
    return value + zero.astype(value.dtype)


def local(
    tokens,
    cotangent,
    routes,
    block_ids,
    attn_gain,
    q_gain,
    k_gain,
    w_query,
    w_key,
    w_value,
    w_out,
    ffn_gain,
    w_router,
    w_gate,
    w_up,
    w_down,
):
    shard_width = w_query.shape[0]
    head_cols = w_query.shape[1]
    ff_here = w_gate.shape[2]
    hidden_cols = EXPERTS * ff_here
    small = jnp.concatenate(
        [attn_gain[:, None], q_gain[:, None], k_gain[:, None], ffn_gain[:, None], w_router], axis=1
    )
    small = lax.all_gather(small, "dp", axis=0, tiled=True)
    w_qkv = lax.all_gather(
        jnp.concatenate([w_query, w_key, w_value], axis=1), "dp", axis=0, tiled=True
    )
    w_o_t = lax.all_gather(w_out.T, "dp", axis=0, tiled=True)
    gate_local = w_gate.transpose(1, 0, 2).reshape(shard_width, hidden_cols)
    full_gate = lax.all_gather(gate_local, "dp", axis=0, tiled=True)
    full_router = small[:, 4:]
    model_width = tokens.shape[1]
    local_rows = tokens.shape[0]
    tensor_rank = lax.axis_index("tensor")
    heads_here = head_cols // HEAD_DIM
    col_start = tensor_rank * head_cols
    gains = small[:, :4].astype(jnp.float32).T
    attn_scale = gains[0]
    query_scale = lax.dynamic_slice_in_dim(gains[1], col_start, head_cols)
    key_scale = lax.dynamic_slice_in_dim(gains[2], col_start, head_cols)
    ffn_scale = gains[3]
    count = lax.axis_size("tensor")
    normed = start_gather(count, tokens, attn_scale[None, :])
    grad_rows = lax.all_gather(after(cotangent, normed), "tensor", axis=0, tiled=True)
    seq_len = normed.shape[0]
    block_row = block_ids[0]
    cosine_table, sine_table = rope_tables(seq_len, HEAD_DIM)
    projected = jnp.dot(normed, w_qkv, preferred_element_type=jnp.float32)
    query_proj = projected[:, :head_cols]
    key_proj = projected[:, head_cols : 2 * head_cols]
    value_low = projected[:, 2 * head_cols :].astype(jnp.bfloat16)
    squares = jnp.stack(
        [jnp.sum(query_proj * query_proj, axis=1), jnp.sum(key_proj * key_proj, axis=1)]
    )
    query_sq, key_sq = small_sum(count, squares, 5)
    up_local = after(w_up, query_sq[None]).transpose(1, 0, 2).reshape(shard_width, hidden_cols)
    down_local = after(w_down, query_sq[None]).transpose(2, 0, 1).reshape(shard_width, hidden_cols)
    full_up = lax.all_gather(up_local, "dp", axis=0, tiled=True)
    full_down = lax.all_gather(down_local, "dp", axis=0, tiled=True)
    query_inv = lax.rsqrt(query_sq / model_width + EPSILON)[:, None]
    key_inv = lax.rsqrt(key_sq / model_width + EPSILON)[:, None]
    query_normed = query_proj * query_inv
    key_normed = key_proj * key_inv
    q_rot = rotate(
        (query_normed * query_scale).reshape(seq_len, heads_here, HEAD_DIM),
        cosine_table,
        sine_table,
    ).astype(jnp.bfloat16)
    k_rot = rotate(
        (key_normed * key_scale).reshape(seq_len, heads_here, HEAD_DIM), cosine_table, sine_table
    ).astype(jnp.bfloat16)
    value_heads = value_low.reshape(seq_len, heads_here, HEAD_DIM)
    mixed, log_totals = attend(q_rot, k_rot, value_heads, block_row)
    mixed_low = mixed.astype(jnp.bfloat16)
    branch_part = jnp.einsum(
        "sf,df->sd", mixed_low, w_o_t, preferred_element_type=jnp.float32
    ).astype(jnp.bfloat16)
    normed_two, middle = middle_exchange(count, branch_part, tokens, ffn_scale[None, :])
    full_router = after(full_router, grad_rows, normed_two)
    logits = jnp.dot(normed_two, full_router, preferred_element_type=jnp.float32)
    router_probs = jax.nn.softmax(logits, axis=-1)
    kept = kept_mask(routes)
    gate_values = router_probs * kept
    gates = jnp.repeat(gate_values, ff_here, axis=1)

    gate_part = jnp.dot(normed_two, full_gate, preferred_element_type=jnp.float32)
    up_part = jnp.dot(normed_two, full_up, preferred_element_type=jnp.float32)
    sigmoid_gate = jax.nn.sigmoid(gate_part)
    silu_gate = gate_part * sigmoid_gate
    hidden = silu_gate * up_part
    hidden_gated = (hidden * gates).astype(jnp.bfloat16)
    combined = jnp.einsum(
        "sk,dk->sd", hidden_gated, full_down, preferred_element_type=jnp.float32
    ).astype(jnp.bfloat16)
    back_hidden = jnp.dot(grad_rows, full_down, preferred_element_type=jnp.float32)
    gate_dot = jnp.sum((hidden * back_hidden).reshape(seq_len, EXPERTS, ff_here), axis=2)
    grad_hidden = back_hidden * gates
    grad_gate_part = (
        grad_hidden * up_part * sigmoid_gate * (1.0 + gate_part * (1.0 - sigmoid_gate))
    ).astype(jnp.bfloat16)
    grad_up_part = (grad_hidden * silu_gate).astype(jnp.bfloat16)
    grad_gate_w = jnp.einsum(
        "sd,sk->dk", normed_two, grad_gate_part, preferred_element_type=jnp.float32
    ).astype(jnp.bfloat16)
    grad_up_w = jnp.einsum(
        "sd,sk->dk", normed_two, grad_up_part, preferred_element_type=jnp.float32
    ).astype(jnp.bfloat16)
    grad_down_w = jnp.einsum(
        "sd,sk->dk", grad_rows, hidden_gated, preferred_element_type=jnp.float32
    ).astype(jnp.bfloat16)
    grad_two_part = after(
        jnp.einsum("sk,dk->sd", grad_gate_part, full_gate, preferred_element_type=jnp.float32)
        + jnp.einsum("sk,dk->sd", grad_up_part, full_up, preferred_element_type=jnp.float32),
        grad_gate_w,
        grad_up_w,
        grad_down_w,
    ).astype(jnp.bfloat16)
    ffn_branch = lax.psum_scatter(
        combined, "tensor", scatter_dimension=0, tiled=True
    ).astype(jnp.float32)
    output = (middle + ffn_branch).astype(jnp.bfloat16)
    grad_probs = small_sum(count, (gate_dot * kept).T, 6).T
    grad_logits = router_probs * (
        grad_probs - jnp.sum(router_probs * grad_probs, axis=1, keepdims=True)
    )
    logits_low = grad_logits.astype(jnp.bfloat16)
    grad_router = jnp.einsum(
        "sd,se->de", normed_two, logits_low, preferred_element_type=jnp.float32
    )
    own_logits = lax.dynamic_slice_in_dim(logits_low, tensor_rank * local_rows, local_rows)
    sum_gate = lax.psum_scatter(grad_gate_w, "dp", scatter_dimension=0, tiled=True)
    sum_up = lax.psum_scatter(grad_up_w, "dp", scatter_dimension=0, tiled=True)
    sum_down = lax.psum_scatter(grad_down_w, "dp", scatter_dimension=0, tiled=True)
    router_part = jnp.einsum(
        "se,de->sd", own_logits, full_router, preferred_element_type=jnp.float32
    )
    grad_attn_rows, grad_middle, grad_ffn_gain = middle_back_exchange(
        count, grad_two_part, router_part, middle, cotangent, ffn_scale[None, :]
    )
    grad_out_w = jnp.einsum(
        "sf,sd->df", mixed_low, grad_attn_rows, preferred_element_type=jnp.float32
    ).astype(jnp.bfloat16)
    grad_router_wide = jnp.pad(grad_router, ((0, 0), (0, 128 - EXPERTS))).astype(jnp.bfloat16)
    sum_out_router = lax.psum_scatter(
        jnp.concatenate([grad_out_w, grad_router_wide], axis=1),
        "dp",
        scatter_dimension=0,
        tiled=True,
    ).astype(jnp.float32)
    grad_mixed = jnp.dot(grad_attn_rows, w_o_t, preferred_element_type=jnp.float32).astype(
        jnp.bfloat16
    )
    grad_q_rot, grad_k_rot, grad_v = attend_back(
        q_rot,
        k_rot,
        value_heads,
        block_row,
        after(log_totals, ffn_branch),
        grad_mixed.reshape(seq_len, heads_here, HEAD_DIM),
    )
    grad_query_normed = rotate_back(grad_q_rot, cosine_table, sine_table).reshape(
        seq_len, head_cols
    )
    grad_key_normed = rotate_back(grad_k_rot, cosine_table, sine_table).reshape(seq_len, head_cols)
    grad_query_gain = jnp.sum(grad_query_normed * query_normed, axis=0)
    grad_key_gain = jnp.sum(grad_key_normed * key_normed, axis=0)
    query_scaled = grad_query_normed * query_scale
    key_scaled = grad_key_normed * key_scale
    dots = jnp.stack(
        [jnp.sum(query_scaled * query_normed, axis=1), jnp.sum(key_scaled * key_normed, axis=1)]
    )
    query_dot, key_dot = small_sum(count, after(dots, sum_gate, sum_up), 7)
    grad_query_proj = (
        query_inv * (query_scaled - query_normed * (query_dot / model_width)[:, None])
    ).astype(jnp.bfloat16)
    grad_key_proj = (key_inv * (key_scaled - key_normed * (key_dot / model_width)[:, None])).astype(
        jnp.bfloat16
    )
    grad_value_low = grad_v.reshape(seq_len, head_cols).astype(jnp.bfloat16)
    grad_qkv = jnp.concatenate([grad_query_proj, grad_key_proj, grad_value_low], axis=1)
    grad_qkv_w = jnp.einsum(
        "sd,sf->df", normed, grad_qkv, preferred_element_type=jnp.float32
    ).astype(jnp.bfloat16)
    grad_normed_part = jnp.einsum(
        "sf,df->sd", grad_qkv, w_qkv, preferred_element_type=jnp.float32
    ).astype(jnp.bfloat16)
    grad_source, grad_attn_gain = end_exchange(
        count, grad_normed_part, grad_middle, tokens, after(attn_scale[None, :], sum_down)
    )
    sum_out_router = after(sum_out_router, grad_attn_gain[None])
    sum_out = sum_out_router[:, :head_cols]
    sum_router = sum_out_router[:, head_cols : head_cols + EXPERTS]
    zero_cols = jnp.zeros((model_width,), jnp.float32)
    query_gain_full = lax.dynamic_update_slice_in_dim(zero_cols, grad_query_gain, col_start, 0)
    key_gain_full = lax.dynamic_update_slice_in_dim(zero_cols, grad_key_gain, col_start, 0)
    gain_stack = jnp.stack([grad_attn_gain, query_gain_full, key_gain_full, grad_ffn_gain])
    total_rows = lax.psum(
        gain_stack,
        ("dp", "tensor"),
    )
    dp_rank = lax.axis_index("dp")
    gain_width = model_width // (lax.axis_size("dp") * count)
    gain_sums = lax.dynamic_slice_in_dim(
        total_rows, (dp_rank * count + tensor_rank) * gain_width, gain_width, 1
    )
    sum_qkv = lax.psum_scatter(grad_qkv_w, "dp", scatter_dimension=0, tiled=True).astype(
        jnp.float32
    )
    grad_gate = sum_gate.reshape(shard_width, EXPERTS, ff_here).transpose(1, 0, 2)
    grad_up = sum_up.reshape(shard_width, EXPERTS, ff_here).transpose(1, 0, 2)
    grad_down = sum_down.reshape(shard_width, EXPERTS, ff_here).transpose(1, 2, 0)
    return (
        output,
        grad_source,
        gain_sums[0],
        gain_sums[1],
        gain_sums[2],
        sum_qkv[:, :head_cols],
        sum_qkv[:, head_cols : 2 * head_cols],
        sum_qkv[:, 2 * head_cols :],
        sum_out.T.astype(jnp.float32),
        gain_sums[3],
        sum_router,
        grad_gate.astype(jnp.float32),
        grad_up.astype(jnp.float32),
        grad_down.astype(jnp.float32),
    )


def solution(mesh):
    placed = (
        P(("dp", "tensor"), None),
        P(("dp", "tensor"), None),
        P("dp", None),
        P("dp", None),
        P("dp"),
        P("dp"),
        P("dp"),
        P("dp", "tensor"),
        P("dp", "tensor"),
        P("dp", "tensor"),
        P("tensor", "dp"),
        P("dp"),
        P("dp", None),
        P(None, "dp", "tensor"),
        P(None, "dp", "tensor"),
        P(None, "tensor", "dp"),
    )
    return jax.shard_map(
        local,
        mesh=mesh,
        in_specs=placed,
        out_specs=(
            P(("dp", "tensor"), None),
            P(("dp", "tensor"), None),
            P(("dp", "tensor")),
            P(("dp", "tensor")),
            P(("dp", "tensor")),
            P("dp", "tensor"),
            P("dp", "tensor"),
            P("dp", "tensor"),
            P("tensor", "dp"),
            P(("dp", "tensor")),
            P("dp", None),
            P(None, "dp", "tensor"),
            P(None, "dp", "tensor"),
            P(None, "tensor", "dp"),
        ),
        check_vma=False,
    )
```

```python
import math

import jax
import jax.numpy as jnp
from jax import lax
from jax.experimental import pallas as pl
from jax.experimental.pallas import tpu as pltpu
from jax.sharding import PartitionSpec as P

HEAD_DIM = 128
EXPERTS = 8
TOPK = 2
QROWS = 512
CAP = 320


EPSILON = 1e-05
MASKED = -1e30
MESH = pl.DeviceIdType.MESH
CHUNK_ROWS = 16


def rms_scale(source):
    return source * lax.rsqrt(jnp.mean(source * source, axis=-1, keepdims=True) + EPSILON)


def norm_back(source, gain_vec, grad_out):
    inverse = lax.rsqrt(jnp.mean(source * source, axis=-1, keepdims=True) + EPSILON)
    normed = source * inverse
    grad_gain = jnp.sum(grad_out * normed, axis=0)
    scaled = grad_out * gain_vec
    grad_in = inverse * (scaled - normed * jnp.mean(scaled * normed, axis=-1, keepdims=True))
    return (grad_in, grad_gain)


def rope_tables(seq_len, head_dim):
    half_dim = head_dim // 2
    frequency = jnp.exp(
        -math.log(10000.0) * 2.0 * jnp.arange(half_dim, dtype=jnp.float32) / head_dim
    )
    angles = jnp.arange(seq_len, dtype=jnp.float32)[:, None] * frequency[None, :]
    return (
        jnp.concatenate([jnp.cos(angles)] * 2, axis=1),
        jnp.concatenate([jnp.sin(angles)] * 2, axis=1),
    )


def rotate(heads_in, cosine_table, sine_table):
    half_dim = heads_in.shape[-1] // 2
    turned = jnp.concatenate([-heads_in[..., half_dim:], heads_in[..., :half_dim]], axis=-1)
    return heads_in * cosine_table[:, None, :] + turned * sine_table[:, None, :]


def rotate_back(grad_in, cosine_table, sine_table):
    half_dim = grad_in.shape[-1] // 2
    sined = grad_in * sine_table[:, None, :]
    turned = jnp.concatenate([sined[..., half_dim:], -sined[..., :half_dim]], axis=-1)
    return grad_in * cosine_table[:, None, :] + turned


def attend(q_rot, k_rot, value_heads, block_row):
    seq_len, heads_here, head_dim = q_rot.shape
    blocks = seq_len // QROWS
    score_scale = head_dim ** (-0.5)
    q_blocks = q_rot.reshape(blocks, QROWS, heads_here, head_dim)
    id_blocks = block_row.reshape(blocks, QROWS)

    def per_block(block_item):
        q_block, id_block = block_item
        scores = (
            jnp.einsum("qhd,khd->hqk", q_block, k_rot, preferred_element_type=jnp.float32)
            * score_scale
        )
        allowed = block_row[None, None, :] <= id_block[None, :, None]
        scores = jnp.where(allowed, scores, MASKED)
        row_top = jnp.max(scores, axis=-1, keepdims=True)
        row_sum = jnp.sum(jnp.exp(scores - row_top), axis=-1, keepdims=True)
        log_total = row_top + jnp.log(row_sum)
        weights_low = jnp.exp(scores - log_total).astype(jnp.bfloat16)
        mixed_block = jnp.einsum(
            "hqk,khd->qhd", weights_low, value_heads, preferred_element_type=jnp.float32
        )
        return (mixed_block.reshape(QROWS, heads_here * head_dim), log_total[..., 0])

    mixed_blocks, log_totals = lax.map(per_block, (q_blocks, id_blocks))
    return (mixed_blocks.reshape(seq_len, heads_here * head_dim), log_totals)


def attend_back(q_rot, k_rot, value_heads, block_row, log_totals, grad_mixed):
    seq_len, heads_here, head_dim = q_rot.shape
    blocks = seq_len // QROWS
    score_scale = head_dim ** (-0.5)
    q_blocks = q_rot.reshape(blocks, QROWS, heads_here, head_dim)
    g_blocks = grad_mixed.reshape(blocks, QROWS, heads_here, head_dim)
    id_blocks = block_row.reshape(blocks, QROWS)

    def back_block(running, block_item):
        q_block, g_block, id_block, log_block = block_item
        scores = (
            jnp.einsum("qhd,khd->hqk", q_block, k_rot, preferred_element_type=jnp.float32)
            * score_scale
        )
        allowed = block_row[None, None, :] <= id_block[None, :, None]
        scores = jnp.where(allowed, scores, MASKED)
        weights = jnp.exp(scores - log_block[..., None])
        weights_low = weights.astype(jnp.bfloat16)
        grad_weights = jnp.einsum(
            "qhd,khd->hqk", g_block, value_heads, preferred_element_type=jnp.float32
        )
        grad_scores = weights * (
            grad_weights - jnp.sum(weights * grad_weights, axis=-1, keepdims=True)
        )
        grad_low = grad_scores.astype(jnp.bfloat16)
        grad_query = (
            jnp.einsum("hqk,khd->qhd", grad_low, k_rot, preferred_element_type=jnp.float32)
            * score_scale
        )
        grad_key = (
            running[0]
            + jnp.einsum("hqk,qhd->khd", grad_low, q_block, preferred_element_type=jnp.float32)
            * score_scale
        )
        grad_value = running[1] + jnp.einsum(
            "hqk,qhd->khd", weights_low, g_block, preferred_element_type=jnp.float32
        )
        return ((grad_key, grad_value), grad_query)

    zero_heads = jnp.zeros(k_rot.shape, jnp.float32)
    sums_out, grad_query = lax.scan(
        back_block, (zero_heads, zero_heads), (q_blocks, g_blocks, id_blocks, log_totals)
    )
    return (grad_query.reshape(seq_len, heads_here, head_dim), sums_out[0], sums_out[1])


def kept_mask(route_rows):
    expert_ids = jnp.arange(EXPERTS, dtype=jnp.int32)
    first = (route_rows[:, 0:1] == expert_ids[None, :]).astype(jnp.int32)
    second = (route_rows[:, 1:2] == expert_ids[None, :]).astype(jnp.int32)
    both = first + second
    earlier = jnp.cumsum(both, axis=0) - both
    return jnp.where((both > 0) & (earlier < CAP), 1.0, 0.0).astype(jnp.float32)


def neighbour_barrier(me, count):
    barrier = pltpu.get_barrier_semaphore()

    @pl.when(me > 0)
    def _():
        pl.semaphore_signal(barrier, inc=1, device_id={"tensor": me - 1}, device_id_type=MESH)

    @pl.when(me < count - 1)
    def _():
        pl.semaphore_signal(barrier, inc=1, device_id={"tensor": me + 1}, device_id_type=MESH)

    pl.semaphore_wait(
        barrier, jnp.minimum(me, 1).astype(jnp.int32) + jnp.minimum(count - 1 - me, 1)
    )


def line_exchange(
    count, chunks, rows, width, part, extras, out_shapes, epilogue, gather, collective_id, prologue=None
):
    reduce = part is not None
    n_extra = len(extras)
    n_out = len(out_shapes)
    last = count - 1
    back_lag = last if reduce else 0
    pass_lag = back_lag if reduce else chunks

    def kernel(*refs):
        refs = list(refs)
        part_ref = refs.pop(0) if reduce else None
        extra_refs = [refs.pop(0) for _ in range(n_extra)]
        full_ref = refs.pop(0) if gather else None
        out_refs = [refs.pop(0) for _ in range(n_out)]
        if reduce:
            sum_right, sum_left, acc = refs.pop(0), refs.pop(0), refs.pop(0)
            rs_send_r, rs_recv_r, rs_send_l, rs_recv_l = [refs.pop(0) for _ in range(4)]
        if gather:
            ag_send_r, ag_recv_r, ag_send_l, ag_recv_l = [refs.pop(0) for _ in range(4)]
        me = lax.axis_index("tensor")
        right, left = jnp.minimum(me + 1, last), jnp.maximum(me - 1, 0)

        def remote(source, target, send_sem, recv_sem, device):
            return pltpu.make_async_remote_copy(
                src_ref=source,
                dst_ref=target,
                send_sem=send_sem,
                recv_sem=recv_sem,
                device_id={"tensor": device},
                device_id_type=MESH,
            )

        def rs_right(block, chunk, source=None):
            here = sum_right.at[block, chunk]
            return remote(
                here if source is None else source,
                here,
                rs_send_r.at[block, chunk],
                rs_recv_r.at[block, chunk],
                right,
            )

        def rs_left(block, chunk, source=None):
            here = sum_left.at[block, chunk]
            return remote(
                here if source is None else source,
                here,
                rs_send_l.at[block, chunk],
                rs_recv_l.at[block, chunk],
                left,
            )

        def ag_right(block, chunk):
            here = full_ref.at[block, chunk]
            return remote(
                here, here, ag_send_r.at[block, chunk], ag_recv_r.at[block, chunk], right
            )

        def ag_left(block, chunk):
            here = full_ref.at[block, chunk]
            return remote(here, here, ag_send_l.at[block, chunk], ag_recv_l.at[block, chunk], left)

        neighbour_barrier(me, count)
        if prologue is not None:
            prologue(extra_refs, out_refs)

        def send_right(chunk):
            for step in range(last):
                far = last - step

                @pl.when(jnp.logical_and(me < far, me == 0))
                def _():
                    rs_right(far, chunk, part_ref.at[far, chunk]).start()

                @pl.when(jnp.logical_and(me < far, me > 0))
                def _():
                    rs_right(far, chunk).wait_recv()
                    sum_right[far, chunk] = sum_right[far, chunk] + part_ref[far, chunk]
                    rs_right(far, chunk).start()

        def send_left(chunk):
            for step in range(last):

                @pl.when(jnp.logical_and(me > step, me == last))
                def _():
                    rs_left(step, chunk, part_ref.at[step, chunk]).start()

                @pl.when(jnp.logical_and(me > step, me < last))
                def _():
                    rs_left(step, chunk).wait_recv()
                    sum_left[step, chunk] = sum_left[step, chunk] + part_ref[step, chunk]
                    rs_left(step, chunk).start()

        def finish(chunk):
            if reduce:
                acc[...] = part_ref[me, chunk].astype(jnp.float32)

                @pl.when(me > 0)
                def _():
                    rs_right(me, chunk).wait_recv()
                    acc[...] = acc[...] + sum_right[me, chunk].astype(jnp.float32)

                @pl.when(me < last)
                def _():
                    rs_left(me, chunk).wait_recv()
                    acc[...] = acc[...] + sum_left[me, chunk].astype(jnp.float32)

                made = epilogue(chunk, acc[...], extra_refs, out_refs)
            else:
                made = epilogue(chunk, None, extra_refs, out_refs)
            if gather:
                full_ref[me, chunk] = made

                @pl.when(me < last)
                def _():
                    ag_right(me, chunk).start()

                @pl.when(me > 0)
                def _():
                    ag_left(me, chunk).start()

        def forward(chunk, step):
            @pl.when(me - step >= 0)
            def _():
                ag_right(jnp.maximum(me - step, 0), chunk).wait_recv()

            @pl.when(jnp.logical_and(me - step >= 0, me < last))
            def _():
                ag_right(jnp.maximum(me - step, 0), chunk).start()

            @pl.when(me + step <= last)
            def _():
                ag_left(jnp.minimum(me + step, last), chunk).wait_recv()

            @pl.when(jnp.logical_and(me + step <= last, me > 0))
            def _():
                ag_left(jnp.minimum(me + step, last), chunk).start()

        def at_chunk(chunk, work):
            @pl.when(jnp.logical_and(chunk >= 0, chunk < chunks))
            def _():
                work(jnp.clip(chunk, 0, chunks - 1))

        def tick(time, carry):
            if reduce:
                at_chunk(time - me, send_right)
                at_chunk(time - (last - me), send_left)
            at_chunk(time - back_lag, finish)
            if gather:
                for step in range(1, count):
                    at_chunk(time - pass_lag - step, lambda chunk: forward(chunk, step))
            return carry

        ticks = chunks + (pass_lag + last if gather else back_lag)
        lax.fori_loop(0, ticks, tick, 0)

        def drain(chunk, carry):
            for block in range(count):
                if reduce:

                    @pl.when(me < block)
                    def _():
                        rs_right(block, chunk).wait_send()

                    @pl.when(me > block)
                    def _():
                        rs_left(block, chunk).wait_send()

                if gather:

                    @pl.when(jnp.logical_and(block <= me, me < last))
                    def _():
                        ag_right(block, chunk).wait_send()

                    @pl.when(jnp.logical_and(block >= me, me > 0))
                    def _():
                        ag_left(block, chunk).wait_send()

            return carry

        lax.fori_loop(0, chunks, drain, 0)

    block = (count, chunks, rows, width)
    shapes = []
    if gather:
        shapes.append(jax.ShapeDtypeStruct(block, jnp.bfloat16))
    shapes.extend(out_shapes)
    scratch = []
    if reduce:
        scratch += [
            pltpu.VMEM(block, jnp.bfloat16),
            pltpu.VMEM(block, jnp.bfloat16),
            pltpu.VMEM((rows, width), jnp.float32),
        ]
        scratch += [pltpu.SemaphoreType.DMA((count, chunks))] * 4
    if gather:
        scratch += [pltpu.SemaphoreType.DMA((count, chunks))] * 4
    operands = ([part] if reduce else []) + list(extras)
    block_bytes = count * chunks * rows * width * 2
    results = pl.pallas_call(
        kernel,
        out_shape=tuple(shapes),
        in_specs=[pl.BlockSpec(memory_space=pltpu.VMEM)] * len(operands),
        out_specs=tuple([pl.BlockSpec(memory_space=pltpu.VMEM)] * len(shapes)),
        scratch_shapes=scratch,
        compiler_params=pltpu.CompilerParams(
            collective_id=collective_id, has_side_effects=True, vmem_limit_bytes=56 * 1024 * 1024
        ),
        cost_estimate=pl.CostEstimate(
            flops=0,
            bytes_accessed=block_bytes * (60 if reduce and gather else 45),
            transcendentals=0,
        ),
    )(*operands)
    return results


def small_sum(count, values, collective_id, axis="tensor"):
    def kernel(in_ref, out_ref, slots, send_sems, recv_sems):
        me = lax.axis_index(axis)
        barrier = pltpu.get_barrier_semaphore()
        for offset in range(1, count):
            peer = lax.rem(me + offset, count)
            pl.semaphore_signal(barrier, inc=1, device_id={axis: peer}, device_id_type=MESH)
        pl.semaphore_wait(barrier, count - 1)

        def send(offset):
            return pltpu.make_async_remote_copy(
                src_ref=in_ref,
                dst_ref=slots.at[offset - 1],
                send_sem=send_sems.at[offset - 1],
                recv_sem=recv_sems.at[offset - 1],
                device_id={axis: lax.rem(me + offset, count)},
                device_id_type=MESH,
            )

        for offset in range(1, count):
            send(offset).start()
        total = in_ref[...]
        for offset in range(1, count):
            send(offset).wait_recv()
            total = total + slots[offset - 1]
        out_ref[...] = total
        for offset in range(1, count):
            send(offset).wait_send()

    return pl.pallas_call(
        kernel,
        out_shape=jax.ShapeDtypeStruct(values.shape, jnp.float32),
        in_specs=[pl.BlockSpec(memory_space=pltpu.VMEM)],
        out_specs=pl.BlockSpec(memory_space=pltpu.VMEM),
        scratch_shapes=[
            pltpu.VMEM((count - 1,) + values.shape, jnp.float32),
            pltpu.SemaphoreType.DMA((count - 1,)),
            pltpu.SemaphoreType.DMA((count - 1,)),
        ],
        compiler_params=pltpu.CompilerParams(collective_id=collective_id, has_side_effects=True),
    )(values)


def start_gather(count, tokens, gain_row):
    rows, width = tokens.shape
    step, chunks = CHUNK_ROWS, rows // CHUNK_ROWS

    def epilogue(chunk, total, extra_refs, out_refs):
        value = extra_refs[0][chunk].astype(jnp.float32)
        return (rms_scale(value) * extra_refs[1][...]).astype(jnp.bfloat16)

    (full,) = line_exchange(
        count,
        chunks,
        step,
        width,
        None,
        [tokens.reshape(chunks, step, width), gain_row],
        [],
        epilogue,
        True,
        1,
    )
    return full.reshape(count * rows, width)


def middle_exchange(count, branch_part, tokens, gain_row):
    rows, width = tokens.shape
    step, chunks = CHUNK_ROWS, rows // CHUNK_ROWS

    def epilogue(chunk, total, extra_refs, out_refs):
        value = extra_refs[0][chunk].astype(jnp.float32) + total
        out_refs[0][chunk] = value
        return (rms_scale(value) * extra_refs[1][...]).astype(jnp.bfloat16)

    full, middle = line_exchange(
        count,
        chunks,
        step,
        width,
        branch_part.reshape(count, chunks, step, width),
        [tokens.reshape(chunks, step, width), gain_row],
        [jax.ShapeDtypeStruct((chunks, step, width), jnp.float32)],
        epilogue,
        True,
        2,
    )
    return full.reshape(count * rows, width), middle.reshape(rows, width)


def norm_back_rows(value, gain_row, grad_out):
    inverse = lax.rsqrt(jnp.mean(value * value, axis=-1, keepdims=True) + EPSILON)
    normed = value * inverse
    scaled = grad_out * gain_row
    grad_in = inverse * (scaled - normed * jnp.mean(scaled * normed, axis=-1, keepdims=True))
    return grad_in, jnp.sum(grad_out * normed, axis=0, keepdims=True)


def zero_gain(extra_refs, out_refs):
    out_refs[1][...] = jnp.zeros_like(out_refs[1])


def middle_back_exchange(count, grad_part, router_part, middle, cotangent, gain_row):
    rows, width = middle.shape
    step, chunks = CHUNK_ROWS, rows // CHUNK_ROWS

    def epilogue(chunk, total, extra_refs, out_refs):
        grad_out = total + extra_refs[0][chunk]
        grad_in, grad_gain = norm_back_rows(extra_refs[1][chunk], extra_refs[3][...], grad_out)
        out_refs[1][...] = out_refs[1][...] + grad_gain
        grad_middle = extra_refs[2][chunk].astype(jnp.float32) + grad_in
        out_refs[0][chunk] = grad_middle
        return grad_middle.astype(jnp.bfloat16)

    full, grad_middle, grad_gain = line_exchange(
        count,
        chunks,
        step,
        width,
        grad_part.reshape(count, chunks, step, width),
        [
            router_part.reshape(chunks, step, width),
            middle.reshape(chunks, step, width),
            cotangent.reshape(chunks, step, width),
            gain_row,
        ],
        [
            jax.ShapeDtypeStruct((chunks, step, width), jnp.float32),
            jax.ShapeDtypeStruct((1, width), jnp.float32),
        ],
        epilogue,
        True,
        3,
        zero_gain,
    )
    return full.reshape(count * rows, width), grad_middle.reshape(rows, width), grad_gain[0]


def end_exchange(count, grad_part, grad_middle, tokens, gain_row):
    rows, width = tokens.shape
    step, chunks = CHUNK_ROWS, rows // CHUNK_ROWS

    def epilogue(chunk, total, extra_refs, out_refs):
        value = extra_refs[1][chunk].astype(jnp.float32)
        grad_in, grad_gain = norm_back_rows(value, extra_refs[2][...], total)
        out_refs[1][...] = out_refs[1][...] + grad_gain
        out_refs[0][chunk] = extra_refs[0][chunk] + grad_in

    grad_source, grad_gain = line_exchange(
        count,
        chunks,
        step,
        width,
        grad_part.reshape(count, chunks, step, width),
        [
            grad_middle.reshape(chunks, step, width),
            tokens.reshape(chunks, step, width),
            gain_row,
        ],
        [
            jax.ShapeDtypeStruct((chunks, step, width), jnp.float32),
            jax.ShapeDtypeStruct((1, width), jnp.float32),
        ],
        epilogue,
        False,
        4,
        zero_gain,
    )
    return grad_source.reshape(rows, width), grad_gain[0]


def expert_kernel(x_ref, c_ref, gates_ref, wg_ref, wu_ref, wd_ref, hg_ref, dg_ref, du_ref, gd_ref):
    expert = pl.program_id(0)
    rows_in = x_ref[...]
    gate_part = jnp.dot(rows_in, wg_ref[...], preferred_element_type=jnp.float32)
    up_part = jnp.dot(rows_in, wu_ref[...], preferred_element_type=jnp.float32)
    back_hidden = jnp.dot(c_ref[...], wd_ref[...], preferred_element_type=jnp.float32)
    mine = lax.broadcasted_iota(jnp.int32, gates_ref.shape, 1) == expert
    gates = jnp.sum(jnp.where(mine, gates_ref[...], 0.0), axis=1, keepdims=True)
    sigmoid_gate = jax.nn.sigmoid(gate_part)
    silu_gate = gate_part * sigmoid_gate
    hidden = silu_gate * up_part
    gate_dot = jnp.sum(hidden * back_hidden, axis=1, keepdims=True)

    @pl.when(expert == 0)
    def _():
        gd_ref[...] = jnp.zeros_like(gd_ref)

    gd_ref[...] = gd_ref[...] + jnp.where(mine, gate_dot, 0.0)
    hg_ref[...] = (hidden * gates).astype(jnp.bfloat16)
    grad_hidden = back_hidden * gates
    dg_ref[...] = (
        grad_hidden * up_part * sigmoid_gate * (1.0 + gate_part * (1.0 - sigmoid_gate))
    ).astype(jnp.bfloat16)
    du_ref[...] = (grad_hidden * silu_gate).astype(jnp.bfloat16)


def expert_parts(rows_in, rows_grad, gates, weights, ff_here):
    seq_len, width = rows_in.shape
    hidden_cols = EXPERTS * ff_here
    whole = pl.BlockSpec(memory_space=pltpu.VMEM)
    part = jax.ShapeDtypeStruct((seq_len, hidden_cols), jnp.bfloat16)
    column = pl.BlockSpec((seq_len, ff_here), lambda e: (0, e))
    flops = 6 * seq_len * width * hidden_cols
    return pl.pallas_call(
        expert_kernel,
        grid=(EXPERTS,),
        out_shape=(part, part, part, jax.ShapeDtypeStruct((seq_len, EXPERTS), jnp.float32)),
        in_specs=[
            whole,
            whole,
            whole,
            pl.BlockSpec((width, ff_here), lambda e: (0, e)),
            pl.BlockSpec((width, ff_here), lambda e: (0, EXPERTS + e)),
            pl.BlockSpec((width, ff_here), lambda e: (0, 2 * EXPERTS + e)),
        ],
        out_specs=(
            column,
            column,
            column,
            pl.BlockSpec((seq_len, EXPERTS), lambda e: (0, 0)),
        ),
        compiler_params=pltpu.CompilerParams(vmem_limit_bytes=56 * 1024 * 1024),
        cost_estimate=pl.CostEstimate(
            flops=flops, bytes_accessed=weights.size * 2, transcendentals=0
        ),
    )(rows_in, rows_grad, gates, weights, weights, weights)


def product_kernel(hg_ref, dg_ref, du_ref, x_ref, c_ref, w_ref, out_ref, dx_ref, dw_ref):
    cols = hg_ref.shape[1]

    def times_weight(left, which):
        right = w_ref[:, which * cols : (which + 1) * cols]
        return lax.dot_general(
            left, right, (((1,), (1,)), ((), ())), preferred_element_type=jnp.float32
        )

    def weight_grad(rows, grad):
        return lax.dot_general(
            rows, grad, (((0,), (0,)), ((), ())), preferred_element_type=jnp.float32
        ).astype(jnp.bfloat16)

    out_ref[...] = times_weight(hg_ref[...], 2).astype(jnp.bfloat16)
    dx_ref[...] = (times_weight(dg_ref[...], 0) + times_weight(du_ref[...], 1)).astype(
        jnp.bfloat16
    )
    dw_ref[:, :cols] = weight_grad(x_ref[...], dg_ref[...])
    dw_ref[:, cols : 2 * cols] = weight_grad(x_ref[...], du_ref[...])
    dw_ref[:, 2 * cols :] = weight_grad(c_ref[...], hg_ref[...])


def expert_products(hg, dg, du, rows_in, rows_grad, weights):
    seq_len, width = rows_in.shape
    cols = hg.shape[1]
    tile = 256
    whole = pl.BlockSpec(memory_space=pltpu.VMEM)
    column = pl.BlockSpec((seq_len, tile), lambda i: (0, i))
    row = pl.BlockSpec((tile, 3 * cols), lambda i: (i, 0))
    flat = jax.ShapeDtypeStruct((seq_len, width), jnp.bfloat16)
    return pl.pallas_call(
        product_kernel,
        grid=(width // tile,),
        out_shape=(flat, flat, jax.ShapeDtypeStruct((width, 3 * cols), jnp.bfloat16)),
        in_specs=[whole, whole, whole, column, column, row],
        out_specs=(column, column, row),
        compiler_params=pltpu.CompilerParams(vmem_limit_bytes=56 * 1024 * 1024),
        cost_estimate=pl.CostEstimate(
            flops=12 * seq_len * width * cols, bytes_accessed=weights.size * 4, transcendentals=0
        ),
    )(hg, dg, du, rows_in, rows_grad, weights)


def after(value, *others):
    product = 0.0
    for other in others:
        corner = jnp.clip(other[0, 0].astype(jnp.float32), -1.0, 1.0)
        product = corner if other is others[0] else product * corner
    zero = product * 0.0
    return value + zero.astype(value.dtype)


def local(
    tokens,
    cotangent,
    routes,
    block_ids,
    attn_gain,
    q_gain,
    k_gain,
    w_query,
    w_key,
    w_value,
    w_out,
    ffn_gain,
    w_router,
    w_gate,
    w_up,
    w_down,
):
    shard_width = w_query.shape[0]
    head_cols = w_query.shape[1]
    ff_here = w_gate.shape[2]
    hidden_cols = EXPERTS * ff_here
    small = jnp.concatenate(
        [attn_gain[:, None], q_gain[:, None], k_gain[:, None], ffn_gain[:, None], w_router], axis=1
    )
    small = lax.all_gather(small, "dp", axis=0, tiled=True)
    w_qkv = lax.all_gather(
        jnp.concatenate([w_query, w_key, w_value], axis=1), "dp", axis=0, tiled=True
    )
    w_o_t = lax.all_gather(w_out.T, "dp", axis=0, tiled=True)
    expert_local = jnp.concatenate(
        [
            w_gate.transpose(1, 0, 2).reshape(shard_width, hidden_cols),
            w_up.transpose(1, 0, 2).reshape(shard_width, hidden_cols),
            w_down.transpose(2, 0, 1).reshape(shard_width, hidden_cols),
        ],
        axis=1,
    )
    full_router = small[:, 4:]
    model_width = tokens.shape[1]
    local_rows = tokens.shape[0]
    tensor_rank = lax.axis_index("tensor")
    heads_here = head_cols // HEAD_DIM
    col_start = tensor_rank * head_cols
    gains = small[:, :4].astype(jnp.float32).T
    attn_scale = gains[0]
    query_scale = lax.dynamic_slice_in_dim(gains[1], col_start, head_cols)
    key_scale = lax.dynamic_slice_in_dim(gains[2], col_start, head_cols)
    ffn_scale = gains[3]
    count = lax.axis_size("tensor")
    normed = start_gather(count, tokens, attn_scale[None, :])
    grad_rows = lax.all_gather(after(cotangent, normed), "tensor", axis=0, tiled=True)
    seq_len = normed.shape[0]
    block_row = block_ids[0]
    cosine_table, sine_table = rope_tables(seq_len, HEAD_DIM)
    projected = jnp.dot(normed, w_qkv, preferred_element_type=jnp.float32)
    query_proj = projected[:, :head_cols]
    key_proj = projected[:, head_cols : 2 * head_cols]
    value_low = projected[:, 2 * head_cols :].astype(jnp.bfloat16)
    squares = jnp.stack(
        [jnp.sum(query_proj * query_proj, axis=1), jnp.sum(key_proj * key_proj, axis=1)]
    )
    query_sq, key_sq = small_sum(count, squares, 5)
    full_experts = lax.all_gather(
        after(expert_local, query_sq[None]), "dp", axis=0, tiled=True
    )
    query_inv = lax.rsqrt(query_sq / model_width + EPSILON)[:, None]
    key_inv = lax.rsqrt(key_sq / model_width + EPSILON)[:, None]
    query_normed = query_proj * query_inv
    key_normed = key_proj * key_inv
    q_rot = rotate(
        (query_normed * query_scale).reshape(seq_len, heads_here, HEAD_DIM),
        cosine_table,
        sine_table,
    ).astype(jnp.bfloat16)
    k_rot = rotate(
        (key_normed * key_scale).reshape(seq_len, heads_here, HEAD_DIM), cosine_table, sine_table
    ).astype(jnp.bfloat16)
    value_heads = value_low.reshape(seq_len, heads_here, HEAD_DIM)
    mixed, log_totals = attend(q_rot, k_rot, value_heads, block_row)
    mixed_low = mixed.astype(jnp.bfloat16)
    branch_part = jnp.einsum(
        "sf,df->sd", mixed_low, w_o_t, preferred_element_type=jnp.float32
    ).astype(jnp.bfloat16)
    normed_two, middle = middle_exchange(count, branch_part, tokens, ffn_scale[None, :])
    logits = jnp.dot(normed_two, full_router, preferred_element_type=jnp.float32)
    router_probs = jax.nn.softmax(logits, axis=-1)
    kept = kept_mask(routes)
    gate_values = router_probs * kept
    hidden_gated, grad_gate_part, grad_up_part, gate_dot = expert_parts(
        normed_two, grad_rows, gate_values, full_experts, ff_here
    )
    combined, grad_two_part, grad_experts_w = expert_products(
        hidden_gated, grad_gate_part, grad_up_part, normed_two, grad_rows, full_experts
    )
    ffn_branch = lax.psum_scatter(
        combined, "tensor", scatter_dimension=0, tiled=True
    ).astype(jnp.float32)
    output = (middle + ffn_branch).astype(jnp.bfloat16)
    grad_probs = small_sum(count, (gate_dot * kept).T, 6).T
    grad_logits = router_probs * (
        grad_probs - jnp.sum(router_probs * grad_probs, axis=1, keepdims=True)
    )
    logits_low = grad_logits.astype(jnp.bfloat16)
    grad_router = jnp.einsum(
        "sd,se->de", normed_two, logits_low, preferred_element_type=jnp.float32
    )
    own_logits = lax.dynamic_slice_in_dim(logits_low, tensor_rank * local_rows, local_rows)
    sum_experts = lax.psum_scatter(grad_experts_w, "dp", scatter_dimension=0, tiled=True)
    router_part = jnp.einsum(
        "se,de->sd", own_logits, full_router, preferred_element_type=jnp.float32
    )
    grad_attn_rows, grad_middle, grad_ffn_gain = middle_back_exchange(
        count, grad_two_part, router_part, middle, cotangent, ffn_scale[None, :]
    )
    grad_out_w = jnp.einsum(
        "sf,sd->df", mixed_low, grad_attn_rows, preferred_element_type=jnp.float32
    ).astype(jnp.bfloat16)
    grad_router_wide = jnp.pad(grad_router, ((0, 0), (0, 128 - EXPERTS))).astype(jnp.bfloat16)
    sum_out_router = lax.psum_scatter(
        jnp.concatenate([grad_out_w, grad_router_wide], axis=1),
        "dp",
        scatter_dimension=0,
        tiled=True,
    ).astype(jnp.float32)
    grad_mixed = jnp.dot(grad_attn_rows, w_o_t, preferred_element_type=jnp.float32).astype(
        jnp.bfloat16
    )
    grad_q_rot, grad_k_rot, grad_v = attend_back(
        q_rot,
        k_rot,
        value_heads,
        block_row,
        log_totals,
        grad_mixed.reshape(seq_len, heads_here, HEAD_DIM),
    )
    grad_query_normed = rotate_back(grad_q_rot, cosine_table, sine_table).reshape(
        seq_len, head_cols
    )
    grad_key_normed = rotate_back(grad_k_rot, cosine_table, sine_table).reshape(seq_len, head_cols)
    grad_query_gain = jnp.sum(grad_query_normed * query_normed, axis=0)
    grad_key_gain = jnp.sum(grad_key_normed * key_normed, axis=0)
    query_scaled = grad_query_normed * query_scale
    key_scaled = grad_key_normed * key_scale
    dots = jnp.stack(
        [jnp.sum(query_scaled * query_normed, axis=1), jnp.sum(key_scaled * key_normed, axis=1)]
    )
    query_dot, key_dot = small_sum(count, after(dots, sum_experts), 7)
    grad_query_proj = (
        query_inv * (query_scaled - query_normed * (query_dot / model_width)[:, None])
    ).astype(jnp.bfloat16)
    grad_key_proj = (key_inv * (key_scaled - key_normed * (key_dot / model_width)[:, None])).astype(
        jnp.bfloat16
    )
    grad_value_low = grad_v.reshape(seq_len, head_cols).astype(jnp.bfloat16)
    grad_qkv = jnp.concatenate([grad_query_proj, grad_key_proj, grad_value_low], axis=1)
    grad_qkv_w = jnp.einsum(
        "sd,sf->df", normed, grad_qkv, preferred_element_type=jnp.float32
    ).astype(jnp.bfloat16)
    grad_normed_part = jnp.einsum(
        "sf,df->sd", grad_qkv, w_qkv, preferred_element_type=jnp.float32
    ).astype(jnp.bfloat16)
    grad_source, grad_attn_gain = end_exchange(
        count, grad_normed_part, grad_middle, tokens, after(attn_scale[None, :], ffn_branch)
    )
    sum_out_router = after(sum_out_router, grad_attn_gain[None])
    sum_out = sum_out_router[:, :head_cols]
    sum_router = sum_out_router[:, head_cols : head_cols + EXPERTS]
    zero_cols = jnp.zeros((model_width,), jnp.float32)
    query_gain_full = lax.dynamic_update_slice_in_dim(zero_cols, grad_query_gain, col_start, 0)
    key_gain_full = lax.dynamic_update_slice_in_dim(zero_cols, grad_key_gain, col_start, 0)
    gain_stack = jnp.stack([grad_attn_gain, query_gain_full, key_gain_full, grad_ffn_gain])
    dp_count = lax.axis_size("dp")
    total_rows = small_sum(count, gain_stack, 8)
    total_rows = small_sum(dp_count, total_rows, 9, "dp")
    dp_rank = lax.axis_index("dp")
    gain_width = model_width // (dp_count * count)
    gain_sums = lax.dynamic_slice_in_dim(
        total_rows, (dp_rank * count + tensor_rank) * gain_width, gain_width, 1
    )
    sum_qkv = lax.psum_scatter(grad_qkv_w, "dp", scatter_dimension=0, tiled=True).astype(
        jnp.float32
    )
    grad_gate, grad_up, grad_down = (
        sum_experts[:, k * hidden_cols : (k + 1) * hidden_cols].reshape(
            shard_width, EXPERTS, ff_here
        )
        for k in range(3)
    )
    grad_gate = grad_gate.transpose(1, 0, 2)
    grad_up = grad_up.transpose(1, 0, 2)
    grad_down = grad_down.transpose(1, 2, 0)
    return (
        output,
        grad_source,
        gain_sums[0],
        gain_sums[1],
        gain_sums[2],
        sum_qkv[:, :head_cols],
        sum_qkv[:, head_cols : 2 * head_cols],
        sum_qkv[:, 2 * head_cols :],
        sum_out.T.astype(jnp.float32),
        gain_sums[3],
        sum_router,
        grad_gate.astype(jnp.float32),
        grad_up.astype(jnp.float32),
        grad_down.astype(jnp.float32),
    )


def solution(mesh):
    placed = (
        P(("dp", "tensor"), None),
        P(("dp", "tensor"), None),
        P("dp", None),
        P("dp", None),
        P("dp"),
        P("dp"),
        P("dp"),
        P("dp", "tensor"),
        P("dp", "tensor"),
        P("dp", "tensor"),
        P("tensor", "dp"),
        P("dp"),
        P("dp", None),
        P(None, "dp", "tensor"),
        P(None, "dp", "tensor"),
        P(None, "tensor", "dp"),
    )
    return jax.shard_map(
        local,
        mesh=mesh,
        in_specs=placed,
        out_specs=(
            P(("dp", "tensor"), None),
            P(("dp", "tensor"), None),
            P(("dp", "tensor")),
            P(("dp", "tensor")),
            P(("dp", "tensor")),
            P("dp", "tensor"),
            P("dp", "tensor"),
            P("dp", "tensor"),
            P("tensor", "dp"),
            P(("dp", "tensor")),
            P("dp", None),
            P(None, "dp", "tensor"),
            P(None, "dp", "tensor"),
            P(None, "tensor", "dp"),
        ),
        check_vma=False,
    )
```

```python
import math

import jax
import jax.numpy as jnp
import numpy as np
from jax import lax
from jax.experimental import pallas as pl
from jax.experimental.pallas import tpu as pltpu
from jax.sharding import PartitionSpec as P

HEAD_DIM = 128
EXPERTS = 8
TOPK = 2
BLOCK = 256
CAP = 320


EPSILON = 1e-05
MASKED = -1e30
MESH = pl.DeviceIdType.MESH
CHUNK_ROWS = 16


def rms_scale(source):
    return source * lax.rsqrt(jnp.mean(source * source, axis=-1, keepdims=True) + EPSILON)


def rope_constants(seq_len):
    half_dim = HEAD_DIM // 2
    frequency = np.exp(-math.log(10000.0) * 2.0 * np.arange(half_dim) / HEAD_DIM)
    angles = np.arange(seq_len)[:, None] * frequency[None, :]
    cosine = np.concatenate([np.cos(angles)] * 2, axis=1).astype(np.float32)
    sine = np.concatenate([-np.sin(angles), np.sin(angles)], axis=1).astype(np.float32)
    return jnp.asarray(cosine), jnp.asarray(sine)


def masked_scores(q_rows, k_rows, ids_col, ids_row):
    scores = lax.dot_general(
        q_rows, k_rows, (((1,), (1,)), ((), ())), preferred_element_type=jnp.float32
    ) * (HEAD_DIM ** (-0.5))
    return jnp.where(ids_row <= ids_col, scores, MASKED)


def key_limit(start, seq_len):
    return min(seq_len, start + 2 * BLOCK)


def attend_kernel(
    q_ref, k_ref, v_ref, inv_ref, qg_ref, kg_ref, cos_ref, sin_ref, col_ref, row_ref,
    q_out, k_out, v_out, mixed_out, log_out,
):
    head = pl.program_id(0)
    seq_len = q_ref.shape[0]
    cosine, sine = cos_ref[...], sin_ref[...]

    def turn(rows):
        return (rows * cosine + pltpu.roll(rows, HEAD_DIM // 2, 1) * sine).astype(jnp.bfloat16)

    q_out[...] = turn(q_ref[...] * inv_ref[:, 0:1] * qg_ref[...])
    k_out[...] = turn(k_ref[...] * inv_ref[:, 1:2] * kg_ref[...])
    v_out[...] = v_ref[...].astype(jnp.bfloat16)

    @pl.when(head == 0)
    def _():
        log_out[...] = jnp.zeros_like(log_out)

    for start in range(0, seq_len, BLOCK):
        rows = pl.ds(start, BLOCK)
        keys = pl.ds(0, key_limit(start, seq_len))
        scores = masked_scores(q_out[rows, :], k_out[keys, :], col_ref[rows, :], row_ref[:, keys])
        top = jnp.max(scores, axis=-1, keepdims=True)
        powers = jnp.exp(scores - top)
        total = jnp.sum(powers, axis=-1, keepdims=True)
        weights = (powers * (1.0 / total)).astype(jnp.bfloat16)
        mixed_out[rows, :] = jnp.dot(
            weights, v_out[keys, :], preferred_element_type=jnp.float32
        ).astype(jnp.bfloat16)
        lane = lax.broadcasted_iota(jnp.int32, (BLOCK, log_out.shape[1]), 1)
        log_out[rows, :] = log_out[rows, :] + jnp.where(
            lane == head, top + jnp.log(total), 0.0
        )


def attend(projected, inverses, q_gain_row, k_gain_row, tables, ids_col, ids_row):
    seq_len = projected.shape[0]
    heads = projected.shape[1] // (3 * HEAD_DIM)
    cols = heads * HEAD_DIM
    whole = pl.BlockSpec(memory_space=pltpu.VMEM)
    gain = pl.BlockSpec((1, HEAD_DIM), lambda h: (0, h))
    column = pl.BlockSpec((seq_len, HEAD_DIM), lambda h: (0, h))
    flat = jax.ShapeDtypeStruct((seq_len, cols), jnp.bfloat16)
    return pl.pallas_call(
        attend_kernel,
        grid=(heads,),
        out_shape=(flat, flat, flat, flat, jax.ShapeDtypeStruct((seq_len, heads), jnp.float32)),
        in_specs=[
            column,
            pl.BlockSpec((seq_len, HEAD_DIM), lambda h: (0, heads + h)),
            pl.BlockSpec((seq_len, HEAD_DIM), lambda h: (0, 2 * heads + h)),
            whole,
            gain,
            gain,
            whole,
            whole,
            whole,
            whole,
        ],
        out_specs=(
            column,
            column,
            column,
            column,
            pl.BlockSpec((seq_len, heads), lambda h: (0, 0)),
        ),
        compiler_params=pltpu.CompilerParams(vmem_limit_bytes=48 * 1024 * 1024),
        cost_estimate=pl.CostEstimate(
            flops=20 * seq_len * seq_len * cols, bytes_accessed=projected.size * 4, transcendentals=0
        ),
    )(
        projected, projected, projected, inverses, q_gain_row, k_gain_row, tables[0], tables[1],
        ids_col, ids_row,
    )


def attend_back_kernel(
    q_ref, k_ref, v_ref, g_ref, log_ref, qp_ref, kp_ref, inv_ref, qg_ref, kg_ref, cos_ref, sin_ref,
    col_ref, row_ref, gq_out, gk_out, gv_out, dot_out, qgain_out, kgain_out, dq_acc, dk_acc, dv_acc,
):
    head = pl.program_id(0)
    seq_len = q_ref.shape[0]
    scale = HEAD_DIM ** (-0.5)
    dk_acc[...] = jnp.zeros_like(dk_acc)
    dv_acc[...] = jnp.zeros_like(dv_acc)

    def down(left, right):
        return lax.dot_general(
            left, right, (((0,), (0,)), ((), ())), preferred_element_type=jnp.float32
        )

    for start in range(0, seq_len, BLOCK):
        rows = pl.ds(start, BLOCK)
        keys = pl.ds(0, key_limit(start, seq_len))
        scores = masked_scores(q_ref[rows, :], k_ref[keys, :], col_ref[rows, :], row_ref[:, keys])
        lane = lax.broadcasted_iota(jnp.int32, (BLOCK, log_ref.shape[1]), 1)
        log_total = jnp.sum(jnp.where(lane == head, log_ref[rows, :], 0.0), axis=1, keepdims=True)
        weights = jnp.exp(scores - log_total)
        grad_weights = lax.dot_general(
            g_ref[rows, :],
            v_ref[keys, :],
            (((1,), (1,)), ((), ())),
            preferred_element_type=jnp.float32,
        )
        grad_scores = (
            weights * (grad_weights - jnp.sum(weights * grad_weights, axis=-1, keepdims=True))
        ).astype(jnp.bfloat16)
        dq_acc[rows, :] = (
            jnp.dot(grad_scores, k_ref[keys, :], preferred_element_type=jnp.float32) * scale
        )
        dk_acc[keys, :] = dk_acc[keys, :] + down(grad_scores, q_ref[rows, :]) * scale
        dv_acc[keys, :] = dv_acc[keys, :] + down(weights.astype(jnp.bfloat16), g_ref[rows, :])
    gv_out[...] = dv_acc[...].astype(jnp.bfloat16)
    cosine, sine = cos_ref[...], sin_ref[...]

    @pl.when(head == 0)
    def _():
        dot_out[...] = jnp.zeros_like(dot_out)

    def turn_back(rows):
        return rows * cosine - pltpu.roll(rows, HEAD_DIM // 2, 1) * sine

    lane = lax.broadcasted_iota(jnp.int32, dot_out.shape, 1)
    for which, acc, proj, gain, out, gain_out in (
        (0, dq_acc, qp_ref, qg_ref, gq_out, qgain_out),
        (1, dk_acc, kp_ref, kg_ref, gk_out, kgain_out),
    ):
        grad = turn_back(acc[...])
        normed = proj[...] * inv_ref[:, which : which + 1]
        gain_out[...] = jnp.sum(grad * normed, axis=0, keepdims=True)
        scaled = grad * gain[...]
        out[...] = scaled
        dot_out[...] = dot_out[...] + jnp.where(
            lane == which, jnp.sum(scaled * normed, axis=1, keepdims=True), 0.0
        )


def attend_back(
    q_rot, k_rot, value_low, grad_mixed, log_totals, projected, inverses, q_gain_row, k_gain_row,
    tables, ids_col, ids_row,
):
    seq_len, cols = q_rot.shape
    heads = cols // HEAD_DIM
    whole = pl.BlockSpec(memory_space=pltpu.VMEM)
    gain = pl.BlockSpec((1, HEAD_DIM), lambda h: (0, h))
    column = pl.BlockSpec((seq_len, HEAD_DIM), lambda h: (0, h))
    wide = jax.ShapeDtypeStruct((seq_len, cols), jnp.float32)
    gain_shape = jax.ShapeDtypeStruct((1, cols), jnp.float32)
    return pl.pallas_call(
        attend_back_kernel,
        grid=(heads,),
        out_shape=(
            wide,
            wide,
            jax.ShapeDtypeStruct((seq_len, cols), jnp.bfloat16),
            jax.ShapeDtypeStruct((seq_len, 2), jnp.float32),
            gain_shape,
            gain_shape,
        ),
        in_specs=[
            column,
            column,
            column,
            column,
            whole,
            column,
            pl.BlockSpec((seq_len, HEAD_DIM), lambda h: (0, heads + h)),
            whole,
            gain,
            gain,
            whole,
            whole,
            whole,
            whole,
        ],
        out_specs=(
            column,
            column,
            column,
            pl.BlockSpec((seq_len, 2), lambda h: (0, 0)),
            gain,
            gain,
        ),
        scratch_shapes=[pltpu.VMEM((seq_len, HEAD_DIM), jnp.float32)] * 3,
        compiler_params=pltpu.CompilerParams(vmem_limit_bytes=48 * 1024 * 1024),
        cost_estimate=pl.CostEstimate(
            flops=60 * seq_len * seq_len * cols, bytes_accessed=projected.size * 4, transcendentals=0
        ),
    )(
        q_rot, k_rot, value_low, grad_mixed, log_totals, projected, projected, inverses,
        q_gain_row, k_gain_row, tables[0], tables[1], ids_col, ids_row,
    )


def kept_mask(route_rows):
    expert_ids = jnp.arange(EXPERTS, dtype=jnp.int32)
    first = (route_rows[:, 0:1] == expert_ids[None, :]).astype(jnp.int32)
    second = (route_rows[:, 1:2] == expert_ids[None, :]).astype(jnp.int32)
    both = first + second
    earlier = jnp.cumsum(both, axis=0) - both
    return jnp.where((both > 0) & (earlier < CAP), 1.0, 0.0).astype(jnp.float32)


def neighbour_barrier(me, count):
    barrier = pltpu.get_barrier_semaphore()

    @pl.when(me > 0)
    def _():
        pl.semaphore_signal(barrier, inc=1, device_id={"tensor": me - 1}, device_id_type=MESH)

    @pl.when(me < count - 1)
    def _():
        pl.semaphore_signal(barrier, inc=1, device_id={"tensor": me + 1}, device_id_type=MESH)

    pl.semaphore_wait(
        barrier, jnp.minimum(me, 1).astype(jnp.int32) + jnp.minimum(count - 1 - me, 1)
    )


def line_exchange(
    count, chunks, rows, width, part, extras, out_shapes, epilogue, gather, collective_id, prologue=None
):
    reduce = part is not None
    n_extra = len(extras)
    n_out = len(out_shapes)
    last = count - 1
    back_lag = last if reduce else 0
    pass_lag = back_lag if reduce else chunks

    def kernel(*refs):
        refs = list(refs)
        part_ref = refs.pop(0) if reduce else None
        extra_refs = [refs.pop(0) for _ in range(n_extra)]
        full_ref = refs.pop(0) if gather else None
        out_refs = [refs.pop(0) for _ in range(n_out)]
        if reduce:
            sum_right, sum_left, acc = refs.pop(0), refs.pop(0), refs.pop(0)
            rs_send_r, rs_recv_r, rs_send_l, rs_recv_l = [refs.pop(0) for _ in range(4)]
        if gather:
            ag_send_r, ag_recv_r, ag_send_l, ag_recv_l = [refs.pop(0) for _ in range(4)]
        me = lax.axis_index("tensor")
        right, left = jnp.minimum(me + 1, last), jnp.maximum(me - 1, 0)

        def remote(source, target, send_sem, recv_sem, device):
            return pltpu.make_async_remote_copy(
                src_ref=source,
                dst_ref=target,
                send_sem=send_sem,
                recv_sem=recv_sem,
                device_id={"tensor": device},
                device_id_type=MESH,
            )

        def rs_right(block, chunk, source=None):
            here = sum_right.at[block, chunk]
            return remote(
                here if source is None else source,
                here,
                rs_send_r.at[block, chunk],
                rs_recv_r.at[block, chunk],
                right,
            )

        def rs_left(block, chunk, source=None):
            here = sum_left.at[block, chunk]
            return remote(
                here if source is None else source,
                here,
                rs_send_l.at[block, chunk],
                rs_recv_l.at[block, chunk],
                left,
            )

        def ag_right(block, chunk):
            here = full_ref.at[block, chunk]
            return remote(
                here, here, ag_send_r.at[block, chunk], ag_recv_r.at[block, chunk], right
            )

        def ag_left(block, chunk):
            here = full_ref.at[block, chunk]
            return remote(here, here, ag_send_l.at[block, chunk], ag_recv_l.at[block, chunk], left)

        neighbour_barrier(me, count)
        if prologue is not None:
            prologue(extra_refs, out_refs)

        def send_right(chunk):
            for step in range(last):
                far = last - step

                @pl.when(jnp.logical_and(me < far, me == 0))
                def _():
                    rs_right(far, chunk, part_ref.at[far, chunk]).start()

                @pl.when(jnp.logical_and(me < far, me > 0))
                def _():
                    rs_right(far, chunk).wait_recv()
                    sum_right[far, chunk] = sum_right[far, chunk] + part_ref[far, chunk]
                    rs_right(far, chunk).start()

        def send_left(chunk):
            for step in range(last):

                @pl.when(jnp.logical_and(me > step, me == last))
                def _():
                    rs_left(step, chunk, part_ref.at[step, chunk]).start()

                @pl.when(jnp.logical_and(me > step, me < last))
                def _():
                    rs_left(step, chunk).wait_recv()
                    sum_left[step, chunk] = sum_left[step, chunk] + part_ref[step, chunk]
                    rs_left(step, chunk).start()

        def finish(chunk):
            if reduce:
                acc[...] = part_ref[me, chunk].astype(jnp.float32)

                @pl.when(me > 0)
                def _():
                    rs_right(me, chunk).wait_recv()
                    acc[...] = acc[...] + sum_right[me, chunk].astype(jnp.float32)

                @pl.when(me < last)
                def _():
                    rs_left(me, chunk).wait_recv()
                    acc[...] = acc[...] + sum_left[me, chunk].astype(jnp.float32)

                made = epilogue(chunk, acc[...], extra_refs, out_refs)
            else:
                made = epilogue(chunk, None, extra_refs, out_refs)
            if gather:
                full_ref[me, chunk] = made

                @pl.when(me < last)
                def _():
                    ag_right(me, chunk).start()

                @pl.when(me > 0)
                def _():
                    ag_left(me, chunk).start()

        def forward(chunk, step):
            @pl.when(me - step >= 0)
            def _():
                ag_right(jnp.maximum(me - step, 0), chunk).wait_recv()

            @pl.when(jnp.logical_and(me - step >= 0, me < last))
            def _():
                ag_right(jnp.maximum(me - step, 0), chunk).start()

            @pl.when(me + step <= last)
            def _():
                ag_left(jnp.minimum(me + step, last), chunk).wait_recv()

            @pl.when(jnp.logical_and(me + step <= last, me > 0))
            def _():
                ag_left(jnp.minimum(me + step, last), chunk).start()

        def at_chunk(chunk, work):
            @pl.when(jnp.logical_and(chunk >= 0, chunk < chunks))
            def _():
                work(jnp.clip(chunk, 0, chunks - 1))

        def tick(time, carry):
            if reduce:
                at_chunk(time - me, send_right)
                at_chunk(time - (last - me), send_left)
            at_chunk(time - back_lag, finish)
            if gather:
                for step in range(1, count):
                    at_chunk(time - pass_lag - step, lambda chunk: forward(chunk, step))
            return carry

        ticks = chunks + (pass_lag + last if gather else back_lag)
        lax.fori_loop(0, ticks, tick, 0)

        def drain(chunk, carry):
            for block in range(count):
                if reduce:

                    @pl.when(me < block)
                    def _():
                        rs_right(block, chunk).wait_send()

                    @pl.when(me > block)
                    def _():
                        rs_left(block, chunk).wait_send()

                if gather:

                    @pl.when(jnp.logical_and(block <= me, me < last))
                    def _():
                        ag_right(block, chunk).wait_send()

                    @pl.when(jnp.logical_and(block >= me, me > 0))
                    def _():
                        ag_left(block, chunk).wait_send()

            return carry

        lax.fori_loop(0, chunks, drain, 0)

    block = (count, chunks, rows, width)
    shapes = []
    if gather:
        shapes.append(jax.ShapeDtypeStruct(block, jnp.bfloat16))
    shapes.extend(out_shapes)
    scratch = []
    if reduce:
        scratch += [
            pltpu.VMEM(block, jnp.bfloat16),
            pltpu.VMEM(block, jnp.bfloat16),
            pltpu.VMEM((rows, width), jnp.float32),
        ]
        scratch += [pltpu.SemaphoreType.DMA((count, chunks))] * 4
    if gather:
        scratch += [pltpu.SemaphoreType.DMA((count, chunks))] * 4
    operands = ([part] if reduce else []) + list(extras)
    block_bytes = count * chunks * rows * width * 2
    results = pl.pallas_call(
        kernel,
        out_shape=tuple(shapes),
        in_specs=[pl.BlockSpec(memory_space=pltpu.VMEM)] * len(operands),
        out_specs=tuple([pl.BlockSpec(memory_space=pltpu.VMEM)] * len(shapes)),
        scratch_shapes=scratch,
        compiler_params=pltpu.CompilerParams(
            collective_id=collective_id, has_side_effects=True, vmem_limit_bytes=56 * 1024 * 1024
        ),
        cost_estimate=pl.CostEstimate(
            flops=0,
            bytes_accessed=block_bytes * (60 if reduce and gather else 45),
            transcendentals=0,
        ),
    )(*operands)
    return results


def small_sum(count, values, collective_id, axis="tensor"):
    def kernel(in_ref, out_ref, slots, send_sems, recv_sems):
        me = lax.axis_index(axis)
        barrier = pltpu.get_barrier_semaphore()
        for offset in range(1, count):
            peer = lax.rem(me + offset, count)
            pl.semaphore_signal(barrier, inc=1, device_id={axis: peer}, device_id_type=MESH)
        pl.semaphore_wait(barrier, count - 1)

        def send(offset):
            return pltpu.make_async_remote_copy(
                src_ref=in_ref,
                dst_ref=slots.at[offset - 1],
                send_sem=send_sems.at[offset - 1],
                recv_sem=recv_sems.at[offset - 1],
                device_id={axis: lax.rem(me + offset, count)},
                device_id_type=MESH,
            )

        for offset in range(1, count):
            send(offset).start()
        total = in_ref[...]
        for offset in range(1, count):
            send(offset).wait_recv()
            total = total + slots[offset - 1]
        out_ref[...] = total
        for offset in range(1, count):
            send(offset).wait_send()

    return pl.pallas_call(
        kernel,
        out_shape=jax.ShapeDtypeStruct(values.shape, jnp.float32),
        in_specs=[pl.BlockSpec(memory_space=pltpu.VMEM)],
        out_specs=pl.BlockSpec(memory_space=pltpu.VMEM),
        scratch_shapes=[
            pltpu.VMEM((count - 1,) + values.shape, jnp.float32),
            pltpu.SemaphoreType.DMA((count - 1,)),
            pltpu.SemaphoreType.DMA((count - 1,)),
        ],
        compiler_params=pltpu.CompilerParams(collective_id=collective_id, has_side_effects=True),
    )(values)


def start_gather(count, tokens, gain_row):
    rows, width = tokens.shape
    step, chunks = CHUNK_ROWS, rows // CHUNK_ROWS

    def epilogue(chunk, total, extra_refs, out_refs):
        value = extra_refs[0][chunk].astype(jnp.float32)
        return (rms_scale(value) * extra_refs[1][...]).astype(jnp.bfloat16)

    (full,) = line_exchange(
        count,
        chunks,
        step,
        width,
        None,
        [tokens.reshape(chunks, step, width), gain_row],
        [],
        epilogue,
        True,
        1,
    )
    return full.reshape(count * rows, width)


def middle_exchange(count, branch_part, tokens, gain_row):
    rows, width = tokens.shape
    step, chunks = CHUNK_ROWS, rows // CHUNK_ROWS

    def epilogue(chunk, total, extra_refs, out_refs):
        value = extra_refs[0][chunk].astype(jnp.float32) + total
        out_refs[0][chunk] = value
        return (rms_scale(value) * extra_refs[1][...]).astype(jnp.bfloat16)

    full, middle = line_exchange(
        count,
        chunks,
        step,
        width,
        branch_part.reshape(count, chunks, step, width),
        [tokens.reshape(chunks, step, width), gain_row],
        [jax.ShapeDtypeStruct((chunks, step, width), jnp.float32)],
        epilogue,
        True,
        2,
    )
    return full.reshape(count * rows, width), middle.reshape(rows, width)


def norm_back_rows(value, gain_row, grad_out):
    inverse = lax.rsqrt(jnp.mean(value * value, axis=-1, keepdims=True) + EPSILON)
    normed = value * inverse
    scaled = grad_out * gain_row
    grad_in = inverse * (scaled - normed * jnp.mean(scaled * normed, axis=-1, keepdims=True))
    return grad_in, jnp.sum(grad_out * normed, axis=0, keepdims=True)


def zero_gain(extra_refs, out_refs):
    out_refs[1][...] = jnp.zeros_like(out_refs[1])


def middle_back_exchange(count, grad_part, router_part, middle, cotangent, gain_row):
    rows, width = middle.shape
    step, chunks = CHUNK_ROWS, rows // CHUNK_ROWS

    def epilogue(chunk, total, extra_refs, out_refs):
        grad_out = total + extra_refs[0][chunk]
        grad_in, grad_gain = norm_back_rows(extra_refs[1][chunk], extra_refs[3][...], grad_out)
        out_refs[1][...] = out_refs[1][...] + grad_gain
        grad_middle = extra_refs[2][chunk].astype(jnp.float32) + grad_in
        out_refs[0][chunk] = grad_middle
        return grad_middle.astype(jnp.bfloat16)

    full, grad_middle, grad_gain = line_exchange(
        count,
        chunks,
        step,
        width,
        grad_part.reshape(count, chunks, step, width),
        [
            router_part.reshape(chunks, step, width),
            middle.reshape(chunks, step, width),
            cotangent.reshape(chunks, step, width),
            gain_row,
        ],
        [
            jax.ShapeDtypeStruct((chunks, step, width), jnp.float32),
            jax.ShapeDtypeStruct((1, width), jnp.float32),
        ],
        epilogue,
        True,
        3,
        zero_gain,
    )
    return full.reshape(count * rows, width), grad_middle.reshape(rows, width), grad_gain[0]


def end_exchange(count, grad_part, grad_middle, tokens, gain_row):
    rows, width = tokens.shape
    step, chunks = CHUNK_ROWS, rows // CHUNK_ROWS

    def epilogue(chunk, total, extra_refs, out_refs):
        value = extra_refs[1][chunk].astype(jnp.float32)
        grad_in, grad_gain = norm_back_rows(value, extra_refs[2][...], total)
        out_refs[1][...] = out_refs[1][...] + grad_gain
        out_refs[0][chunk] = extra_refs[0][chunk] + grad_in

    grad_source, grad_gain = line_exchange(
        count,
        chunks,
        step,
        width,
        grad_part.reshape(count, chunks, step, width),
        [
            grad_middle.reshape(chunks, step, width),
            tokens.reshape(chunks, step, width),
            gain_row,
        ],
        [
            jax.ShapeDtypeStruct((chunks, step, width), jnp.float32),
            jax.ShapeDtypeStruct((1, width), jnp.float32),
        ],
        epilogue,
        False,
        4,
        zero_gain,
    )
    return grad_source.reshape(rows, width), grad_gain[0]


def expert_kernel(x_ref, c_ref, gates_ref, wg_ref, wu_ref, wd_ref, hg_ref, dg_ref, du_ref, gd_ref):
    expert = pl.program_id(0)
    rows_in = x_ref[...]
    gate_part = jnp.dot(rows_in, wg_ref[...], preferred_element_type=jnp.float32)
    up_part = jnp.dot(rows_in, wu_ref[...], preferred_element_type=jnp.float32)
    back_hidden = jnp.dot(c_ref[...], wd_ref[...], preferred_element_type=jnp.float32)
    mine = lax.broadcasted_iota(jnp.int32, gates_ref.shape, 1) == expert
    gates = jnp.sum(jnp.where(mine, gates_ref[...], 0.0), axis=1, keepdims=True)
    sigmoid_gate = jax.nn.sigmoid(gate_part)
    silu_gate = gate_part * sigmoid_gate
    hidden = silu_gate * up_part
    gate_dot = jnp.sum(hidden * back_hidden, axis=1, keepdims=True)

    @pl.when(expert == 0)
    def _():
        gd_ref[...] = jnp.zeros_like(gd_ref)

    gd_ref[...] = gd_ref[...] + jnp.where(mine, gate_dot, 0.0)
    hg_ref[...] = (hidden * gates).astype(jnp.bfloat16)
    grad_hidden = back_hidden * gates
    dg_ref[...] = (
        grad_hidden * up_part * sigmoid_gate * (1.0 + gate_part * (1.0 - sigmoid_gate))
    ).astype(jnp.bfloat16)
    du_ref[...] = (grad_hidden * silu_gate).astype(jnp.bfloat16)


def expert_parts(rows_in, rows_grad, gates, weights, ff_here):
    seq_len, width = rows_in.shape
    hidden_cols = EXPERTS * ff_here
    whole = pl.BlockSpec(memory_space=pltpu.VMEM)
    part = jax.ShapeDtypeStruct((seq_len, hidden_cols), jnp.bfloat16)
    column = pl.BlockSpec((seq_len, ff_here), lambda e: (0, e))
    flops = 6 * seq_len * width * hidden_cols
    return pl.pallas_call(
        expert_kernel,
        grid=(EXPERTS,),
        out_shape=(part, part, part, jax.ShapeDtypeStruct((seq_len, EXPERTS), jnp.float32)),
        in_specs=[
            whole,
            whole,
            whole,
            pl.BlockSpec((width, ff_here), lambda e: (0, e)),
            pl.BlockSpec((width, ff_here), lambda e: (0, EXPERTS + e)),
            pl.BlockSpec((width, ff_here), lambda e: (0, 2 * EXPERTS + e)),
        ],
        out_specs=(
            column,
            column,
            column,
            pl.BlockSpec((seq_len, EXPERTS), lambda e: (0, 0)),
        ),
        compiler_params=pltpu.CompilerParams(vmem_limit_bytes=56 * 1024 * 1024),
        cost_estimate=pl.CostEstimate(
            flops=flops, bytes_accessed=weights.size * 2, transcendentals=0
        ),
    )(rows_in, rows_grad, gates, weights, weights, weights)


def product_kernel(hg_ref, dg_ref, du_ref, x_ref, c_ref, w_ref, dx_ref, dw_ref):
    cols = hg_ref.shape[1]

    def times_weight(left, which):
        right = w_ref[:, which * cols : (which + 1) * cols]
        return lax.dot_general(
            left, right, (((1,), (1,)), ((), ())), preferred_element_type=jnp.float32
        )

    def weight_grad(rows, grad):
        return lax.dot_general(
            rows, grad, (((0,), (0,)), ((), ())), preferred_element_type=jnp.float32
        ).astype(jnp.bfloat16)

    dx_ref[...] = (times_weight(dg_ref[...], 0) + times_weight(du_ref[...], 1)).astype(
        jnp.bfloat16
    )
    dw_ref[:, :cols] = weight_grad(x_ref[...], dg_ref[...])
    dw_ref[:, cols : 2 * cols] = weight_grad(x_ref[...], du_ref[...])
    dw_ref[:, 2 * cols :] = weight_grad(c_ref[...], hg_ref[...])


def expert_products(hg, dg, du, rows_in, rows_grad, weights):
    seq_len, width = rows_in.shape
    cols = hg.shape[1]
    tile = 256
    whole = pl.BlockSpec(memory_space=pltpu.VMEM)
    column = pl.BlockSpec((seq_len, tile), lambda i: (0, i))
    row = pl.BlockSpec((tile, 3 * cols), lambda i: (i, 0))
    flat = jax.ShapeDtypeStruct((seq_len, width), jnp.bfloat16)
    return pl.pallas_call(
        product_kernel,
        grid=(width // tile,),
        out_shape=(flat, jax.ShapeDtypeStruct((width, 3 * cols), jnp.bfloat16)),
        in_specs=[whole, whole, whole, column, column, row],
        out_specs=(column, row),
        compiler_params=pltpu.CompilerParams(vmem_limit_bytes=56 * 1024 * 1024),
        cost_estimate=pl.CostEstimate(
            flops=10 * seq_len * width * cols, bytes_accessed=weights.size * 4, transcendentals=0
        ),
    )(hg, dg, du, rows_in, rows_grad, weights)


def output_kernel(hg_ref, w_ref, out_ref):
    out_ref[...] = lax.dot_general(
        hg_ref[...], w_ref[...], (((1,), (1,)), ((), ())), preferred_element_type=jnp.float32
    ).astype(jnp.bfloat16)


def expert_output(hg, weights):
    seq_len, cols = hg.shape
    width = weights.shape[0]
    tile = 256
    return pl.pallas_call(
        output_kernel,
        grid=(width // tile,),
        out_shape=jax.ShapeDtypeStruct((seq_len, width), jnp.bfloat16),
        in_specs=[
            pl.BlockSpec(memory_space=pltpu.VMEM),
            pl.BlockSpec((tile, cols), lambda i: (i, 2)),
        ],
        out_specs=pl.BlockSpec((seq_len, tile), lambda i: (0, i)),
        compiler_params=pltpu.CompilerParams(vmem_limit_bytes=40 * 1024 * 1024),
        cost_estimate=pl.CostEstimate(
            flops=2 * seq_len * width * cols, bytes_accessed=width * cols * 2, transcendentals=0
        ),
    )(hg, weights)


def after(value, *others):
    product = 0.0
    for other in others:
        corner = jnp.clip(other[0, 0].astype(jnp.float32), -1.0, 1.0)
        product = corner if other is others[0] else product * corner
    zero = product * 0.0
    return value + zero.astype(value.dtype)


def local(
    tokens,
    cotangent,
    routes,
    block_ids,
    attn_gain,
    q_gain,
    k_gain,
    w_query,
    w_key,
    w_value,
    w_out,
    ffn_gain,
    w_router,
    w_gate,
    w_up,
    w_down,
):
    shard_width = w_query.shape[0]
    head_cols = w_query.shape[1]
    ff_here = w_gate.shape[2]
    hidden_cols = EXPERTS * ff_here
    small = jnp.concatenate(
        [attn_gain[:, None], q_gain[:, None], k_gain[:, None], ffn_gain[:, None], w_router], axis=1
    )
    small = lax.all_gather(small, "dp", axis=0, tiled=True)
    w_heads = lax.all_gather(
        jnp.concatenate([w_query, w_key, w_value, w_out.T], axis=1), "dp", axis=0, tiled=True
    )
    w_qkv = w_heads[:, : 3 * head_cols]
    w_o_t = w_heads[:, 3 * head_cols :]
    expert_local = jnp.concatenate(
        [
            w_gate.transpose(1, 0, 2).reshape(shard_width, hidden_cols),
            w_up.transpose(1, 0, 2).reshape(shard_width, hidden_cols),
            w_down.transpose(2, 0, 1).reshape(shard_width, hidden_cols),
        ],
        axis=1,
    )
    full_router = small[:, 4:]
    model_width = tokens.shape[1]
    local_rows = tokens.shape[0]
    tensor_rank = lax.axis_index("tensor")
    col_start = tensor_rank * head_cols
    gains = small[:, :4].astype(jnp.float32).T
    attn_scale = gains[0]
    query_scale = lax.dynamic_slice_in_dim(gains[1], col_start, head_cols)
    key_scale = lax.dynamic_slice_in_dim(gains[2], col_start, head_cols)
    ffn_scale = gains[3]
    count = lax.axis_size("tensor")
    normed = start_gather(count, tokens, attn_scale[None, :])
    grad_rows = lax.all_gather(after(cotangent, normed), "tensor", axis=0, tiled=True)
    seq_len = normed.shape[0]
    ids_row, ids_col = block_ids, block_ids.T
    tables = rope_constants(seq_len)
    projected = jnp.dot(normed, w_qkv, preferred_element_type=jnp.float32)
    query_proj = projected[:, :head_cols]
    key_proj = projected[:, head_cols : 2 * head_cols]
    squares = jnp.stack(
        [jnp.sum(query_proj * query_proj, axis=1), jnp.sum(key_proj * key_proj, axis=1)]
    )
    squares = small_sum(count, squares, 5)
    full_experts = lax.all_gather(
        after(expert_local, squares), "dp", axis=0, tiled=True
    )
    inverses = lax.rsqrt(squares / model_width + EPSILON).T
    query_row, key_row = query_scale[None, :], key_scale[None, :]
    q_rot, k_rot, value_low, mixed_low, log_totals = attend(
        projected, inverses, query_row, key_row, tables, ids_col, ids_row
    )
    branch_part = jnp.einsum(
        "sf,df->sd", mixed_low, w_o_t, preferred_element_type=jnp.float32
    ).astype(jnp.bfloat16)
    normed_two, middle = middle_exchange(count, branch_part, tokens, ffn_scale[None, :])
    logits = jnp.dot(normed_two, full_router, preferred_element_type=jnp.float32)
    router_probs = jax.nn.softmax(logits, axis=-1)
    kept = kept_mask(routes)
    gate_values = router_probs * kept
    hidden_gated, grad_gate_part, grad_up_part, gate_dot = expert_parts(
        normed_two, grad_rows, gate_values, full_experts, ff_here
    )
    combined = expert_output(hidden_gated, full_experts)
    grad_two_part, grad_experts_w = expert_products(
        hidden_gated,
        grad_gate_part,
        grad_up_part,
        normed_two,
        grad_rows,
        full_experts,
    )
    ffn_branch = lax.psum_scatter(
        combined, "tensor", scatter_dimension=0, tiled=True
    ).astype(jnp.float32)
    output = (middle + ffn_branch).astype(jnp.bfloat16)
    grad_probs = small_sum(count, (gate_dot * kept).T, 6).T
    grad_logits = router_probs * (
        grad_probs - jnp.sum(router_probs * grad_probs, axis=1, keepdims=True)
    )
    logits_low = grad_logits.astype(jnp.bfloat16)
    grad_router = jnp.einsum(
        "sd,se->de", normed_two, logits_low, preferred_element_type=jnp.float32
    )
    own_logits = lax.dynamic_slice_in_dim(logits_low, tensor_rank * local_rows, local_rows)
    sum_experts = lax.psum_scatter(grad_experts_w, "dp", scatter_dimension=0, tiled=True)
    router_part = jnp.einsum(
        "se,de->sd", own_logits, full_router, preferred_element_type=jnp.float32
    )
    grad_attn_rows, grad_middle, grad_ffn_gain = middle_back_exchange(
        count, grad_two_part, router_part, middle, cotangent, ffn_scale[None, :]
    )
    grad_out_w = jnp.einsum(
        "sf,sd->df", mixed_low, grad_attn_rows, preferred_element_type=jnp.float32
    ).astype(jnp.bfloat16)
    grad_mixed = jnp.dot(grad_attn_rows, w_o_t, preferred_element_type=jnp.float32).astype(
        jnp.bfloat16
    )
    query_scaled, key_scaled, grad_value_low, dots, grad_query_gain, grad_key_gain = attend_back(
        q_rot,
        k_rot,
        value_low,
        grad_mixed,
        after(log_totals, ffn_branch),
        projected,
        inverses,
        query_row,
        key_row,
        tables,
        ids_col,
        ids_row,
    )
    dots = small_sum(count, after(dots.T, sum_experts), 7).T / model_width
    query_inv, key_inv = inverses[:, 0:1], inverses[:, 1:2]
    grad_query_proj = (
        query_inv * (query_scaled - query_proj * query_inv * dots[:, 0:1])
    ).astype(jnp.bfloat16)
    grad_key_proj = (key_inv * (key_scaled - key_proj * key_inv * dots[:, 1:2])).astype(
        jnp.bfloat16
    )
    grad_qkv = jnp.concatenate([grad_query_proj, grad_key_proj, grad_value_low], axis=1)
    grad_qkv_w = jnp.einsum(
        "sd,sf->df", normed, grad_qkv, preferred_element_type=jnp.float32
    ).astype(jnp.bfloat16)
    grad_router_wide = jnp.pad(grad_router, ((0, 0), (0, 128 - EXPERTS))).astype(jnp.bfloat16)
    sum_heads = lax.psum_scatter(
        jnp.concatenate([grad_qkv_w, grad_out_w, grad_router_wide], axis=1),
        "dp",
        scatter_dimension=0,
        tiled=True,
    ).astype(jnp.float32)
    grad_normed_part = jnp.einsum(
        "sf,df->sd", grad_qkv, w_qkv, preferred_element_type=jnp.float32
    ).astype(jnp.bfloat16)
    grad_source, grad_attn_gain = end_exchange(
        count, grad_normed_part, grad_middle, tokens, attn_scale[None, :]
    )
    zero_cols = jnp.zeros((model_width,), jnp.float32)
    query_gain_full = lax.dynamic_update_slice_in_dim(zero_cols, grad_query_gain[0], col_start, 0)
    key_gain_full = lax.dynamic_update_slice_in_dim(zero_cols, grad_key_gain[0], col_start, 0)
    gain_stack = jnp.stack([grad_attn_gain, query_gain_full, key_gain_full, grad_ffn_gain])
    dp_count = lax.axis_size("dp")
    total_rows = small_sum(count, gain_stack, 8)
    total_rows = small_sum(dp_count, total_rows, 9, "dp")
    dp_rank = lax.axis_index("dp")
    gain_width = model_width // (dp_count * count)
    gain_sums = lax.dynamic_slice_in_dim(
        total_rows, (dp_rank * count + tensor_rank) * gain_width, gain_width, 1
    )
    sum_qkv = sum_heads[:, : 3 * head_cols]
    sum_out = sum_heads[:, 3 * head_cols : 4 * head_cols]
    sum_router = sum_heads[:, 4 * head_cols : 4 * head_cols + EXPERTS]
    grad_gate, grad_up, grad_down = (
        sum_experts[:, k * hidden_cols : (k + 1) * hidden_cols].reshape(
            shard_width, EXPERTS, ff_here
        )
        for k in range(3)
    )
    grad_gate = grad_gate.transpose(1, 0, 2)
    grad_up = grad_up.transpose(1, 0, 2)
    grad_down = grad_down.transpose(1, 2, 0)
    return (
        output,
        grad_source,
        gain_sums[0],
        gain_sums[1],
        gain_sums[2],
        sum_qkv[:, :head_cols],
        sum_qkv[:, head_cols : 2 * head_cols],
        sum_qkv[:, 2 * head_cols :],
        sum_out.T.astype(jnp.float32),
        gain_sums[3],
        sum_router,
        grad_gate.astype(jnp.float32),
        grad_up.astype(jnp.float32),
        grad_down.astype(jnp.float32),
    )


def solution(mesh):
    placed = (
        P(("dp", "tensor"), None),
        P(("dp", "tensor"), None),
        P("dp", None),
        P("dp", None),
        P("dp"),
        P("dp"),
        P("dp"),
        P("dp", "tensor"),
        P("dp", "tensor"),
        P("dp", "tensor"),
        P("tensor", "dp"),
        P("dp"),
        P("dp", None),
        P(None, "dp", "tensor"),
        P(None, "dp", "tensor"),
        P(None, "tensor", "dp"),
    )
    return jax.shard_map(
        local,
        mesh=mesh,
        in_specs=placed,
        out_specs=(
            P(("dp", "tensor"), None),
            P(("dp", "tensor"), None),
            P(("dp", "tensor")),
            P(("dp", "tensor")),
            P(("dp", "tensor")),
            P("dp", "tensor"),
            P("dp", "tensor"),
            P("dp", "tensor"),
            P("tensor", "dp"),
            P(("dp", "tensor")),
            P("dp", None),
            P(None, "dp", "tensor"),
            P(None, "dp", "tensor"),
            P(None, "tensor", "dp"),
        ),
        check_vma=False,
    )
```

```python
import math

import jax
import jax.numpy as jnp
import numpy as np
from jax import lax
from jax.experimental import pallas as pl
from jax.experimental.pallas import tpu as pltpu
from jax.sharding import PartitionSpec as P

HEAD_DIM = 128
EXPERTS = 8
TOPK = 2
BLOCK = 256
CAP = 320


EPSILON = 1e-05
MASKED = -1e30
MESH = pl.DeviceIdType.MESH
CHUNK_ROWS = 16


def rms_scale(source):
    return source * lax.rsqrt(jnp.mean(source * source, axis=-1, keepdims=True) + EPSILON)


def rope_constants(seq_len):
    half_dim = HEAD_DIM // 2
    frequency = np.exp(-math.log(10000.0) * 2.0 * np.arange(half_dim) / HEAD_DIM)
    angles = np.arange(seq_len)[:, None] * frequency[None, :]
    cosine = np.concatenate([np.cos(angles)] * 2, axis=1).astype(np.float32)
    sine = np.concatenate([-np.sin(angles), np.sin(angles)], axis=1).astype(np.float32)
    return jnp.asarray(cosine), jnp.asarray(sine)


def masked_scores(q_rows, k_rows, ids_col, ids_row):
    scores = lax.dot_general(
        q_rows, k_rows, (((1,), (1,)), ((), ())), preferred_element_type=jnp.float32
    ) * (HEAD_DIM ** (-0.5))
    return jnp.where(ids_row <= ids_col, scores, MASKED)


def key_limit(start, seq_len):
    return min(seq_len, start + 2 * BLOCK)


def attend_kernel(
    q_ref, k_ref, v_ref, inv_ref, qg_ref, kg_ref, cos_ref, sin_ref, col_ref, row_ref,
    q_out, k_out, v_out, mixed_out, log_out,
):
    head = pl.program_id(0)
    seq_len = q_ref.shape[0]
    cosine, sine = cos_ref[...], sin_ref[...]

    def turn(rows):
        return (rows * cosine + pltpu.roll(rows, HEAD_DIM // 2, 1) * sine).astype(jnp.bfloat16)

    q_out[...] = turn(q_ref[...] * inv_ref[:, 0:1] * qg_ref[...])
    k_out[...] = turn(k_ref[...] * inv_ref[:, 1:2] * kg_ref[...])
    v_out[...] = v_ref[...].astype(jnp.bfloat16)

    @pl.when(head == 0)
    def _():
        log_out[...] = jnp.zeros_like(log_out)

    for start in range(0, seq_len, BLOCK):
        rows = pl.ds(start, BLOCK)
        keys = pl.ds(0, key_limit(start, seq_len))
        scores = masked_scores(q_out[rows, :], k_out[keys, :], col_ref[rows, :], row_ref[:, keys])
        top = jnp.max(scores, axis=-1, keepdims=True)
        powers = jnp.exp(scores - top)
        total = jnp.sum(powers, axis=-1, keepdims=True)
        weights = (powers * (1.0 / total)).astype(jnp.bfloat16)
        mixed_out[rows, :] = jnp.dot(
            weights, v_out[keys, :], preferred_element_type=jnp.float32
        ).astype(jnp.bfloat16)
        lane = lax.broadcasted_iota(jnp.int32, (BLOCK, log_out.shape[1]), 1)
        log_out[rows, :] = log_out[rows, :] + jnp.where(
            lane == head, top + jnp.log(total), 0.0
        )


def attend(projected, inverses, q_gain_row, k_gain_row, tables, ids_col, ids_row):
    seq_len = projected.shape[0]
    heads = projected.shape[1] // (3 * HEAD_DIM)
    cols = heads * HEAD_DIM
    whole = pl.BlockSpec(memory_space=pltpu.VMEM)
    gain = pl.BlockSpec((1, HEAD_DIM), lambda h: (0, h))
    column = pl.BlockSpec((seq_len, HEAD_DIM), lambda h: (0, h))
    flat = jax.ShapeDtypeStruct((seq_len, cols), jnp.bfloat16)
    return pl.pallas_call(
        attend_kernel,
        grid=(heads,),
        out_shape=(flat, flat, flat, flat, jax.ShapeDtypeStruct((seq_len, heads), jnp.float32)),
        in_specs=[
            column,
            pl.BlockSpec((seq_len, HEAD_DIM), lambda h: (0, heads + h)),
            pl.BlockSpec((seq_len, HEAD_DIM), lambda h: (0, 2 * heads + h)),
            whole,
            gain,
            gain,
            whole,
            whole,
            whole,
            whole,
        ],
        out_specs=(
            column,
            column,
            column,
            column,
            pl.BlockSpec((seq_len, heads), lambda h: (0, 0)),
        ),
        compiler_params=pltpu.CompilerParams(vmem_limit_bytes=48 * 1024 * 1024),
        cost_estimate=pl.CostEstimate(
            flops=20 * seq_len * seq_len * cols, bytes_accessed=projected.size * 4, transcendentals=0
        ),
    )(
        projected, projected, projected, inverses, q_gain_row, k_gain_row, tables[0], tables[1],
        ids_col, ids_row,
    )


def attend_back_kernel(
    q_ref, k_ref, v_ref, g_ref, log_ref, qp_ref, kp_ref, inv_ref, qg_ref, kg_ref, cos_ref, sin_ref,
    col_ref, row_ref, gq_out, gk_out, gv_out, dot_out, qgain_out, kgain_out, dq_acc, dk_acc, dv_acc,
):
    head = pl.program_id(0)
    seq_len = q_ref.shape[0]
    scale = HEAD_DIM ** (-0.5)
    dk_acc[...] = jnp.zeros_like(dk_acc)
    dv_acc[...] = jnp.zeros_like(dv_acc)

    def down(left, right):
        return lax.dot_general(
            left, right, (((0,), (0,)), ((), ())), preferred_element_type=jnp.float32
        )

    for start in range(0, seq_len, BLOCK):
        rows = pl.ds(start, BLOCK)
        keys = pl.ds(0, key_limit(start, seq_len))
        scores = masked_scores(q_ref[rows, :], k_ref[keys, :], col_ref[rows, :], row_ref[:, keys])
        lane = lax.broadcasted_iota(jnp.int32, (BLOCK, log_ref.shape[1]), 1)
        log_total = jnp.sum(jnp.where(lane == head, log_ref[rows, :], 0.0), axis=1, keepdims=True)
        weights = jnp.exp(scores - log_total)
        grad_weights = lax.dot_general(
            g_ref[rows, :],
            v_ref[keys, :],
            (((1,), (1,)), ((), ())),
            preferred_element_type=jnp.float32,
        )
        grad_scores = (
            weights * (grad_weights - jnp.sum(weights * grad_weights, axis=-1, keepdims=True))
        ).astype(jnp.bfloat16)
        dq_acc[rows, :] = (
            jnp.dot(grad_scores, k_ref[keys, :], preferred_element_type=jnp.float32) * scale
        )
        dk_acc[keys, :] = dk_acc[keys, :] + down(grad_scores, q_ref[rows, :]) * scale
        dv_acc[keys, :] = dv_acc[keys, :] + down(weights.astype(jnp.bfloat16), g_ref[rows, :])
    gv_out[...] = dv_acc[...].astype(jnp.bfloat16)
    cosine, sine = cos_ref[...], sin_ref[...]

    @pl.when(head == 0)
    def _():
        dot_out[...] = jnp.zeros_like(dot_out)

    def turn_back(rows):
        return rows * cosine - pltpu.roll(rows, HEAD_DIM // 2, 1) * sine

    lane = lax.broadcasted_iota(jnp.int32, dot_out.shape, 1)
    for which, acc, proj, gain, out, gain_out in (
        (0, dq_acc, qp_ref, qg_ref, gq_out, qgain_out),
        (1, dk_acc, kp_ref, kg_ref, gk_out, kgain_out),
    ):
        grad = turn_back(acc[...])
        normed = proj[...] * inv_ref[:, which : which + 1]
        gain_out[...] = jnp.sum(grad * normed, axis=0, keepdims=True)
        scaled = grad * gain[...]
        out[...] = scaled
        dot_out[...] = dot_out[...] + jnp.where(
            lane == which, jnp.sum(scaled * normed, axis=1, keepdims=True), 0.0
        )


def attend_back(
    q_rot, k_rot, value_low, grad_mixed, log_totals, projected, inverses, q_gain_row, k_gain_row,
    tables, ids_col, ids_row,
):
    seq_len, cols = q_rot.shape
    heads = cols // HEAD_DIM
    whole = pl.BlockSpec(memory_space=pltpu.VMEM)
    gain = pl.BlockSpec((1, HEAD_DIM), lambda h: (0, h))
    column = pl.BlockSpec((seq_len, HEAD_DIM), lambda h: (0, h))
    wide = jax.ShapeDtypeStruct((seq_len, cols), jnp.float32)
    gain_shape = jax.ShapeDtypeStruct((1, cols), jnp.float32)
    return pl.pallas_call(
        attend_back_kernel,
        grid=(heads,),
        out_shape=(
            wide,
            wide,
            jax.ShapeDtypeStruct((seq_len, cols), jnp.bfloat16),
            jax.ShapeDtypeStruct((seq_len, 2), jnp.float32),
            gain_shape,
            gain_shape,
        ),
        in_specs=[
            column,
            column,
            column,
            column,
            whole,
            column,
            pl.BlockSpec((seq_len, HEAD_DIM), lambda h: (0, heads + h)),
            whole,
            gain,
            gain,
            whole,
            whole,
            whole,
            whole,
        ],
        out_specs=(
            column,
            column,
            column,
            pl.BlockSpec((seq_len, 2), lambda h: (0, 0)),
            gain,
            gain,
        ),
        scratch_shapes=[pltpu.VMEM((seq_len, HEAD_DIM), jnp.float32)] * 3,
        compiler_params=pltpu.CompilerParams(vmem_limit_bytes=48 * 1024 * 1024),
        cost_estimate=pl.CostEstimate(
            flops=60 * seq_len * seq_len * cols, bytes_accessed=projected.size * 4, transcendentals=0
        ),
    )(
        q_rot, k_rot, value_low, grad_mixed, log_totals, projected, projected, inverses,
        q_gain_row, k_gain_row, tables[0], tables[1], ids_col, ids_row,
    )


def kept_mask(route_rows):
    expert_ids = jnp.arange(EXPERTS, dtype=jnp.int32)
    first = (route_rows[:, 0:1] == expert_ids[None, :]).astype(jnp.int32)
    second = (route_rows[:, 1:2] == expert_ids[None, :]).astype(jnp.int32)
    both = first + second
    earlier = jnp.cumsum(both, axis=0) - both
    return jnp.where((both > 0) & (earlier < CAP), 1.0, 0.0).astype(jnp.float32)


def neighbour_barrier(me, count):
    barrier = pltpu.get_barrier_semaphore()

    @pl.when(me > 0)
    def _():
        pl.semaphore_signal(barrier, inc=1, device_id={"tensor": me - 1}, device_id_type=MESH)

    @pl.when(me < count - 1)
    def _():
        pl.semaphore_signal(barrier, inc=1, device_id={"tensor": me + 1}, device_id_type=MESH)

    pl.semaphore_wait(
        barrier, jnp.minimum(me, 1).astype(jnp.int32) + jnp.minimum(count - 1 - me, 1)
    )


def line_exchange(
    count, chunks, rows, width, part, extras, out_shapes, epilogue, gather, collective_id, prologue=None, waits=()
):
    reduce = part is not None
    n_extra = len(extras)
    n_out = len(out_shapes)
    last = count - 1
    back_lag = last if reduce else 0
    pass_lag = back_lag if reduce else chunks

    def kernel(*refs):
        refs = list(refs)
        part_ref = refs.pop(0) if reduce else None
        extra_refs = [refs.pop(0) for _ in range(n_extra)]
        del refs[: len(waits)]
        full_ref = refs.pop(0) if gather else None
        out_refs = [refs.pop(0) for _ in range(n_out)]
        if reduce:
            sum_right, sum_left, acc = refs.pop(0), refs.pop(0), refs.pop(0)
            rs_send_r, rs_recv_r, rs_send_l, rs_recv_l = [refs.pop(0) for _ in range(4)]
        if gather:
            ag_send_r, ag_recv_r, ag_send_l, ag_recv_l = [refs.pop(0) for _ in range(4)]
        me = lax.axis_index("tensor")
        right, left = jnp.minimum(me + 1, last), jnp.maximum(me - 1, 0)

        def remote(source, target, send_sem, recv_sem, device):
            return pltpu.make_async_remote_copy(
                src_ref=source,
                dst_ref=target,
                send_sem=send_sem,
                recv_sem=recv_sem,
                device_id={"tensor": device},
                device_id_type=MESH,
            )

        def rs_right(block, chunk, source=None):
            here = sum_right.at[block, chunk]
            return remote(
                here if source is None else source,
                here,
                rs_send_r.at[block, chunk],
                rs_recv_r.at[block, chunk],
                right,
            )

        def rs_left(block, chunk, source=None):
            here = sum_left.at[block, chunk]
            return remote(
                here if source is None else source,
                here,
                rs_send_l.at[block, chunk],
                rs_recv_l.at[block, chunk],
                left,
            )

        def ag_right(block, chunk):
            here = full_ref.at[block, chunk]
            return remote(
                here, here, ag_send_r.at[block, chunk], ag_recv_r.at[block, chunk], right
            )

        def ag_left(block, chunk):
            here = full_ref.at[block, chunk]
            return remote(here, here, ag_send_l.at[block, chunk], ag_recv_l.at[block, chunk], left)

        neighbour_barrier(me, count)
        if prologue is not None:
            prologue(extra_refs, out_refs)

        def send_right(chunk):
            for step in range(last):
                far = last - step

                @pl.when(jnp.logical_and(me < far, me == 0))
                def _():
                    rs_right(far, chunk, part_ref.at[far, chunk]).start()

                @pl.when(jnp.logical_and(me < far, me > 0))
                def _():
                    rs_right(far, chunk).wait_recv()
                    sum_right[far, chunk] = sum_right[far, chunk] + part_ref[far, chunk]
                    rs_right(far, chunk).start()

        def send_left(chunk):
            for step in range(last):

                @pl.when(jnp.logical_and(me > step, me == last))
                def _():
                    rs_left(step, chunk, part_ref.at[step, chunk]).start()

                @pl.when(jnp.logical_and(me > step, me < last))
                def _():
                    rs_left(step, chunk).wait_recv()
                    sum_left[step, chunk] = sum_left[step, chunk] + part_ref[step, chunk]
                    rs_left(step, chunk).start()

        def finish(chunk):
            if reduce:
                acc[...] = part_ref[me, chunk].astype(jnp.float32)

                @pl.when(me > 0)
                def _():
                    rs_right(me, chunk).wait_recv()
                    acc[...] = acc[...] + sum_right[me, chunk].astype(jnp.float32)

                @pl.when(me < last)
                def _():
                    rs_left(me, chunk).wait_recv()
                    acc[...] = acc[...] + sum_left[me, chunk].astype(jnp.float32)

                made = epilogue(chunk, acc[...], extra_refs, out_refs)
            else:
                made = epilogue(chunk, None, extra_refs, out_refs)
            if gather:
                full_ref[me, chunk] = made

                @pl.when(me < last)
                def _():
                    ag_right(me, chunk).start()

                @pl.when(me > 0)
                def _():
                    ag_left(me, chunk).start()

        def forward(chunk, step):
            @pl.when(me - step >= 0)
            def _():
                ag_right(jnp.maximum(me - step, 0), chunk).wait_recv()

            @pl.when(jnp.logical_and(me - step >= 0, me < last))
            def _():
                ag_right(jnp.maximum(me - step, 0), chunk).start()

            @pl.when(me + step <= last)
            def _():
                ag_left(jnp.minimum(me + step, last), chunk).wait_recv()

            @pl.when(jnp.logical_and(me + step <= last, me > 0))
            def _():
                ag_left(jnp.minimum(me + step, last), chunk).start()

        def at_chunk(chunk, work):
            @pl.when(jnp.logical_and(chunk >= 0, chunk < chunks))
            def _():
                work(jnp.clip(chunk, 0, chunks - 1))

        def tick(time, carry):
            if reduce:
                at_chunk(time - me, send_right)
                at_chunk(time - (last - me), send_left)
            at_chunk(time - back_lag, finish)
            if gather:
                for step in range(1, count):
                    at_chunk(time - pass_lag - step, lambda chunk: forward(chunk, step))
            return carry

        ticks = chunks + (pass_lag + last if gather else back_lag)
        lax.fori_loop(0, ticks, tick, 0)

        def drain(chunk, carry):
            for block in range(count):
                if reduce:

                    @pl.when(me < block)
                    def _():
                        rs_right(block, chunk).wait_send()

                    @pl.when(me > block)
                    def _():
                        rs_left(block, chunk).wait_send()

                if gather:

                    @pl.when(jnp.logical_and(block <= me, me < last))
                    def _():
                        ag_right(block, chunk).wait_send()

                    @pl.when(jnp.logical_and(block >= me, me > 0))
                    def _():
                        ag_left(block, chunk).wait_send()

            return carry

        lax.fori_loop(0, chunks, drain, 0)

    block = (count, chunks, rows, width)
    shapes = []
    if gather:
        shapes.append(jax.ShapeDtypeStruct(block, jnp.bfloat16))
    shapes.extend(out_shapes)
    scratch = []
    if reduce:
        scratch += [
            pltpu.VMEM(block, jnp.bfloat16),
            pltpu.VMEM(block, jnp.bfloat16),
            pltpu.VMEM((rows, width), jnp.float32),
        ]
        scratch += [pltpu.SemaphoreType.DMA((count, chunks))] * 4
    if gather:
        scratch += [pltpu.SemaphoreType.DMA((count, chunks))] * 4
    operands = ([part] if reduce else []) + list(extras)
    block_bytes = count * chunks * rows * width * 2
    results = pl.pallas_call(
        kernel,
        out_shape=tuple(shapes),
        in_specs=[pl.BlockSpec(memory_space=pltpu.VMEM)] * len(operands)
        + [pl.BlockSpec(memory_space=pl.ANY)] * len(waits),
        out_specs=tuple([pl.BlockSpec(memory_space=pltpu.VMEM)] * len(shapes)),
        scratch_shapes=scratch,
        compiler_params=pltpu.CompilerParams(
            collective_id=collective_id, has_side_effects=True, vmem_limit_bytes=56 * 1024 * 1024
        ),
        cost_estimate=pl.CostEstimate(
            flops=0,
            bytes_accessed=block_bytes * (60 if reduce and gather else 45),
            transcendentals=0,
        ),
    )(*operands, *waits)
    return results


def small_sum(count, values, collective_id, axis="tensor"):
    def kernel(in_ref, out_ref, slots, send_sems, recv_sems):
        me = lax.axis_index(axis)
        barrier = pltpu.get_barrier_semaphore()
        for offset in range(1, count):
            peer = lax.rem(me + offset, count)
            pl.semaphore_signal(barrier, inc=1, device_id={axis: peer}, device_id_type=MESH)
        pl.semaphore_wait(barrier, count - 1)

        def send(offset):
            return pltpu.make_async_remote_copy(
                src_ref=in_ref,
                dst_ref=slots.at[offset - 1],
                send_sem=send_sems.at[offset - 1],
                recv_sem=recv_sems.at[offset - 1],
                device_id={axis: lax.rem(me + offset, count)},
                device_id_type=MESH,
            )

        for offset in range(1, count):
            send(offset).start()
        total = in_ref[...]
        for offset in range(1, count):
            send(offset).wait_recv()
            total = total + slots[offset - 1]
        out_ref[...] = total
        for offset in range(1, count):
            send(offset).wait_send()

    return pl.pallas_call(
        kernel,
        out_shape=jax.ShapeDtypeStruct(values.shape, jnp.float32),
        in_specs=[pl.BlockSpec(memory_space=pltpu.VMEM)],
        out_specs=pl.BlockSpec(memory_space=pltpu.VMEM),
        scratch_shapes=[
            pltpu.VMEM((count - 1,) + values.shape, jnp.float32),
            pltpu.SemaphoreType.DMA((count - 1,)),
            pltpu.SemaphoreType.DMA((count - 1,)),
        ],
        compiler_params=pltpu.CompilerParams(collective_id=collective_id, has_side_effects=True),
    )(values)


def start_gather(count, tokens):
    rows, width = tokens.shape
    step, chunks = CHUNK_ROWS, rows // CHUNK_ROWS

    def epilogue(chunk, total, extra_refs, out_refs):
        value = extra_refs[0][chunk].astype(jnp.float32)
        return rms_scale(value).astype(jnp.bfloat16)

    (full,) = line_exchange(
        count,
        chunks,
        step,
        width,
        None,
        [tokens.reshape(chunks, step, width)],
        [],
        epilogue,
        True,
        1,
    )
    return full.reshape(count * rows, width)


def middle_exchange(count, branch_part, tokens, gain_row, waits):
    rows, width = tokens.shape
    step, chunks = CHUNK_ROWS, rows // CHUNK_ROWS

    def epilogue(chunk, total, extra_refs, out_refs):
        value = extra_refs[0][chunk].astype(jnp.float32) + total
        out_refs[0][chunk] = value
        return (rms_scale(value) * extra_refs[1][...]).astype(jnp.bfloat16)

    full, middle = line_exchange(
        count,
        chunks,
        step,
        width,
        branch_part.reshape(count, chunks, step, width),
        [tokens.reshape(chunks, step, width), gain_row],
        [jax.ShapeDtypeStruct((chunks, step, width), jnp.float32)],
        epilogue,
        True,
        2,
        None,
        waits,
    )
    return full.reshape(count * rows, width), middle.reshape(rows, width)


def norm_back_rows(value, gain_row, grad_out):
    inverse = lax.rsqrt(jnp.mean(value * value, axis=-1, keepdims=True) + EPSILON)
    normed = value * inverse
    scaled = grad_out * gain_row
    grad_in = inverse * (scaled - normed * jnp.mean(scaled * normed, axis=-1, keepdims=True))
    return grad_in, jnp.sum(grad_out * normed, axis=0, keepdims=True)


def zero_gain(extra_refs, out_refs):
    out_refs[1][...] = jnp.zeros_like(out_refs[1])


def middle_back_exchange(count, grad_part, router_part, middle, cotangent, gain_row):
    rows, width = middle.shape
    step, chunks = CHUNK_ROWS, rows // CHUNK_ROWS

    def epilogue(chunk, total, extra_refs, out_refs):
        grad_out = total + extra_refs[0][chunk]
        grad_in, grad_gain = norm_back_rows(extra_refs[1][chunk], extra_refs[3][...], grad_out)
        out_refs[1][...] = out_refs[1][...] + grad_gain
        grad_middle = extra_refs[2][chunk].astype(jnp.float32) + grad_in
        out_refs[0][chunk] = grad_middle
        return grad_middle.astype(jnp.bfloat16)

    full, grad_middle, grad_gain = line_exchange(
        count,
        chunks,
        step,
        width,
        grad_part.reshape(count, chunks, step, width),
        [
            router_part.reshape(chunks, step, width),
            middle.reshape(chunks, step, width),
            cotangent.reshape(chunks, step, width),
            gain_row,
        ],
        [
            jax.ShapeDtypeStruct((chunks, step, width), jnp.float32),
            jax.ShapeDtypeStruct((1, width), jnp.float32),
        ],
        epilogue,
        True,
        3,
        zero_gain,
    )
    return full.reshape(count * rows, width), grad_middle.reshape(rows, width), grad_gain[0]


def end_exchange(count, grad_part, grad_middle, tokens, gain_row):
    rows, width = tokens.shape
    step, chunks = CHUNK_ROWS, rows // CHUNK_ROWS

    def epilogue(chunk, total, extra_refs, out_refs):
        value = extra_refs[1][chunk].astype(jnp.float32)
        grad_in, grad_gain = norm_back_rows(value, extra_refs[2][...], total)
        out_refs[1][...] = out_refs[1][...] + grad_gain
        out_refs[0][chunk] = extra_refs[0][chunk] + grad_in

    grad_source, grad_gain = line_exchange(
        count,
        chunks,
        step,
        width,
        grad_part.reshape(count, chunks, step, width),
        [
            grad_middle.reshape(chunks, step, width),
            tokens.reshape(chunks, step, width),
            gain_row,
        ],
        [
            jax.ShapeDtypeStruct((chunks, step, width), jnp.float32),
            jax.ShapeDtypeStruct((1, width), jnp.float32),
        ],
        epilogue,
        False,
        4,
        zero_gain,
    )
    return grad_source.reshape(rows, width), grad_gain[0]


def expert_kernel(x_ref, c_ref, gates_ref, wg_ref, wu_ref, wd_ref, hg_ref, dg_ref, du_ref, gd_ref):
    expert = pl.program_id(0)
    rows_in = x_ref[...]
    gate_part = jnp.dot(rows_in, wg_ref[...], preferred_element_type=jnp.float32)
    up_part = jnp.dot(rows_in, wu_ref[...], preferred_element_type=jnp.float32)
    back_hidden = jnp.dot(c_ref[...], wd_ref[...], preferred_element_type=jnp.float32)
    mine = lax.broadcasted_iota(jnp.int32, gates_ref.shape, 1) == expert
    gates = jnp.sum(jnp.where(mine, gates_ref[...], 0.0), axis=1, keepdims=True)
    sigmoid_gate = jax.nn.sigmoid(gate_part)
    silu_gate = gate_part * sigmoid_gate
    hidden = silu_gate * up_part
    gate_dot = jnp.sum(hidden * back_hidden, axis=1, keepdims=True)

    @pl.when(expert == 0)
    def _():
        gd_ref[...] = jnp.zeros_like(gd_ref)

    gd_ref[...] = gd_ref[...] + jnp.where(mine, gate_dot, 0.0)
    hg_ref[...] = (hidden * gates).astype(jnp.bfloat16)
    grad_hidden = back_hidden * gates
    dg_ref[...] = (
        grad_hidden * up_part * sigmoid_gate * (1.0 + gate_part * (1.0 - sigmoid_gate))
    ).astype(jnp.bfloat16)
    du_ref[...] = (grad_hidden * silu_gate).astype(jnp.bfloat16)


def expert_parts(rows_in, rows_grad, gates, weights, down, ff_here):
    seq_len, width = rows_in.shape
    hidden_cols = EXPERTS * ff_here
    whole = pl.BlockSpec(memory_space=pltpu.VMEM)
    part = jax.ShapeDtypeStruct((seq_len, hidden_cols), jnp.bfloat16)
    column = pl.BlockSpec((seq_len, ff_here), lambda e: (0, e))
    flops = 6 * seq_len * width * hidden_cols
    return pl.pallas_call(
        expert_kernel,
        grid=(EXPERTS,),
        out_shape=(part, part, part, jax.ShapeDtypeStruct((seq_len, EXPERTS), jnp.float32)),
        in_specs=[
            whole,
            whole,
            whole,
            pl.BlockSpec((width, ff_here), lambda e: (0, e)),
            pl.BlockSpec((width, ff_here), lambda e: (0, EXPERTS + e)),
            pl.BlockSpec((width, ff_here), lambda e: (0, e)),
        ],
        out_specs=(
            column,
            column,
            column,
            pl.BlockSpec((seq_len, EXPERTS), lambda e: (0, 0)),
        ),
        compiler_params=pltpu.CompilerParams(vmem_limit_bytes=56 * 1024 * 1024),
        cost_estimate=pl.CostEstimate(
            flops=flops, bytes_accessed=weights.size * 2, transcendentals=0
        ),
    )(rows_in, rows_grad, gates, weights, weights, down)


def product_kernel(hg_ref, dg_ref, du_ref, x_ref, c_ref, w_ref, dx_ref, dw_ref):
    cols = hg_ref.shape[1]

    def times_weight(left, which):
        right = w_ref[:, which * cols : (which + 1) * cols]
        return lax.dot_general(
            left, right, (((1,), (1,)), ((), ())), preferred_element_type=jnp.float32
        )

    def weight_grad(rows, grad):
        return lax.dot_general(
            rows, grad, (((0,), (0,)), ((), ())), preferred_element_type=jnp.float32
        ).astype(jnp.bfloat16)

    dx_ref[...] = (times_weight(dg_ref[...], 0) + times_weight(du_ref[...], 1)).astype(
        jnp.bfloat16
    )
    dw_ref[:, :cols] = weight_grad(x_ref[...], dg_ref[...])
    dw_ref[:, cols : 2 * cols] = weight_grad(x_ref[...], du_ref[...])
    dw_ref[:, 2 * cols :] = weight_grad(c_ref[...], hg_ref[...])


def expert_products(hg, dg, du, rows_in, rows_grad, weights):
    seq_len, width = rows_in.shape
    cols = hg.shape[1]
    tile = 256
    whole = pl.BlockSpec(memory_space=pltpu.VMEM)
    column = pl.BlockSpec((seq_len, tile), lambda i: (0, i))
    row = pl.BlockSpec((tile, 3 * cols), lambda i: (i, 0))
    pair = pl.BlockSpec((tile, 2 * cols), lambda i: (i, 0))
    flat = jax.ShapeDtypeStruct((seq_len, width), jnp.bfloat16)
    return pl.pallas_call(
        product_kernel,
        grid=(width // tile,),
        out_shape=(flat, jax.ShapeDtypeStruct((width, 3 * cols), jnp.bfloat16)),
        in_specs=[whole, whole, whole, column, column, pair],
        out_specs=(column, row),
        compiler_params=pltpu.CompilerParams(vmem_limit_bytes=56 * 1024 * 1024),
        cost_estimate=pl.CostEstimate(
            flops=10 * seq_len * width * cols, bytes_accessed=weights.size * 4, transcendentals=0
        ),
    )(hg, dg, du, rows_in, rows_grad, weights)


def output_kernel(hg_ref, w_ref, out_ref):
    out_ref[...] = lax.dot_general(
        hg_ref[...], w_ref[...], (((1,), (1,)), ((), ())), preferred_element_type=jnp.float32
    ).astype(jnp.bfloat16)


def expert_output(hg, weights):
    seq_len, cols = hg.shape
    width = weights.shape[0]
    tile = 256
    return pl.pallas_call(
        output_kernel,
        grid=(width // tile,),
        out_shape=jax.ShapeDtypeStruct((seq_len, width), jnp.bfloat16),
        in_specs=[
            pl.BlockSpec(memory_space=pltpu.VMEM),
            pl.BlockSpec((tile, cols), lambda i: (i, 0)),
        ],
        out_specs=pl.BlockSpec((seq_len, tile), lambda i: (0, i)),
        compiler_params=pltpu.CompilerParams(vmem_limit_bytes=40 * 1024 * 1024),
        cost_estimate=pl.CostEstimate(
            flops=2 * seq_len * width * cols, bytes_accessed=width * cols * 2, transcendentals=0
        ),
    )(hg, weights)


def split_kernel(gate_ref, up_ref, down_ref, gate_out, up_out, down_out):
    gate_out[0] = gate_ref[...].astype(jnp.float32)
    up_out[0] = up_ref[...].astype(jnp.float32)
    down_out[0] = down_ref[...].astype(jnp.float32).T


def split_experts(sums, ff_here):
    width = sums.shape[0]

    def part(which):
        return pl.BlockSpec((width, ff_here), lambda e: (0, which * EXPERTS + e))

    wide = jax.ShapeDtypeStruct((EXPERTS, width, ff_here), jnp.float32)
    tall = jax.ShapeDtypeStruct((EXPERTS, ff_here, width), jnp.float32)
    wide_spec = pl.BlockSpec((1, width, ff_here), lambda e: (e, 0, 0))
    tall_spec = pl.BlockSpec((1, ff_here, width), lambda e: (e, 0, 0))
    return pl.pallas_call(
        split_kernel,
        grid=(EXPERTS,),
        out_shape=(wide, wide, tall),
        in_specs=[part(0), part(1), part(2)],
        out_specs=(wide_spec, wide_spec, tall_spec),
    )(sums, sums, sums)


def scatter_sum(dp_count, count, values, collective_id):
    total_count = dp_count * count

    def kernel(in_ref, out_ref, slots, send_sems, recv_sems):
        me = lax.axis_index("dp") * count + lax.axis_index("tensor")

        def peer(offset):
            other = lax.rem(me + offset, total_count)
            return other, {"dp": other // count, "tensor": lax.rem(other, count)}

        barrier = pltpu.get_barrier_semaphore()

        def greet(offset, carry):
            pl.semaphore_signal(
                barrier, inc=1, device_id=peer(offset)[1], device_id_type=MESH
            )
            return carry

        lax.fori_loop(1, total_count, greet, 0)
        pl.semaphore_wait(barrier, total_count - 1)

        def send(offset):
            other, device = peer(offset)
            return pltpu.make_async_remote_copy(
                src_ref=in_ref.at[other],
                dst_ref=slots.at[offset - 1],
                send_sem=send_sems.at[offset - 1],
                recv_sem=recv_sems.at[offset - 1],
                device_id=device,
                device_id_type=MESH,
            )

        def start(offset, carry):
            send(offset).start()
            return carry

        lax.fori_loop(1, total_count, start, 0)

        def collect(offset, total):
            send(offset).wait_recv()
            return total + slots[offset - 1]

        out_ref[...] = lax.fori_loop(1, total_count, collect, in_ref[me])

        def finish(offset, carry):
            send(offset).wait_send()
            return carry

        lax.fori_loop(1, total_count, finish, 0)

    block = values.shape[1:]
    return pl.pallas_call(
        kernel,
        out_shape=jax.ShapeDtypeStruct(block, jnp.float32),
        in_specs=[pl.BlockSpec(memory_space=pltpu.VMEM)],
        out_specs=pl.BlockSpec(memory_space=pltpu.VMEM),
        scratch_shapes=[
            pltpu.VMEM((total_count - 1,) + block, jnp.float32),
            pltpu.SemaphoreType.DMA((total_count - 1,)),
            pltpu.SemaphoreType.DMA((total_count - 1,)),
        ],
        compiler_params=pltpu.CompilerParams(collective_id=collective_id, has_side_effects=True),
    )(values)


def after(value, *others):
    product = 0.0
    for other in others:
        corner = jnp.clip(other[0, 0].astype(jnp.float32), -1.0, 1.0)
        product = corner if other is others[0] else product * corner
    zero = product * 0.0
    return value + zero.astype(value.dtype)


def local(
    tokens,
    cotangent,
    routes,
    block_ids,
    attn_gain,
    q_gain,
    k_gain,
    w_query,
    w_key,
    w_value,
    w_out,
    ffn_gain,
    w_router,
    w_gate,
    w_up,
    w_down,
):
    shard_width = w_query.shape[0]
    head_cols = w_query.shape[1]
    ff_here = w_gate.shape[2]
    hidden_cols = EXPERTS * ff_here
    small_cols = jnp.concatenate(
        [attn_gain[:, None], q_gain[:, None], k_gain[:, None], ffn_gain[:, None], w_router], axis=1
    )
    small_cols = jnp.pad(small_cols, ((0, 0), (0, 128 - small_cols.shape[1])))
    w_heads = lax.all_gather(
        jnp.concatenate([w_query, w_key, w_value, w_out.T, small_cols], axis=1), "dp", axis=0, tiled=True
    )
    w_qkv = w_heads[:, : 3 * head_cols]
    w_o_t = w_heads[:, 3 * head_cols : 4 * head_cols]
    small = w_heads[:, 4 * head_cols : 4 * head_cols + 4 + EXPERTS]
    full_down = lax.all_gather(
        w_down.transpose(2, 0, 1).reshape(shard_width, hidden_cols), "dp", axis=0, tiled=True
    )
    expert_local = jnp.concatenate(
        [
            w_gate.transpose(1, 0, 2).reshape(shard_width, hidden_cols),
            w_up.transpose(1, 0, 2).reshape(shard_width, hidden_cols),
        ],
        axis=1,
    )
    full_router = small[:, 4:]
    model_width = tokens.shape[1]
    local_rows = tokens.shape[0]
    tensor_rank = lax.axis_index("tensor")
    col_start = tensor_rank * head_cols
    gains = small[:, :4].astype(jnp.float32).T
    attn_scale = gains[0]
    query_scale = lax.dynamic_slice_in_dim(gains[1], col_start, head_cols)
    key_scale = lax.dynamic_slice_in_dim(gains[2], col_start, head_cols)
    ffn_scale = gains[3]
    count = lax.axis_size("tensor")
    unit_rows = start_gather(count, tokens)
    normed = (unit_rows.astype(jnp.float32) * attn_scale[None, :]).astype(jnp.bfloat16)
    grad_rows = lax.all_gather(after(cotangent, unit_rows), "tensor", axis=0, tiled=True)
    seq_len = normed.shape[0]
    ids_row, ids_col = block_ids, block_ids.T
    tables = rope_constants(seq_len)
    projected = jnp.dot(normed, w_qkv, preferred_element_type=jnp.float32)
    query_proj = projected[:, :head_cols]
    key_proj = projected[:, head_cols : 2 * head_cols]
    squares = jnp.stack(
        [jnp.sum(query_proj * query_proj, axis=1), jnp.sum(key_proj * key_proj, axis=1)]
    )
    squares = small_sum(count, squares, 5)
    full_gate_up = lax.all_gather(
        after(expert_local, squares), "dp", axis=0, tiled=True
    )
    inverses = lax.rsqrt(squares / model_width + EPSILON).T
    query_row, key_row = query_scale[None, :], key_scale[None, :]
    q_rot, k_rot, value_low, mixed_low, log_totals = attend(
        projected, inverses, query_row, key_row, tables, ids_col, ids_row
    )
    branch_part = jnp.einsum(
        "sf,df->sd", mixed_low, w_o_t, preferred_element_type=jnp.float32
    ).astype(jnp.bfloat16)
    normed_two, middle = middle_exchange(
        count, branch_part, tokens, ffn_scale[None, :], (full_down,)
    )
    logits = jnp.dot(normed_two, full_router, preferred_element_type=jnp.float32)
    router_probs = jax.nn.softmax(logits, axis=-1)
    kept = kept_mask(routes)
    gate_values = router_probs * kept
    hidden_gated, grad_gate_part, grad_up_part, gate_dot = expert_parts(
        normed_two, grad_rows, gate_values, full_gate_up, full_down, ff_here
    )
    combined = expert_output(hidden_gated, full_down)
    grad_two_part, grad_experts_w = expert_products(
        hidden_gated,
        grad_gate_part,
        grad_up_part,
        normed_two,
        grad_rows,
        full_gate_up,
    )
    ffn_branch = lax.psum_scatter(
        combined, "tensor", scatter_dimension=0, tiled=True
    ).astype(jnp.float32)
    output = (middle + ffn_branch).astype(jnp.bfloat16)
    grad_probs = small_sum(count, (gate_dot * kept).T, 6).T
    grad_logits = router_probs * (
        grad_probs - jnp.sum(router_probs * grad_probs, axis=1, keepdims=True)
    )
    logits_low = grad_logits.astype(jnp.bfloat16)
    grad_router = jnp.einsum(
        "sd,se->de", normed_two, logits_low, preferred_element_type=jnp.float32
    )
    own_logits = lax.dynamic_slice_in_dim(logits_low, tensor_rank * local_rows, local_rows)
    sum_experts = lax.psum_scatter(grad_experts_w, "dp", scatter_dimension=0, tiled=True)
    router_part = jnp.einsum(
        "se,de->sd", own_logits, full_router, preferred_element_type=jnp.float32
    )
    grad_attn_rows, grad_middle, grad_ffn_gain = middle_back_exchange(
        count, grad_two_part, router_part, middle, cotangent, ffn_scale[None, :]
    )
    grad_out_w = jnp.einsum(
        "sf,sd->df", mixed_low, grad_attn_rows, preferred_element_type=jnp.float32
    ).astype(jnp.bfloat16)
    grad_mixed = jnp.dot(grad_attn_rows, w_o_t, preferred_element_type=jnp.float32).astype(
        jnp.bfloat16
    )
    query_scaled, key_scaled, grad_value_low, dots, grad_query_gain, grad_key_gain = attend_back(
        q_rot,
        k_rot,
        value_low,
        grad_mixed,
        after(log_totals, ffn_branch),
        projected,
        inverses,
        query_row,
        key_row,
        tables,
        ids_col,
        ids_row,
    )
    dots = small_sum(count, after(dots.T, sum_experts), 7).T / model_width
    query_inv, key_inv = inverses[:, 0:1], inverses[:, 1:2]
    grad_query_proj = (
        query_inv * (query_scaled - query_proj * query_inv * dots[:, 0:1])
    ).astype(jnp.bfloat16)
    grad_key_proj = (key_inv * (key_scaled - key_proj * key_inv * dots[:, 1:2])).astype(
        jnp.bfloat16
    )
    grad_qkv = jnp.concatenate([grad_query_proj, grad_key_proj, grad_value_low], axis=1)
    grad_qkv_w = (
        jnp.einsum("sd,sf->df", unit_rows, grad_qkv, preferred_element_type=jnp.float32)
        * attn_scale[:, None]
    ).astype(jnp.bfloat16)
    grad_router_wide = jnp.pad(grad_router, ((0, 0), (0, 128 - EXPERTS))).astype(jnp.bfloat16)
    sum_heads = lax.psum_scatter(
        jnp.concatenate([grad_qkv_w, grad_out_w, grad_router_wide], axis=1),
        "dp",
        scatter_dimension=0,
        tiled=True,
    ).astype(jnp.float32)
    grad_normed_part = jnp.einsum(
        "sf,df->sd", grad_qkv, w_qkv, preferred_element_type=jnp.float32
    ).astype(jnp.bfloat16)
    grad_source, grad_attn_gain = end_exchange(
        count, grad_normed_part, grad_middle, tokens, attn_scale[None, :]
    )
    zero_cols = jnp.zeros((model_width,), jnp.float32)
    query_gain_full = lax.dynamic_update_slice_in_dim(zero_cols, grad_query_gain[0], col_start, 0)
    key_gain_full = lax.dynamic_update_slice_in_dim(zero_cols, grad_key_gain[0], col_start, 0)
    gain_stack = jnp.stack([grad_attn_gain, query_gain_full, key_gain_full, grad_ffn_gain])
    dp_count = lax.axis_size("dp")
    gain_width = model_width // (dp_count * count)
    gain_blocks = gain_stack.reshape(4, dp_count * count, gain_width).transpose(1, 0, 2)
    gain_blocks = jnp.pad(gain_blocks, ((0, 0), (0, 4), (0, 128 - gain_width)))
    gain_sums = scatter_sum(dp_count, count, gain_blocks, 8)[:4, :gain_width]
    sum_qkv = sum_heads[:, : 3 * head_cols]
    sum_out = sum_heads[:, 3 * head_cols : 4 * head_cols]
    sum_router = sum_heads[:, 4 * head_cols : 4 * head_cols + EXPERTS]
    grad_gate, grad_up, grad_down = split_experts(sum_experts, ff_here)
    return (
        output,
        grad_source,
        gain_sums[0],
        gain_sums[1],
        gain_sums[2],
        sum_qkv[:, :head_cols],
        sum_qkv[:, head_cols : 2 * head_cols],
        sum_qkv[:, 2 * head_cols :],
        sum_out.T.astype(jnp.float32),
        gain_sums[3],
        sum_router,
        grad_gate,
        grad_up,
        grad_down,
    )


def solution(mesh):
    placed = (
        P(("dp", "tensor"), None),
        P(("dp", "tensor"), None),
        P("dp", None),
        P("dp", None),
        P("dp"),
        P("dp"),
        P("dp"),
        P("dp", "tensor"),
        P("dp", "tensor"),
        P("dp", "tensor"),
        P("tensor", "dp"),
        P("dp"),
        P("dp", None),
        P(None, "dp", "tensor"),
        P(None, "dp", "tensor"),
        P(None, "tensor", "dp"),
    )
    return jax.shard_map(
        local,
        mesh=mesh,
        in_specs=placed,
        out_specs=(
            P(("dp", "tensor"), None),
            P(("dp", "tensor"), None),
            P(("dp", "tensor")),
            P(("dp", "tensor")),
            P(("dp", "tensor")),
            P("dp", "tensor"),
            P("dp", "tensor"),
            P("dp", "tensor"),
            P("tensor", "dp"),
            P(("dp", "tensor")),
            P("dp", None),
            P(None, "dp", "tensor"),
            P(None, "dp", "tensor"),
            P(None, "tensor", "dp"),
        ),
        check_vma=False,
    )
```

```python
import math

import jax
import jax.numpy as jnp
import numpy as np
from jax import lax
from jax.experimental import pallas as pl
from jax.experimental.pallas import tpu as pltpu
from jax.sharding import PartitionSpec as P

HEAD_DIM = 128
EXPERTS = 8
TOPK = 2
BLOCK = 256
CAP = 320


EPSILON = 1e-05
MASKED = -1e30
MESH = pl.DeviceIdType.MESH
CHUNK_ROWS = 16


def rms_scale(source):
    return source * lax.rsqrt(jnp.mean(source * source, axis=-1, keepdims=True) + EPSILON)


def rope_constants(seq_len):
    half_dim = HEAD_DIM // 2
    frequency = np.exp(-math.log(10000.0) * 2.0 * np.arange(half_dim) / HEAD_DIM)
    angles = np.arange(seq_len)[:, None] * frequency[None, :]
    cosine = np.concatenate([np.cos(angles)] * 2, axis=1).astype(np.float32)
    sine = np.concatenate([-np.sin(angles), np.sin(angles)], axis=1).astype(np.float32)
    return jnp.asarray(cosine), jnp.asarray(sine)


def masked_scores(q_rows, k_rows, ids_col, ids_row):
    scores = lax.dot_general(
        q_rows, k_rows, (((1,), (1,)), ((), ())), preferred_element_type=jnp.float32
    ) * (HEAD_DIM ** (-0.5))
    return jnp.where(ids_row <= ids_col, scores, MASKED)


def key_limit(start, seq_len):
    return min(seq_len, start + 2 * BLOCK)


def attend_kernel(
    q_ref, k_ref, v_ref, inv_ref, qg_ref, kg_ref, cos_ref, sin_ref, col_ref, row_ref,
    q_out, k_out, v_out, mixed_out, log_out,
):
    head = pl.program_id(0)
    seq_len = q_ref.shape[0]
    cosine, sine = cos_ref[...], sin_ref[...]

    def turn(rows):
        return (rows * cosine + pltpu.roll(rows, HEAD_DIM // 2, 1) * sine).astype(jnp.bfloat16)

    q_out[...] = turn(q_ref[...] * inv_ref[:, 0:1] * qg_ref[...])
    k_out[...] = turn(k_ref[...] * inv_ref[:, 1:2] * kg_ref[...])
    v_out[...] = v_ref[...].astype(jnp.bfloat16)

    @pl.when(head == 0)
    def _():
        log_out[...] = jnp.zeros_like(log_out)

    for start in range(0, seq_len, BLOCK):
        rows = pl.ds(start, BLOCK)
        keys = pl.ds(0, key_limit(start, seq_len))
        scores = masked_scores(q_out[rows, :], k_out[keys, :], col_ref[rows, :], row_ref[:, keys])
        top = jnp.max(scores, axis=-1, keepdims=True)
        powers = jnp.exp(scores - top)
        total = jnp.sum(powers, axis=-1, keepdims=True)
        weights = (powers * (1.0 / total)).astype(jnp.bfloat16)
        mixed_out[rows, :] = jnp.dot(
            weights, v_out[keys, :], preferred_element_type=jnp.float32
        ).astype(jnp.bfloat16)
        lane = lax.broadcasted_iota(jnp.int32, (BLOCK, log_out.shape[1]), 1)
        log_out[rows, :] = log_out[rows, :] + jnp.where(
            lane == head, top + jnp.log(total), 0.0
        )


def attend(projected, inverses, q_gain_row, k_gain_row, tables, ids_col, ids_row):
    seq_len = projected.shape[0]
    heads = projected.shape[1] // (3 * HEAD_DIM)
    cols = heads * HEAD_DIM
    whole = pl.BlockSpec(memory_space=pltpu.VMEM)
    gain = pl.BlockSpec((1, HEAD_DIM), lambda h: (0, h))
    column = pl.BlockSpec((seq_len, HEAD_DIM), lambda h: (0, h))
    flat = jax.ShapeDtypeStruct((seq_len, cols), jnp.bfloat16)
    return pl.pallas_call(
        attend_kernel,
        grid=(heads,),
        out_shape=(flat, flat, flat, flat, jax.ShapeDtypeStruct((seq_len, heads), jnp.float32)),
        in_specs=[
            column,
            pl.BlockSpec((seq_len, HEAD_DIM), lambda h: (0, heads + h)),
            pl.BlockSpec((seq_len, HEAD_DIM), lambda h: (0, 2 * heads + h)),
            whole,
            gain,
            gain,
            whole,
            whole,
            whole,
            whole,
        ],
        out_specs=(
            column,
            column,
            column,
            column,
            pl.BlockSpec((seq_len, heads), lambda h: (0, 0)),
        ),
        compiler_params=pltpu.CompilerParams(vmem_limit_bytes=48 * 1024 * 1024),
        cost_estimate=pl.CostEstimate(
            flops=20 * seq_len * seq_len * cols, bytes_accessed=projected.size * 4, transcendentals=0
        ),
    )(
        projected, projected, projected, inverses, q_gain_row, k_gain_row, tables[0], tables[1],
        ids_col, ids_row,
    )


def attend_back_kernel(
    q_ref, k_ref, v_ref, g_ref, log_ref, qp_ref, kp_ref, inv_ref, qg_ref, kg_ref, cos_ref, sin_ref,
    col_ref, row_ref, gq_out, gk_out, gv_out, dot_out, qgain_out, kgain_out, dq_acc, dk_acc, dv_acc,
):
    head = pl.program_id(0)
    seq_len = q_ref.shape[0]
    scale = HEAD_DIM ** (-0.5)
    dk_acc[...] = jnp.zeros_like(dk_acc)
    dv_acc[...] = jnp.zeros_like(dv_acc)

    def down(left, right):
        return lax.dot_general(
            left, right, (((0,), (0,)), ((), ())), preferred_element_type=jnp.float32
        )

    for start in range(0, seq_len, BLOCK):
        rows = pl.ds(start, BLOCK)
        keys = pl.ds(0, key_limit(start, seq_len))
        scores = masked_scores(q_ref[rows, :], k_ref[keys, :], col_ref[rows, :], row_ref[:, keys])
        lane = lax.broadcasted_iota(jnp.int32, (BLOCK, log_ref.shape[1]), 1)
        log_total = jnp.sum(jnp.where(lane == head, log_ref[rows, :], 0.0), axis=1, keepdims=True)
        weights = jnp.exp(scores - log_total)
        grad_weights = lax.dot_general(
            g_ref[rows, :],
            v_ref[keys, :],
            (((1,), (1,)), ((), ())),
            preferred_element_type=jnp.float32,
        )
        grad_scores = (
            weights * (grad_weights - jnp.sum(weights * grad_weights, axis=-1, keepdims=True))
        ).astype(jnp.bfloat16)
        dq_acc[rows, :] = (
            jnp.dot(grad_scores, k_ref[keys, :], preferred_element_type=jnp.float32) * scale
        )
        dk_acc[keys, :] = dk_acc[keys, :] + down(grad_scores, q_ref[rows, :]) * scale
        dv_acc[keys, :] = dv_acc[keys, :] + down(weights.astype(jnp.bfloat16), g_ref[rows, :])
    gv_out[...] = dv_acc[...].astype(jnp.bfloat16)
    cosine, sine = cos_ref[...], sin_ref[...]

    @pl.when(head == 0)
    def _():
        dot_out[...] = jnp.zeros_like(dot_out)

    def turn_back(rows):
        return rows * cosine - pltpu.roll(rows, HEAD_DIM // 2, 1) * sine

    lane = lax.broadcasted_iota(jnp.int32, dot_out.shape, 1)
    for which, acc, proj, gain, out, gain_out in (
        (0, dq_acc, qp_ref, qg_ref, gq_out, qgain_out),
        (1, dk_acc, kp_ref, kg_ref, gk_out, kgain_out),
    ):
        grad = turn_back(acc[...])
        normed = proj[...] * inv_ref[:, which : which + 1]
        gain_out[...] = jnp.sum(grad * normed, axis=0, keepdims=True)
        scaled = grad * gain[...]
        out[...] = scaled
        dot_out[...] = dot_out[...] + jnp.where(
            lane == which, jnp.sum(scaled * normed, axis=1, keepdims=True), 0.0
        )


def attend_back(
    q_rot, k_rot, value_low, grad_mixed, log_totals, projected, inverses, q_gain_row, k_gain_row,
    tables, ids_col, ids_row,
):
    seq_len, cols = q_rot.shape
    heads = cols // HEAD_DIM
    whole = pl.BlockSpec(memory_space=pltpu.VMEM)
    gain = pl.BlockSpec((1, HEAD_DIM), lambda h: (0, h))
    column = pl.BlockSpec((seq_len, HEAD_DIM), lambda h: (0, h))
    wide = jax.ShapeDtypeStruct((seq_len, cols), jnp.float32)
    gain_shape = jax.ShapeDtypeStruct((1, cols), jnp.float32)
    return pl.pallas_call(
        attend_back_kernel,
        grid=(heads,),
        out_shape=(
            wide,
            wide,
            jax.ShapeDtypeStruct((seq_len, cols), jnp.bfloat16),
            jax.ShapeDtypeStruct((seq_len, 2), jnp.float32),
            gain_shape,
            gain_shape,
        ),
        in_specs=[
            column,
            column,
            column,
            column,
            whole,
            column,
            pl.BlockSpec((seq_len, HEAD_DIM), lambda h: (0, heads + h)),
            whole,
            gain,
            gain,
            whole,
            whole,
            whole,
            whole,
        ],
        out_specs=(
            column,
            column,
            column,
            pl.BlockSpec((seq_len, 2), lambda h: (0, 0)),
            gain,
            gain,
        ),
        scratch_shapes=[pltpu.VMEM((seq_len, HEAD_DIM), jnp.float32)] * 3,
        compiler_params=pltpu.CompilerParams(vmem_limit_bytes=48 * 1024 * 1024),
        cost_estimate=pl.CostEstimate(
            flops=60 * seq_len * seq_len * cols, bytes_accessed=projected.size * 4, transcendentals=0
        ),
    )(
        q_rot, k_rot, value_low, grad_mixed, log_totals, projected, projected, inverses,
        q_gain_row, k_gain_row, tables[0], tables[1], ids_col, ids_row,
    )


def kept_mask(route_rows):
    expert_ids = jnp.arange(EXPERTS, dtype=jnp.int32)
    first = (route_rows[:, 0:1] == expert_ids[None, :]).astype(jnp.int32)
    second = (route_rows[:, 1:2] == expert_ids[None, :]).astype(jnp.int32)
    both = first + second
    earlier = jnp.cumsum(both, axis=0) - both
    return jnp.where((both > 0) & (earlier < CAP), 1.0, 0.0).astype(jnp.float32)


def neighbour_barrier(me, count):
    barrier = pltpu.get_barrier_semaphore()

    @pl.when(me > 0)
    def _():
        pl.semaphore_signal(barrier, inc=1, device_id={"tensor": me - 1}, device_id_type=MESH)

    @pl.when(me < count - 1)
    def _():
        pl.semaphore_signal(barrier, inc=1, device_id={"tensor": me + 1}, device_id_type=MESH)

    pl.semaphore_wait(
        barrier, jnp.minimum(me, 1).astype(jnp.int32) + jnp.minimum(count - 1 - me, 1)
    )


def line_exchange(
    count, chunks, rows, width, part, extras, out_shapes, epilogue, gather, collective_id, prologue=None, waits=()
):
    reduce = part is not None
    n_extra = len(extras)
    n_out = len(out_shapes)
    last = count - 1
    back_lag = last if reduce else 0
    pass_lag = back_lag if reduce else chunks

    def kernel(*refs):
        refs = list(refs)
        part_ref = refs.pop(0) if reduce else None
        extra_refs = [refs.pop(0) for _ in range(n_extra)]
        del refs[: len(waits)]
        full_ref = refs.pop(0) if gather else None
        out_refs = [refs.pop(0) for _ in range(n_out)]
        if reduce:
            sum_right, sum_left, acc = refs.pop(0), refs.pop(0), refs.pop(0)
            rs_send_r, rs_recv_r, rs_send_l, rs_recv_l = [refs.pop(0) for _ in range(4)]
        if gather:
            ag_send_r, ag_recv_r, ag_send_l, ag_recv_l = [refs.pop(0) for _ in range(4)]
        me = lax.axis_index("tensor")
        right, left = jnp.minimum(me + 1, last), jnp.maximum(me - 1, 0)

        def remote(source, target, send_sem, recv_sem, device):
            return pltpu.make_async_remote_copy(
                src_ref=source,
                dst_ref=target,
                send_sem=send_sem,
                recv_sem=recv_sem,
                device_id={"tensor": device},
                device_id_type=MESH,
            )

        def rs_right(block, chunk, source=None):
            here = sum_right.at[block, chunk]
            return remote(
                here if source is None else source,
                here,
                rs_send_r.at[block, chunk],
                rs_recv_r.at[block, chunk],
                right,
            )

        def rs_left(block, chunk, source=None):
            here = sum_left.at[block, chunk]
            return remote(
                here if source is None else source,
                here,
                rs_send_l.at[block, chunk],
                rs_recv_l.at[block, chunk],
                left,
            )

        def ag_right(block, chunk):
            here = full_ref.at[block, chunk]
            return remote(
                here, here, ag_send_r.at[block, chunk], ag_recv_r.at[block, chunk], right
            )

        def ag_left(block, chunk):
            here = full_ref.at[block, chunk]
            return remote(here, here, ag_send_l.at[block, chunk], ag_recv_l.at[block, chunk], left)

        neighbour_barrier(me, count)
        if prologue is not None:
            prologue(extra_refs, out_refs)

        def send_right(chunk):
            for step in range(last):
                far = last - step

                @pl.when(jnp.logical_and(me < far, me == 0))
                def _():
                    rs_right(far, chunk, part_ref.at[far, chunk]).start()

                @pl.when(jnp.logical_and(me < far, me > 0))
                def _():
                    rs_right(far, chunk).wait_recv()
                    sum_right[far, chunk] = sum_right[far, chunk] + part_ref[far, chunk]
                    rs_right(far, chunk).start()

        def send_left(chunk):
            for step in range(last):

                @pl.when(jnp.logical_and(me > step, me == last))
                def _():
                    rs_left(step, chunk, part_ref.at[step, chunk]).start()

                @pl.when(jnp.logical_and(me > step, me < last))
                def _():
                    rs_left(step, chunk).wait_recv()
                    sum_left[step, chunk] = sum_left[step, chunk] + part_ref[step, chunk]
                    rs_left(step, chunk).start()

        def finish(chunk):
            if reduce:
                acc[...] = part_ref[me, chunk].astype(jnp.float32)

                @pl.when(me > 0)
                def _():
                    rs_right(me, chunk).wait_recv()
                    acc[...] = acc[...] + sum_right[me, chunk].astype(jnp.float32)

                @pl.when(me < last)
                def _():
                    rs_left(me, chunk).wait_recv()
                    acc[...] = acc[...] + sum_left[me, chunk].astype(jnp.float32)

                made = epilogue(chunk, acc[...], extra_refs, out_refs)
            else:
                made = epilogue(chunk, None, extra_refs, out_refs)
            if gather:
                full_ref[me, chunk] = made

                @pl.when(me < last)
                def _():
                    ag_right(me, chunk).start()

                @pl.when(me > 0)
                def _():
                    ag_left(me, chunk).start()

        def forward(chunk, step):
            @pl.when(me - step >= 0)
            def _():
                ag_right(jnp.maximum(me - step, 0), chunk).wait_recv()

            @pl.when(jnp.logical_and(me - step >= 0, me < last))
            def _():
                ag_right(jnp.maximum(me - step, 0), chunk).start()

            @pl.when(me + step <= last)
            def _():
                ag_left(jnp.minimum(me + step, last), chunk).wait_recv()

            @pl.when(jnp.logical_and(me + step <= last, me > 0))
            def _():
                ag_left(jnp.minimum(me + step, last), chunk).start()

        def at_chunk(chunk, work):
            @pl.when(jnp.logical_and(chunk >= 0, chunk < chunks))
            def _():
                work(jnp.clip(chunk, 0, chunks - 1))

        def tick(time, carry):
            if reduce:
                at_chunk(time - me, send_right)
                at_chunk(time - (last - me), send_left)
            at_chunk(time - back_lag, finish)
            if gather:
                for step in range(1, count):
                    at_chunk(time - pass_lag - step, lambda chunk: forward(chunk, step))
            return carry

        ticks = chunks + (pass_lag + last if gather else back_lag)
        lax.fori_loop(0, ticks, tick, 0)

        def drain(chunk, carry):
            for block in range(count):
                if reduce:

                    @pl.when(me < block)
                    def _():
                        rs_right(block, chunk).wait_send()

                    @pl.when(me > block)
                    def _():
                        rs_left(block, chunk).wait_send()

                if gather:

                    @pl.when(jnp.logical_and(block <= me, me < last))
                    def _():
                        ag_right(block, chunk).wait_send()

                    @pl.when(jnp.logical_and(block >= me, me > 0))
                    def _():
                        ag_left(block, chunk).wait_send()

            return carry

        lax.fori_loop(0, chunks, drain, 0)

    block = (count, chunks, rows, width)
    shapes = []
    if gather:
        shapes.append(jax.ShapeDtypeStruct(block, jnp.bfloat16))
    shapes.extend(out_shapes)
    scratch = []
    if reduce:
        scratch += [
            pltpu.VMEM(block, jnp.bfloat16),
            pltpu.VMEM(block, jnp.bfloat16),
            pltpu.VMEM((rows, width), jnp.float32),
        ]
        scratch += [pltpu.SemaphoreType.DMA((count, chunks))] * 4
    if gather:
        scratch += [pltpu.SemaphoreType.DMA((count, chunks))] * 4
    operands = ([part] if reduce else []) + list(extras)
    block_bytes = count * chunks * rows * width * 2
    results = pl.pallas_call(
        kernel,
        out_shape=tuple(shapes),
        in_specs=[pl.BlockSpec(memory_space=pltpu.VMEM)] * len(operands)
        + [pl.BlockSpec(memory_space=pl.ANY)] * len(waits),
        out_specs=tuple([pl.BlockSpec(memory_space=pltpu.VMEM)] * len(shapes)),
        scratch_shapes=scratch,
        compiler_params=pltpu.CompilerParams(
            collective_id=collective_id, has_side_effects=True, vmem_limit_bytes=56 * 1024 * 1024
        ),
        cost_estimate=pl.CostEstimate(
            flops=0,
            bytes_accessed=block_bytes * (60 if reduce and gather else 45),
            transcendentals=0,
        ),
    )(*operands, *waits)
    return results


def small_sum(count, values, collective_id, axis="tensor"):
    def kernel(in_ref, out_ref, slots, send_sems, recv_sems):
        me = lax.axis_index(axis)
        barrier = pltpu.get_barrier_semaphore()
        for offset in range(1, count):
            peer = lax.rem(me + offset, count)
            pl.semaphore_signal(barrier, inc=1, device_id={axis: peer}, device_id_type=MESH)
        pl.semaphore_wait(barrier, count - 1)

        def send(offset):
            return pltpu.make_async_remote_copy(
                src_ref=in_ref,
                dst_ref=slots.at[offset - 1],
                send_sem=send_sems.at[offset - 1],
                recv_sem=recv_sems.at[offset - 1],
                device_id={axis: lax.rem(me + offset, count)},
                device_id_type=MESH,
            )

        for offset in range(1, count):
            send(offset).start()
        total = in_ref[...]
        for offset in range(1, count):
            send(offset).wait_recv()
            total = total + slots[offset - 1]
        out_ref[...] = total
        for offset in range(1, count):
            send(offset).wait_send()

    return pl.pallas_call(
        kernel,
        out_shape=jax.ShapeDtypeStruct(values.shape, jnp.float32),
        in_specs=[pl.BlockSpec(memory_space=pltpu.VMEM)],
        out_specs=pl.BlockSpec(memory_space=pltpu.VMEM),
        scratch_shapes=[
            pltpu.VMEM((count - 1,) + values.shape, jnp.float32),
            pltpu.SemaphoreType.DMA((count - 1,)),
            pltpu.SemaphoreType.DMA((count - 1,)),
        ],
        compiler_params=pltpu.CompilerParams(collective_id=collective_id, has_side_effects=True),
    )(values)


def start_gather(count, tokens):
    rows, width = tokens.shape
    step, chunks = CHUNK_ROWS, rows // CHUNK_ROWS

    def epilogue(chunk, total, extra_refs, out_refs):
        value = extra_refs[0][chunk].astype(jnp.float32)
        return rms_scale(value).astype(jnp.bfloat16)

    (full,) = line_exchange(
        count,
        chunks,
        step,
        width,
        None,
        [tokens.reshape(chunks, step, width)],
        [],
        epilogue,
        True,
        1,
    )
    return full.reshape(count * rows, width)


def middle_exchange(count, branch_part, tokens, gain_row, waits):
    rows, width = tokens.shape
    step, chunks = CHUNK_ROWS, rows // CHUNK_ROWS

    def epilogue(chunk, total, extra_refs, out_refs):
        value = extra_refs[0][chunk].astype(jnp.float32) + total
        out_refs[0][chunk] = value
        return (rms_scale(value) * extra_refs[1][...]).astype(jnp.bfloat16)

    full, middle = line_exchange(
        count,
        chunks,
        step,
        width,
        branch_part.reshape(count, chunks, step, width),
        [tokens.reshape(chunks, step, width), gain_row],
        [jax.ShapeDtypeStruct((chunks, step, width), jnp.float32)],
        epilogue,
        True,
        2,
        None,
        waits,
    )
    return full.reshape(count * rows, width), middle.reshape(rows, width)


def norm_back_rows(value, gain_row, grad_out):
    inverse = lax.rsqrt(jnp.mean(value * value, axis=-1, keepdims=True) + EPSILON)
    normed = value * inverse
    scaled = grad_out * gain_row
    grad_in = inverse * (scaled - normed * jnp.mean(scaled * normed, axis=-1, keepdims=True))
    return grad_in, jnp.sum(grad_out * normed, axis=0, keepdims=True)


def zero_gain(extra_refs, out_refs):
    out_refs[1][...] = jnp.zeros_like(out_refs[1])


def middle_back_exchange(count, grad_part, router_part, middle, cotangent, gain_row):
    rows, width = middle.shape
    step, chunks = CHUNK_ROWS, rows // CHUNK_ROWS

    def epilogue(chunk, total, extra_refs, out_refs):
        grad_out = total + extra_refs[0][chunk]
        grad_in, grad_gain = norm_back_rows(extra_refs[1][chunk], extra_refs[3][...], grad_out)
        out_refs[1][...] = out_refs[1][...] + grad_gain
        grad_middle = extra_refs[2][chunk].astype(jnp.float32) + grad_in
        out_refs[0][chunk] = grad_middle
        return grad_middle.astype(jnp.bfloat16)

    full, grad_middle, grad_gain = line_exchange(
        count,
        chunks,
        step,
        width,
        grad_part.reshape(count, chunks, step, width),
        [
            router_part.reshape(chunks, step, width),
            middle.reshape(chunks, step, width),
            cotangent.reshape(chunks, step, width),
            gain_row,
        ],
        [
            jax.ShapeDtypeStruct((chunks, step, width), jnp.float32),
            jax.ShapeDtypeStruct((1, width), jnp.float32),
        ],
        epilogue,
        True,
        3,
        zero_gain,
    )
    return full.reshape(count * rows, width), grad_middle.reshape(rows, width), grad_gain[0]


def end_exchange(count, grad_part, grad_middle, tokens, gain_row):
    rows, width = tokens.shape
    step, chunks = CHUNK_ROWS, rows // CHUNK_ROWS

    def epilogue(chunk, total, extra_refs, out_refs):
        value = extra_refs[1][chunk].astype(jnp.float32)
        grad_in, grad_gain = norm_back_rows(value, extra_refs[2][...], total)
        out_refs[1][...] = out_refs[1][...] + grad_gain
        out_refs[0][chunk] = extra_refs[0][chunk] + grad_in

    grad_source, grad_gain = line_exchange(
        count,
        chunks,
        step,
        width,
        grad_part.reshape(count, chunks, step, width),
        [
            grad_middle.reshape(chunks, step, width),
            tokens.reshape(chunks, step, width),
            gain_row,
        ],
        [
            jax.ShapeDtypeStruct((chunks, step, width), jnp.float32),
            jax.ShapeDtypeStruct((1, width), jnp.float32),
        ],
        epilogue,
        False,
        4,
        zero_gain,
    )
    return grad_source.reshape(rows, width), grad_gain[0]


def expert_kernel(x_ref, c_ref, gates_ref, wg_ref, wu_ref, wd_ref, hg_ref, dg_ref, du_ref, gd_ref):
    expert = pl.program_id(0)
    rows_in = x_ref[...]
    gate_part = jnp.dot(rows_in, wg_ref[...], preferred_element_type=jnp.float32)
    up_part = jnp.dot(rows_in, wu_ref[...], preferred_element_type=jnp.float32)
    back_hidden = jnp.dot(c_ref[...], wd_ref[...], preferred_element_type=jnp.float32)
    mine = lax.broadcasted_iota(jnp.int32, gates_ref.shape, 1) == expert
    gates = jnp.sum(jnp.where(mine, gates_ref[...], 0.0), axis=1, keepdims=True)
    sigmoid_gate = jax.nn.sigmoid(gate_part)
    silu_gate = gate_part * sigmoid_gate
    hidden = silu_gate * up_part
    gate_dot = jnp.sum(hidden * back_hidden, axis=1, keepdims=True)

    @pl.when(expert == 0)
    def _():
        gd_ref[...] = jnp.zeros_like(gd_ref)

    gd_ref[...] = gd_ref[...] + jnp.where(mine, gate_dot, 0.0)
    hg_ref[...] = (hidden * gates).astype(jnp.bfloat16)
    grad_hidden = back_hidden * gates
    dg_ref[...] = (
        grad_hidden * up_part * sigmoid_gate * (1.0 + gate_part * (1.0 - sigmoid_gate))
    ).astype(jnp.bfloat16)
    du_ref[...] = (grad_hidden * silu_gate).astype(jnp.bfloat16)


def expert_parts(rows_in, rows_grad, gates, weights, down, ff_here):
    seq_len, width = rows_in.shape
    hidden_cols = EXPERTS * ff_here
    whole = pl.BlockSpec(memory_space=pltpu.VMEM)
    part = jax.ShapeDtypeStruct((seq_len, hidden_cols), jnp.bfloat16)
    column = pl.BlockSpec((seq_len, ff_here), lambda e: (0, e))
    flops = 6 * seq_len * width * hidden_cols
    return pl.pallas_call(
        expert_kernel,
        grid=(EXPERTS,),
        out_shape=(part, part, part, jax.ShapeDtypeStruct((seq_len, EXPERTS), jnp.float32)),
        in_specs=[
            whole,
            whole,
            whole,
            pl.BlockSpec((width, ff_here), lambda e: (0, e)),
            pl.BlockSpec((width, ff_here), lambda e: (0, EXPERTS + e)),
            pl.BlockSpec((width, ff_here), lambda e: (0, e)),
        ],
        out_specs=(
            column,
            column,
            column,
            pl.BlockSpec((seq_len, EXPERTS), lambda e: (0, 0)),
        ),
        compiler_params=pltpu.CompilerParams(vmem_limit_bytes=56 * 1024 * 1024),
        cost_estimate=pl.CostEstimate(
            flops=flops, bytes_accessed=weights.size * 2, transcendentals=0
        ),
    )(rows_in, rows_grad, gates, weights, weights, down)


def product_kernel(hg_ref, dg_ref, du_ref, x_ref, c_ref, w_ref, dx_ref, dw_ref):
    cols = hg_ref.shape[1]

    def times_weight(left, which):
        right = w_ref[:, which * cols : (which + 1) * cols]
        return lax.dot_general(
            left, right, (((1,), (1,)), ((), ())), preferred_element_type=jnp.float32
        )

    def weight_grad(rows, grad):
        return lax.dot_general(
            rows, grad, (((0,), (0,)), ((), ())), preferred_element_type=jnp.float32
        ).astype(jnp.bfloat16)

    dx_ref[...] = (times_weight(dg_ref[...], 0) + times_weight(du_ref[...], 1)).astype(
        jnp.bfloat16
    )
    dw_ref[:, :cols] = weight_grad(x_ref[...], dg_ref[...])
    dw_ref[:, cols : 2 * cols] = weight_grad(x_ref[...], du_ref[...])
    dw_ref[:, 2 * cols :] = weight_grad(c_ref[...], hg_ref[...])


def expert_products(hg, dg, du, rows_in, rows_grad, weights):
    seq_len, width = rows_in.shape
    cols = hg.shape[1]
    tile = 256
    whole = pl.BlockSpec(memory_space=pltpu.VMEM)
    column = pl.BlockSpec((seq_len, tile), lambda i: (0, i))
    row = pl.BlockSpec((tile, 3 * cols), lambda i: (i, 0))
    pair = pl.BlockSpec((tile, 2 * cols), lambda i: (i, 0))
    flat = jax.ShapeDtypeStruct((seq_len, width), jnp.bfloat16)
    return pl.pallas_call(
        product_kernel,
        grid=(width // tile,),
        out_shape=(flat, jax.ShapeDtypeStruct((width, 3 * cols), jnp.bfloat16)),
        in_specs=[whole, whole, whole, column, column, pair],
        out_specs=(column, row),
        compiler_params=pltpu.CompilerParams(vmem_limit_bytes=56 * 1024 * 1024),
        cost_estimate=pl.CostEstimate(
            flops=10 * seq_len * width * cols, bytes_accessed=weights.size * 4, transcendentals=0
        ),
    )(hg, dg, du, rows_in, rows_grad, weights)


def output_kernel(hg_ref, w_ref, out_ref):
    out_ref[...] = lax.dot_general(
        hg_ref[...], w_ref[...], (((1,), (1,)), ((), ())), preferred_element_type=jnp.float32
    ).astype(jnp.bfloat16)


def expert_output(hg, weights):
    seq_len, cols = hg.shape
    width = weights.shape[0]
    tile = 256
    return pl.pallas_call(
        output_kernel,
        grid=(width // tile,),
        out_shape=jax.ShapeDtypeStruct((seq_len, width), jnp.bfloat16),
        in_specs=[
            pl.BlockSpec(memory_space=pltpu.VMEM),
            pl.BlockSpec((tile, cols), lambda i: (i, 0)),
        ],
        out_specs=pl.BlockSpec((seq_len, tile), lambda i: (0, i)),
        compiler_params=pltpu.CompilerParams(vmem_limit_bytes=40 * 1024 * 1024),
        cost_estimate=pl.CostEstimate(
            flops=2 * seq_len * width * cols, bytes_accessed=width * cols * 2, transcendentals=0
        ),
    )(hg, weights)


def split_kernel(gate_ref, up_ref, down_ref, gate_out, up_out, down_out):
    gate_out[0] = gate_ref[...].astype(jnp.float32)
    up_out[0] = up_ref[...].astype(jnp.float32)
    down_out[0] = down_ref[...].astype(jnp.float32).T


def split_experts(sums, ff_here):
    width = sums.shape[0]

    def part(which):
        return pl.BlockSpec((width, ff_here), lambda e: (0, which * EXPERTS + e))

    wide = jax.ShapeDtypeStruct((EXPERTS, width, ff_here), jnp.float32)
    tall = jax.ShapeDtypeStruct((EXPERTS, ff_here, width), jnp.float32)
    wide_spec = pl.BlockSpec((1, width, ff_here), lambda e: (e, 0, 0))
    tall_spec = pl.BlockSpec((1, ff_here, width), lambda e: (e, 0, 0))
    return pl.pallas_call(
        split_kernel,
        grid=(EXPERTS,),
        out_shape=(wide, wide, tall),
        in_specs=[part(0), part(1), part(2)],
        out_specs=(wide_spec, wide_spec, tall_spec),
    )(sums, sums, sums)


def scatter_sum(dp_count, count, values, collective_id):
    total_count = dp_count * count

    def kernel(in_ref, out_ref, slots, send_sems, recv_sems):
        me = lax.axis_index("dp") * count + lax.axis_index("tensor")

        def peer(offset):
            other = lax.rem(me + offset, total_count)
            return other, {"dp": other // count, "tensor": lax.rem(other, count)}

        barrier = pltpu.get_barrier_semaphore()

        def greet(offset, carry):
            pl.semaphore_signal(
                barrier, inc=1, device_id=peer(offset)[1], device_id_type=MESH
            )
            return carry

        lax.fori_loop(1, total_count, greet, 0)
        pl.semaphore_wait(barrier, total_count - 1)

        def send(offset):
            other, device = peer(offset)
            return pltpu.make_async_remote_copy(
                src_ref=in_ref.at[other],
                dst_ref=slots.at[offset - 1],
                send_sem=send_sems.at[offset - 1],
                recv_sem=recv_sems.at[offset - 1],
                device_id=device,
                device_id_type=MESH,
            )

        def start(offset, carry):
            send(offset).start()
            return carry

        lax.fori_loop(1, total_count, start, 0)

        def collect(offset, total):
            send(offset).wait_recv()
            return total + slots[offset - 1]

        out_ref[...] = lax.fori_loop(1, total_count, collect, in_ref[me])

        def finish(offset, carry):
            send(offset).wait_send()
            return carry

        lax.fori_loop(1, total_count, finish, 0)

    block = values.shape[1:]
    return pl.pallas_call(
        kernel,
        out_shape=jax.ShapeDtypeStruct(block, jnp.float32),
        in_specs=[pl.BlockSpec(memory_space=pltpu.VMEM)],
        out_specs=pl.BlockSpec(memory_space=pltpu.VMEM),
        scratch_shapes=[
            pltpu.VMEM((total_count - 1,) + block, jnp.float32),
            pltpu.SemaphoreType.DMA((total_count - 1,)),
            pltpu.SemaphoreType.DMA((total_count - 1,)),
        ],
        compiler_params=pltpu.CompilerParams(collective_id=collective_id, has_side_effects=True),
    )(values)


def permute_step(pair, count, step):
    if step == count - 1 and count > 3:
        me = lax.axis_index("tensor")
        block = jnp.where(me == count - 2, pair[0], pair[1])
        block = lax.ppermute(block, "tensor", [(count - 2, count - 1), (1, 0)])
        return block, block
    return (
        lax.ppermute(pair[0], "tensor", [(i, i + 1) for i in range(step - 1, count - 1)]),
        lax.ppermute(pair[1], "tensor", [(i, i - 1) for i in range(1, count - step + 1)]),
    )


def tie(values, *waits):
    def kernel(*refs):
        del refs

    place = pl.BlockSpec(memory_space=pl.ANY)
    return pl.pallas_call(
        kernel,
        out_shape=tuple(jax.ShapeDtypeStruct(value.shape, value.dtype) for value in values),
        in_specs=[place] * (len(values) + len(waits)),
        out_specs=tuple([place] * len(values)),
        input_output_aliases={k: k for k in range(len(values))},
    )(*values, *waits)


def place_blocks(pairs, count):
    me = lax.axis_index("tensor")
    rows, width = pairs[0][0].shape
    full = jnp.zeros((count * rows, width), pairs[0][0].dtype)
    for step in range(count):
        piece = pairs[0][0]
        if step > 0:
            piece = jnp.where(me >= step, pairs[step][0], pairs[count - step][1])
        start = lax.rem(me - step + count, count) * rows
        full = lax.dynamic_update_slice_in_dim(full, piece, start, 0)
    return full


def after(value, *others):
    product = 0.0
    for other in others:
        corner = jnp.clip(other[0, 0].astype(jnp.float32), -1.0, 1.0)
        product = corner if other is others[0] else product * corner
    zero = product * 0.0
    return value + zero.astype(value.dtype)


def local(
    tokens,
    cotangent,
    routes,
    block_ids,
    attn_gain,
    q_gain,
    k_gain,
    w_query,
    w_key,
    w_value,
    w_out,
    ffn_gain,
    w_router,
    w_gate,
    w_up,
    w_down,
):
    shard_width = w_query.shape[0]
    head_cols = w_query.shape[1]
    ff_here = w_gate.shape[2]
    hidden_cols = EXPERTS * ff_here
    small_cols = jnp.concatenate(
        [attn_gain[:, None], q_gain[:, None], k_gain[:, None], ffn_gain[:, None], w_router], axis=1
    )
    small_cols = jnp.pad(small_cols, ((0, 0), (0, 128 - small_cols.shape[1])))
    w_heads = lax.all_gather(
        jnp.concatenate([w_query, w_key, w_value, w_out.T, small_cols], axis=1), "dp", axis=0, tiled=True
    )
    w_qkv = w_heads[:, : 3 * head_cols]
    w_o_t = w_heads[:, 3 * head_cols : 4 * head_cols]
    small = w_heads[:, 4 * head_cols : 4 * head_cols + 4 + EXPERTS]
    full_down = lax.all_gather(
        w_down.transpose(2, 0, 1).reshape(shard_width, hidden_cols), "dp", axis=0, tiled=True
    )
    expert_local = jnp.concatenate(
        [
            w_gate.transpose(1, 0, 2).reshape(shard_width, hidden_cols),
            w_up.transpose(1, 0, 2).reshape(shard_width, hidden_cols),
        ],
        axis=1,
    )
    full_router = small[:, 4:]
    model_width = tokens.shape[1]
    local_rows = tokens.shape[0]
    tensor_rank = lax.axis_index("tensor")
    col_start = tensor_rank * head_cols
    gains = small[:, :4].astype(jnp.float32).T
    attn_scale = gains[0]
    query_scale = lax.dynamic_slice_in_dim(gains[1], col_start, head_cols)
    key_scale = lax.dynamic_slice_in_dim(gains[2], col_start, head_cols)
    ffn_scale = gains[3]
    count = lax.axis_size("tensor")
    unit_rows = start_gather(count, tokens)
    normed = (unit_rows.astype(jnp.float32) * attn_scale[None, :]).astype(jnp.bfloat16)
    pairs = [(cotangent, cotangent)]
    first = after(cotangent, unit_rows)
    pairs.append(permute_step((first, first), count, 1))
    seq_len = normed.shape[0]
    ids_row, ids_col = block_ids, block_ids.T
    tables = rope_constants(seq_len)
    projected = jnp.dot(normed, w_qkv, preferred_element_type=jnp.float32)
    query_proj = projected[:, :head_cols]
    key_proj = projected[:, head_cols : 2 * head_cols]
    squares = jnp.stack(
        [jnp.sum(query_proj * query_proj, axis=1), jnp.sum(key_proj * key_proj, axis=1)]
    )
    squares = small_sum(count, squares, 5)
    full_gate_up = lax.all_gather(
        expert_local, "dp", axis=0, tiled=True
    )
    pairs[1] = tie(pairs[1], squares)
    pairs.append(permute_step(pairs[1], count, 2))
    inverses = lax.rsqrt(squares / model_width + EPSILON).T
    query_row, key_row = query_scale[None, :], key_scale[None, :]
    q_rot, k_rot, value_low, mixed_low, log_totals = attend(
        projected, inverses, query_row, key_row, tables, ids_col, ids_row
    )
    for step in range(3, count):
        if step == 3:
            pairs[-1] = tie(pairs[-1], log_totals)
        pairs.append(permute_step(pairs[-1], count, step))
    branch_part = jnp.einsum(
        "sf,df->sd", mixed_low, w_o_t, preferred_element_type=jnp.float32
    ).astype(jnp.bfloat16)
    normed_two, middle = middle_exchange(
        count, branch_part, tokens, ffn_scale[None, :], ()
    )
    grad_rows = place_blocks(pairs, count)
    logits = jnp.dot(normed_two, full_router, preferred_element_type=jnp.float32)
    router_probs = jax.nn.softmax(logits, axis=-1)
    kept = kept_mask(routes)
    gate_values = router_probs * kept
    hidden_gated, grad_gate_part, grad_up_part, gate_dot = expert_parts(
        normed_two, grad_rows, gate_values, full_gate_up, full_down, ff_here
    )
    combined = expert_output(hidden_gated, full_down)
    grad_two_part, grad_experts_w = expert_products(
        hidden_gated,
        grad_gate_part,
        grad_up_part,
        normed_two,
        grad_rows,
        full_gate_up,
    )
    ffn_branch = lax.psum_scatter(
        combined, "tensor", scatter_dimension=0, tiled=True
    ).astype(jnp.float32)
    output = (middle + ffn_branch).astype(jnp.bfloat16)
    grad_probs = small_sum(count, (gate_dot * kept).T, 6).T
    grad_logits = router_probs * (
        grad_probs - jnp.sum(router_probs * grad_probs, axis=1, keepdims=True)
    )
    logits_low = grad_logits.astype(jnp.bfloat16)
    grad_router = jnp.einsum(
        "sd,se->de", normed_two, logits_low, preferred_element_type=jnp.float32
    )
    own_logits = lax.dynamic_slice_in_dim(logits_low, tensor_rank * local_rows, local_rows)
    sum_experts = lax.psum_scatter(grad_experts_w, "dp", scatter_dimension=0, tiled=True)
    router_part = jnp.einsum(
        "se,de->sd", own_logits, full_router, preferred_element_type=jnp.float32
    )
    grad_attn_rows, grad_middle, grad_ffn_gain = middle_back_exchange(
        count, grad_two_part, router_part, middle, cotangent, ffn_scale[None, :]
    )
    grad_out_w = jnp.einsum(
        "sf,sd->df", mixed_low, grad_attn_rows, preferred_element_type=jnp.float32
    ).astype(jnp.bfloat16)
    grad_mixed = jnp.dot(grad_attn_rows, w_o_t, preferred_element_type=jnp.float32).astype(
        jnp.bfloat16
    )
    query_scaled, key_scaled, grad_value_low, dots, grad_query_gain, grad_key_gain = attend_back(
        q_rot,
        k_rot,
        value_low,
        grad_mixed,
        after(log_totals, ffn_branch),
        projected,
        inverses,
        query_row,
        key_row,
        tables,
        ids_col,
        ids_row,
    )
    dots = small_sum(count, after(dots.T, sum_experts), 7).T / model_width
    query_inv, key_inv = inverses[:, 0:1], inverses[:, 1:2]
    grad_query_proj = (
        query_inv * (query_scaled - query_proj * query_inv * dots[:, 0:1])
    ).astype(jnp.bfloat16)
    grad_key_proj = (key_inv * (key_scaled - key_proj * key_inv * dots[:, 1:2])).astype(
        jnp.bfloat16
    )
    grad_qkv = jnp.concatenate([grad_query_proj, grad_key_proj, grad_value_low], axis=1)
    grad_qkv_w = (
        jnp.einsum("sd,sf->df", unit_rows, grad_qkv, preferred_element_type=jnp.float32)
        * attn_scale[:, None]
    ).astype(jnp.bfloat16)
    grad_router_wide = jnp.pad(grad_router, ((0, 0), (0, 128 - EXPERTS))).astype(jnp.bfloat16)
    sum_heads = lax.psum_scatter(
        jnp.concatenate([grad_qkv_w, grad_out_w, grad_router_wide], axis=1),
        "dp",
        scatter_dimension=0,
        tiled=True,
    ).astype(jnp.float32)
    grad_normed_part = jnp.einsum(
        "sf,df->sd", grad_qkv, w_qkv, preferred_element_type=jnp.float32
    ).astype(jnp.bfloat16)
    grad_source, grad_attn_gain = end_exchange(
        count, grad_normed_part, grad_middle, tokens, attn_scale[None, :]
    )
    zero_cols = jnp.zeros((model_width,), jnp.float32)
    query_gain_full = lax.dynamic_update_slice_in_dim(zero_cols, grad_query_gain[0], col_start, 0)
    key_gain_full = lax.dynamic_update_slice_in_dim(zero_cols, grad_key_gain[0], col_start, 0)
    gain_stack = jnp.stack([grad_attn_gain, query_gain_full, key_gain_full, grad_ffn_gain])
    dp_count = lax.axis_size("dp")
    gain_width = model_width // (dp_count * count)
    gain_blocks = gain_stack.reshape(4, dp_count * count, gain_width).transpose(1, 0, 2)
    gain_blocks = jnp.pad(gain_blocks, ((0, 0), (0, 4), (0, 128 - gain_width)))
    gain_sums = scatter_sum(dp_count, count, gain_blocks, 8)[:4, :gain_width]
    sum_qkv = sum_heads[:, : 3 * head_cols]
    sum_out = sum_heads[:, 3 * head_cols : 4 * head_cols]
    sum_router = sum_heads[:, 4 * head_cols : 4 * head_cols + EXPERTS]
    grad_gate, grad_up, grad_down = split_experts(sum_experts, ff_here)
    return (
        output,
        grad_source,
        gain_sums[0],
        gain_sums[1],
        gain_sums[2],
        sum_qkv[:, :head_cols],
        sum_qkv[:, head_cols : 2 * head_cols],
        sum_qkv[:, 2 * head_cols :],
        sum_out.T.astype(jnp.float32),
        gain_sums[3],
        sum_router,
        grad_gate,
        grad_up,
        grad_down,
    )


def solution(mesh):
    placed = (
        P(("dp", "tensor"), None),
        P(("dp", "tensor"), None),
        P("dp", None),
        P("dp", None),
        P("dp"),
        P("dp"),
        P("dp"),
        P("dp", "tensor"),
        P("dp", "tensor"),
        P("dp", "tensor"),
        P("tensor", "dp"),
        P("dp"),
        P("dp", None),
        P(None, "dp", "tensor"),
        P(None, "dp", "tensor"),
        P(None, "tensor", "dp"),
    )
    return jax.shard_map(
        local,
        mesh=mesh,
        in_specs=placed,
        out_specs=(
            P(("dp", "tensor"), None),
            P(("dp", "tensor"), None),
            P(("dp", "tensor")),
            P(("dp", "tensor")),
            P(("dp", "tensor")),
            P("dp", "tensor"),
            P("dp", "tensor"),
            P("dp", "tensor"),
            P("tensor", "dp"),
            P(("dp", "tensor")),
            P("dp", None),
            P(None, "dp", "tensor"),
            P(None, "dp", "tensor"),
            P(None, "tensor", "dp"),
        ),
        check_vma=False,
    )
```

```python
import math

import jax
import jax.numpy as jnp
import numpy as np
from jax import lax
from jax.experimental import pallas as pl
from jax.experimental.pallas import tpu as pltpu
from jax.sharding import PartitionSpec as P

HEAD_DIM = 128
EXPERTS = 8
TOPK = 2
BLOCK = 256
CAP = 320


EPSILON = 1e-05
MASKED = -1e30
MESH = pl.DeviceIdType.MESH
CHUNK_ROWS = 8


def rms_scale(source):
    return source * lax.rsqrt(jnp.mean(source * source, axis=-1, keepdims=True) + EPSILON)


def rope_constants(seq_len):
    half_dim = HEAD_DIM // 2
    frequency = np.exp(-math.log(10000.0) * 2.0 * np.arange(half_dim) / HEAD_DIM)
    angles = np.arange(seq_len)[:, None] * frequency[None, :]
    cosine = np.concatenate([np.cos(angles)] * 2, axis=1).astype(np.float32)
    sine = np.concatenate([-np.sin(angles), np.sin(angles)], axis=1).astype(np.float32)
    return jnp.asarray(cosine), jnp.asarray(sine)


def masked_scores(q_rows, k_rows, ids_col, ids_row):
    scores = lax.dot_general(
        q_rows, k_rows, (((1,), (1,)), ((), ())), preferred_element_type=jnp.float32
    ) * (HEAD_DIM ** (-0.5))
    return jnp.where(ids_row <= ids_col, scores, MASKED)


def key_limit(start, seq_len):
    return min(seq_len, start + 2 * BLOCK)


def attend_kernel(
    q_ref, k_ref, v_ref, inv_ref, qg_ref, kg_ref, cos_ref, sin_ref, col_ref, row_ref,
    q_out, k_out, v_out, mixed_out, log_out,
):
    head = pl.program_id(0)
    seq_len = q_ref.shape[0]
    cosine, sine = cos_ref[...], sin_ref[...]

    def turn(rows):
        return (rows * cosine + pltpu.roll(rows, HEAD_DIM // 2, 1) * sine).astype(jnp.bfloat16)

    q_out[...] = turn(q_ref[...] * inv_ref[:, 0:1] * qg_ref[...])
    k_out[...] = turn(k_ref[...] * inv_ref[:, 1:2] * kg_ref[...])
    v_out[...] = v_ref[...].astype(jnp.bfloat16)

    @pl.when(head == 0)
    def _():
        log_out[...] = jnp.zeros_like(log_out)

    for start in range(0, seq_len, BLOCK):
        rows = pl.ds(start, BLOCK)
        keys = pl.ds(0, key_limit(start, seq_len))
        scores = masked_scores(q_out[rows, :], k_out[keys, :], col_ref[rows, :], row_ref[:, keys])
        top = jnp.max(scores, axis=-1, keepdims=True)
        powers = jnp.exp(scores - top)
        total = jnp.sum(powers, axis=-1, keepdims=True)
        weights = (powers * (1.0 / total)).astype(jnp.bfloat16)
        mixed_out[rows, :] = jnp.dot(
            weights, v_out[keys, :], preferred_element_type=jnp.float32
        ).astype(jnp.bfloat16)
        lane = lax.broadcasted_iota(jnp.int32, (BLOCK, log_out.shape[1]), 1)
        log_out[rows, :] = log_out[rows, :] + jnp.where(
            lane == head, top + jnp.log(total), 0.0
        )


def attend(projected, inverses, q_gain_row, k_gain_row, tables, ids_col, ids_row):
    seq_len = projected.shape[0]
    heads = projected.shape[1] // (3 * HEAD_DIM)
    cols = heads * HEAD_DIM
    whole = pl.BlockSpec(memory_space=pltpu.VMEM)
    gain = pl.BlockSpec((1, HEAD_DIM), lambda h: (0, h))
    column = pl.BlockSpec((seq_len, HEAD_DIM), lambda h: (0, h))
    flat = jax.ShapeDtypeStruct((seq_len, cols), jnp.bfloat16)
    return pl.pallas_call(
        attend_kernel,
        grid=(heads,),
        out_shape=(flat, flat, flat, flat, jax.ShapeDtypeStruct((seq_len, heads), jnp.float32)),
        in_specs=[
            column,
            pl.BlockSpec((seq_len, HEAD_DIM), lambda h: (0, heads + h)),
            pl.BlockSpec((seq_len, HEAD_DIM), lambda h: (0, 2 * heads + h)),
            whole,
            gain,
            gain,
            whole,
            whole,
            whole,
            whole,
        ],
        out_specs=(
            column,
            column,
            column,
            column,
            pl.BlockSpec((seq_len, heads), lambda h: (0, 0)),
        ),
        compiler_params=pltpu.CompilerParams(vmem_limit_bytes=48 * 1024 * 1024),
        cost_estimate=pl.CostEstimate(
            flops=20 * seq_len * seq_len * cols, bytes_accessed=projected.size * 4, transcendentals=0
        ),
    )(
        projected, projected, projected, inverses, q_gain_row, k_gain_row, tables[0], tables[1],
        ids_col, ids_row,
    )


def attend_back_kernel(
    q_ref, k_ref, v_ref, g_ref, log_ref, qp_ref, kp_ref, inv_ref, qg_ref, kg_ref, cos_ref, sin_ref,
    col_ref, row_ref, gq_out, gk_out, gv_out, dot_out, qgain_out, kgain_out, dq_acc, dk_acc, dv_acc,
):
    head = pl.program_id(0)
    seq_len = q_ref.shape[0]
    scale = HEAD_DIM ** (-0.5)
    dk_acc[...] = jnp.zeros_like(dk_acc)
    dv_acc[...] = jnp.zeros_like(dv_acc)

    def down(left, right):
        return lax.dot_general(
            left, right, (((0,), (0,)), ((), ())), preferred_element_type=jnp.float32
        )

    for start in range(0, seq_len, BLOCK):
        rows = pl.ds(start, BLOCK)
        keys = pl.ds(0, key_limit(start, seq_len))
        scores = masked_scores(q_ref[rows, :], k_ref[keys, :], col_ref[rows, :], row_ref[:, keys])
        lane = lax.broadcasted_iota(jnp.int32, (BLOCK, log_ref.shape[1]), 1)
        log_total = jnp.sum(jnp.where(lane == head, log_ref[rows, :], 0.0), axis=1, keepdims=True)
        weights = jnp.exp(scores - log_total)
        grad_weights = lax.dot_general(
            g_ref[rows, :],
            v_ref[keys, :],
            (((1,), (1,)), ((), ())),
            preferred_element_type=jnp.float32,
        )
        grad_scores = (
            weights * (grad_weights - jnp.sum(weights * grad_weights, axis=-1, keepdims=True))
        ).astype(jnp.bfloat16)
        dq_acc[rows, :] = (
            jnp.dot(grad_scores, k_ref[keys, :], preferred_element_type=jnp.float32) * scale
        )
        dk_acc[keys, :] = dk_acc[keys, :] + down(grad_scores, q_ref[rows, :]) * scale
        dv_acc[keys, :] = dv_acc[keys, :] + down(weights.astype(jnp.bfloat16), g_ref[rows, :])
    gv_out[...] = dv_acc[...].astype(jnp.bfloat16)
    cosine, sine = cos_ref[...], sin_ref[...]

    @pl.when(head == 0)
    def _():
        dot_out[...] = jnp.zeros_like(dot_out)

    def turn_back(rows):
        return rows * cosine - pltpu.roll(rows, HEAD_DIM // 2, 1) * sine

    lane = lax.broadcasted_iota(jnp.int32, dot_out.shape, 1)
    for which, acc, proj, gain, out, gain_out in (
        (0, dq_acc, qp_ref, qg_ref, gq_out, qgain_out),
        (1, dk_acc, kp_ref, kg_ref, gk_out, kgain_out),
    ):
        grad = turn_back(acc[...])
        normed = proj[...] * inv_ref[:, which : which + 1]
        gain_out[...] = jnp.sum(grad * normed, axis=0, keepdims=True)
        scaled = grad * gain[...]
        out[...] = scaled
        dot_out[...] = dot_out[...] + jnp.where(
            lane == which, jnp.sum(scaled * normed, axis=1, keepdims=True), 0.0
        )


def attend_back(
    q_rot, k_rot, value_low, grad_mixed, log_totals, projected, inverses, q_gain_row, k_gain_row,
    tables, ids_col, ids_row,
):
    seq_len, cols = q_rot.shape
    heads = cols // HEAD_DIM
    whole = pl.BlockSpec(memory_space=pltpu.VMEM)
    gain = pl.BlockSpec((1, HEAD_DIM), lambda h: (0, h))
    column = pl.BlockSpec((seq_len, HEAD_DIM), lambda h: (0, h))
    wide = jax.ShapeDtypeStruct((seq_len, cols), jnp.float32)
    gain_shape = jax.ShapeDtypeStruct((1, cols), jnp.float32)
    return pl.pallas_call(
        attend_back_kernel,
        grid=(heads,),
        out_shape=(
            wide,
            wide,
            jax.ShapeDtypeStruct((seq_len, cols), jnp.bfloat16),
            jax.ShapeDtypeStruct((seq_len, 2), jnp.float32),
            gain_shape,
            gain_shape,
        ),
        in_specs=[
            column,
            column,
            column,
            column,
            whole,
            column,
            pl.BlockSpec((seq_len, HEAD_DIM), lambda h: (0, heads + h)),
            whole,
            gain,
            gain,
            whole,
            whole,
            whole,
            whole,
        ],
        out_specs=(
            column,
            column,
            column,
            pl.BlockSpec((seq_len, 2), lambda h: (0, 0)),
            gain,
            gain,
        ),
        scratch_shapes=[pltpu.VMEM((seq_len, HEAD_DIM), jnp.float32)] * 3,
        compiler_params=pltpu.CompilerParams(vmem_limit_bytes=48 * 1024 * 1024),
        cost_estimate=pl.CostEstimate(
            flops=60 * seq_len * seq_len * cols, bytes_accessed=projected.size * 4, transcendentals=0
        ),
    )(
        q_rot, k_rot, value_low, grad_mixed, log_totals, projected, projected, inverses,
        q_gain_row, k_gain_row, tables[0], tables[1], ids_col, ids_row,
    )


def kept_mask(route_rows):
    expert_ids = jnp.arange(EXPERTS, dtype=jnp.int32)
    first = (route_rows[:, 0:1] == expert_ids[None, :]).astype(jnp.int32)
    second = (route_rows[:, 1:2] == expert_ids[None, :]).astype(jnp.int32)
    both = first + second
    earlier = jnp.cumsum(both, axis=0) - both
    return jnp.where((both > 0) & (earlier < CAP), 1.0, 0.0).astype(jnp.float32)


def neighbour_barrier(me, count):
    barrier = pltpu.get_barrier_semaphore()

    @pl.when(me > 0)
    def _():
        pl.semaphore_signal(barrier, inc=1, device_id={"tensor": me - 1}, device_id_type=MESH)

    @pl.when(me < count - 1)
    def _():
        pl.semaphore_signal(barrier, inc=1, device_id={"tensor": me + 1}, device_id_type=MESH)

    pl.semaphore_wait(
        barrier, jnp.minimum(me, 1).astype(jnp.int32) + jnp.minimum(count - 1 - me, 1)
    )


def line_exchange(
    count, chunks, rows, width, part, extras, out_shapes, epilogue, gather, collective_id, prologue=None, waits=()
):
    reduce = part is not None
    n_extra = len(extras)
    n_out = len(out_shapes)
    last = count - 1
    back_lag = last if reduce else 0
    pass_lag = back_lag if reduce else chunks

    def kernel(*refs):
        refs = list(refs)
        part_ref = refs.pop(0) if reduce else None
        extra_refs = [refs.pop(0) for _ in range(n_extra)]
        del refs[: len(waits)]
        full_ref = refs.pop(0) if gather else None
        out_refs = [refs.pop(0) for _ in range(n_out)]
        if reduce:
            sum_right, sum_left, acc = refs.pop(0), refs.pop(0), refs.pop(0)
            rs_send_r, rs_recv_r, rs_send_l, rs_recv_l = [refs.pop(0) for _ in range(4)]
        if gather:
            ag_send_r, ag_recv_r, ag_send_l, ag_recv_l = [refs.pop(0) for _ in range(4)]
        me = lax.axis_index("tensor")
        right, left = jnp.minimum(me + 1, last), jnp.maximum(me - 1, 0)

        def remote(source, target, send_sem, recv_sem, device):
            return pltpu.make_async_remote_copy(
                src_ref=source,
                dst_ref=target,
                send_sem=send_sem,
                recv_sem=recv_sem,
                device_id={"tensor": device},
                device_id_type=MESH,
            )

        def rs_right(block, chunk, source=None):
            here = sum_right.at[block, chunk]
            return remote(
                here if source is None else source,
                here,
                rs_send_r.at[block, chunk],
                rs_recv_r.at[block, chunk],
                right,
            )

        def rs_left(block, chunk, source=None):
            here = sum_left.at[block, chunk]
            return remote(
                here if source is None else source,
                here,
                rs_send_l.at[block, chunk],
                rs_recv_l.at[block, chunk],
                left,
            )

        def ag_right(block, chunk):
            here = full_ref.at[block, chunk]
            return remote(
                here, here, ag_send_r.at[block, chunk], ag_recv_r.at[block, chunk], right
            )

        def ag_left(block, chunk):
            here = full_ref.at[block, chunk]
            return remote(here, here, ag_send_l.at[block, chunk], ag_recv_l.at[block, chunk], left)

        neighbour_barrier(me, count)
        if prologue is not None:
            prologue(extra_refs, out_refs)

        def send_right(chunk):
            for step in range(last):
                far = last - step

                @pl.when(jnp.logical_and(me < far, me == 0))
                def _():
                    rs_right(far, chunk, part_ref.at[far, chunk]).start()

                @pl.when(jnp.logical_and(me < far, me > 0))
                def _():
                    rs_right(far, chunk).wait_recv()
                    sum_right[far, chunk] = sum_right[far, chunk] + part_ref[far, chunk]
                    rs_right(far, chunk).start()

        def send_left(chunk):
            for step in range(last):

                @pl.when(jnp.logical_and(me > step, me == last))
                def _():
                    rs_left(step, chunk, part_ref.at[step, chunk]).start()

                @pl.when(jnp.logical_and(me > step, me < last))
                def _():
                    rs_left(step, chunk).wait_recv()
                    sum_left[step, chunk] = sum_left[step, chunk] + part_ref[step, chunk]
                    rs_left(step, chunk).start()

        def finish(chunk):
            if reduce:
                acc[...] = part_ref[me, chunk].astype(jnp.float32)

                @pl.when(me > 0)
                def _():
                    rs_right(me, chunk).wait_recv()
                    acc[...] = acc[...] + sum_right[me, chunk].astype(jnp.float32)

                @pl.when(me < last)
                def _():
                    rs_left(me, chunk).wait_recv()
                    acc[...] = acc[...] + sum_left[me, chunk].astype(jnp.float32)

                made = epilogue(chunk, acc[...], extra_refs, out_refs)
            else:
                made = epilogue(chunk, None, extra_refs, out_refs)
            if gather:
                full_ref[me, chunk] = made

                @pl.when(me < last)
                def _():
                    ag_right(me, chunk).start()

                @pl.when(me > 0)
                def _():
                    ag_left(me, chunk).start()

        def forward(chunk, step):
            @pl.when(me - step >= 0)
            def _():
                ag_right(jnp.maximum(me - step, 0), chunk).wait_recv()

            @pl.when(jnp.logical_and(me - step >= 0, me < last))
            def _():
                ag_right(jnp.maximum(me - step, 0), chunk).start()

            @pl.when(me + step <= last)
            def _():
                ag_left(jnp.minimum(me + step, last), chunk).wait_recv()

            @pl.when(jnp.logical_and(me + step <= last, me > 0))
            def _():
                ag_left(jnp.minimum(me + step, last), chunk).start()

        def at_chunk(chunk, work):
            @pl.when(jnp.logical_and(chunk >= 0, chunk < chunks))
            def _():
                work(jnp.clip(chunk, 0, chunks - 1))

        def tick(time, carry):
            if reduce:
                at_chunk(time - me, send_right)
                at_chunk(time - (last - me), send_left)
            at_chunk(time - back_lag, finish)
            if gather:
                for step in range(1, count):
                    at_chunk(time - pass_lag - step, lambda chunk: forward(chunk, step))
            return carry

        ticks = chunks + (pass_lag + last if gather else back_lag)
        lax.fori_loop(0, ticks, tick, 0)

        def drain(chunk, carry):
            for block in range(count):
                if reduce:

                    @pl.when(me < block)
                    def _():
                        rs_right(block, chunk).wait_send()

                    @pl.when(me > block)
                    def _():
                        rs_left(block, chunk).wait_send()

                if gather:

                    @pl.when(jnp.logical_and(block <= me, me < last))
                    def _():
                        ag_right(block, chunk).wait_send()

                    @pl.when(jnp.logical_and(block >= me, me > 0))
                    def _():
                        ag_left(block, chunk).wait_send()

            return carry

        lax.fori_loop(0, chunks, drain, 0)

    block = (count, chunks, rows, width)
    shapes = []
    if gather:
        shapes.append(jax.ShapeDtypeStruct(block, jnp.bfloat16))
    shapes.extend(out_shapes)
    scratch = []
    if reduce:
        scratch += [
            pltpu.VMEM(block, jnp.bfloat16),
            pltpu.VMEM(block, jnp.bfloat16),
            pltpu.VMEM((rows, width), jnp.float32),
        ]
        scratch += [pltpu.SemaphoreType.DMA((count, chunks))] * 4
    if gather:
        scratch += [pltpu.SemaphoreType.DMA((count, chunks))] * 4
    operands = ([part] if reduce else []) + list(extras)
    block_bytes = count * chunks * rows * width * 2
    results = pl.pallas_call(
        kernel,
        out_shape=tuple(shapes),
        in_specs=[pl.BlockSpec(memory_space=pltpu.VMEM)] * len(operands)
        + [pl.BlockSpec(memory_space=pl.ANY)] * len(waits),
        out_specs=tuple([pl.BlockSpec(memory_space=pltpu.VMEM)] * len(shapes)),
        scratch_shapes=scratch,
        compiler_params=pltpu.CompilerParams(
            collective_id=collective_id, has_side_effects=True, vmem_limit_bytes=56 * 1024 * 1024
        ),
        cost_estimate=pl.CostEstimate(
            flops=0,
            bytes_accessed=block_bytes * (60 if reduce and gather else 45),
            transcendentals=0,
        ),
    )(*operands, *waits)
    return results


def small_sum(count, values, collective_id, axis="tensor"):
    def kernel(in_ref, out_ref, slots, send_sems, recv_sems):
        me = lax.axis_index(axis)
        barrier = pltpu.get_barrier_semaphore()
        for offset in range(1, count):
            peer = lax.rem(me + offset, count)
            pl.semaphore_signal(barrier, inc=1, device_id={axis: peer}, device_id_type=MESH)
        pl.semaphore_wait(barrier, count - 1)

        def send(offset):
            return pltpu.make_async_remote_copy(
                src_ref=in_ref,
                dst_ref=slots.at[offset - 1],
                send_sem=send_sems.at[offset - 1],
                recv_sem=recv_sems.at[offset - 1],
                device_id={axis: lax.rem(me + offset, count)},
                device_id_type=MESH,
            )

        for offset in range(1, count):
            send(offset).start()
        total = in_ref[...]
        for offset in range(1, count):
            send(offset).wait_recv()
            total = total + slots[offset - 1]
        out_ref[...] = total
        for offset in range(1, count):
            send(offset).wait_send()

    return pl.pallas_call(
        kernel,
        out_shape=jax.ShapeDtypeStruct(values.shape, jnp.float32),
        in_specs=[pl.BlockSpec(memory_space=pltpu.VMEM)],
        out_specs=pl.BlockSpec(memory_space=pltpu.VMEM),
        scratch_shapes=[
            pltpu.VMEM((count - 1,) + values.shape, jnp.float32),
            pltpu.SemaphoreType.DMA((count - 1,)),
            pltpu.SemaphoreType.DMA((count - 1,)),
        ],
        compiler_params=pltpu.CompilerParams(collective_id=collective_id, has_side_effects=True),
    )(values)


def start_gather(count, tokens):
    rows, width = tokens.shape
    step, chunks = CHUNK_ROWS, rows // CHUNK_ROWS

    def epilogue(chunk, total, extra_refs, out_refs):
        value = extra_refs[0][chunk].astype(jnp.float32)
        return rms_scale(value).astype(jnp.bfloat16)

    (full,) = line_exchange(
        count,
        chunks,
        step,
        width,
        None,
        [tokens.reshape(chunks, step, width)],
        [],
        epilogue,
        True,
        1,
    )
    return full.reshape(count * rows, width)


def middle_exchange(count, branch_part, tokens, gain_row, waits):
    rows, width = tokens.shape
    step, chunks = CHUNK_ROWS, rows // CHUNK_ROWS

    def epilogue(chunk, total, extra_refs, out_refs):
        value = extra_refs[0][chunk].astype(jnp.float32) + total
        out_refs[0][chunk] = value
        return (rms_scale(value) * extra_refs[1][...]).astype(jnp.bfloat16)

    full, middle = line_exchange(
        count,
        chunks,
        step,
        width,
        branch_part.reshape(count, chunks, step, width),
        [tokens.reshape(chunks, step, width), gain_row],
        [jax.ShapeDtypeStruct((chunks, step, width), jnp.float32)],
        epilogue,
        True,
        2,
        None,
        waits,
    )
    return full.reshape(count * rows, width), middle.reshape(rows, width)


def norm_back_rows(value, gain_row, grad_out):
    inverse = lax.rsqrt(jnp.mean(value * value, axis=-1, keepdims=True) + EPSILON)
    normed = value * inverse
    scaled = grad_out * gain_row
    grad_in = inverse * (scaled - normed * jnp.mean(scaled * normed, axis=-1, keepdims=True))
    return grad_in, jnp.sum(grad_out * normed, axis=0, keepdims=True)


def zero_gain(extra_refs, out_refs):
    out_refs[1][...] = jnp.zeros_like(out_refs[1])


def middle_back_exchange(count, grad_part, router_part, middle, cotangent, gain_row):
    rows, width = middle.shape
    step, chunks = CHUNK_ROWS, rows // CHUNK_ROWS

    def epilogue(chunk, total, extra_refs, out_refs):
        grad_out = total + extra_refs[0][chunk]
        grad_in, grad_gain = norm_back_rows(extra_refs[1][chunk], extra_refs[3][...], grad_out)
        out_refs[1][...] = out_refs[1][...] + grad_gain
        grad_middle = extra_refs[2][chunk].astype(jnp.float32) + grad_in
        out_refs[0][chunk] = grad_middle
        return grad_middle.astype(jnp.bfloat16)

    full, grad_middle, grad_gain = line_exchange(
        count,
        chunks,
        step,
        width,
        grad_part.reshape(count, chunks, step, width),
        [
            router_part.reshape(chunks, step, width),
            middle.reshape(chunks, step, width),
            cotangent.reshape(chunks, step, width),
            gain_row,
        ],
        [
            jax.ShapeDtypeStruct((chunks, step, width), jnp.float32),
            jax.ShapeDtypeStruct((1, width), jnp.float32),
        ],
        epilogue,
        True,
        3,
        zero_gain,
    )
    return full.reshape(count * rows, width), grad_middle.reshape(rows, width), grad_gain[0]


def end_exchange(count, grad_part, grad_middle, tokens, gain_row, waits):
    rows, width = tokens.shape
    step, chunks = CHUNK_ROWS, rows // CHUNK_ROWS

    def epilogue(chunk, total, extra_refs, out_refs):
        value = extra_refs[1][chunk].astype(jnp.float32)
        grad_in, grad_gain = norm_back_rows(value, extra_refs[2][...], total)
        out_refs[1][...] = out_refs[1][...] + grad_gain
        out_refs[0][chunk] = extra_refs[0][chunk] + grad_in

    grad_source, grad_gain = line_exchange(
        count,
        chunks,
        step,
        width,
        grad_part.reshape(count, chunks, step, width),
        [
            grad_middle.reshape(chunks, step, width),
            tokens.reshape(chunks, step, width),
            gain_row,
        ],
        [
            jax.ShapeDtypeStruct((chunks, step, width), jnp.float32),
            jax.ShapeDtypeStruct((1, width), jnp.float32),
        ],
        epilogue,
        False,
        4,
        zero_gain,
        waits,
    )
    return grad_source.reshape(rows, width), grad_gain[0]


def expert_kernel(x_ref, c_ref, gates_ref, wg_ref, wu_ref, wd_ref, hg_ref, dg_ref, du_ref, gd_ref):
    expert = pl.program_id(0)
    rows_in = x_ref[...]
    gate_part = jnp.dot(rows_in, wg_ref[...], preferred_element_type=jnp.float32)
    up_part = jnp.dot(rows_in, wu_ref[...], preferred_element_type=jnp.float32)
    back_hidden = jnp.dot(c_ref[...], wd_ref[...], preferred_element_type=jnp.float32)
    mine = lax.broadcasted_iota(jnp.int32, gates_ref.shape, 1) == expert
    gates = jnp.sum(jnp.where(mine, gates_ref[...], 0.0), axis=1, keepdims=True)
    sigmoid_gate = jax.nn.sigmoid(gate_part)
    silu_gate = gate_part * sigmoid_gate
    hidden = silu_gate * up_part
    gate_dot = jnp.sum(hidden * back_hidden, axis=1, keepdims=True)

    @pl.when(expert == 0)
    def _():
        gd_ref[...] = jnp.zeros_like(gd_ref)

    gd_ref[...] = gd_ref[...] + jnp.where(mine, gate_dot, 0.0)
    hg_ref[...] = (hidden * gates).astype(jnp.bfloat16)
    grad_hidden = back_hidden * gates
    dg_ref[...] = (
        grad_hidden * up_part * sigmoid_gate * (1.0 + gate_part * (1.0 - sigmoid_gate))
    ).astype(jnp.bfloat16)
    du_ref[...] = (grad_hidden * silu_gate).astype(jnp.bfloat16)


def expert_parts(rows_in, rows_grad, gates, weights, down, ff_here):
    seq_len, width = rows_in.shape
    hidden_cols = EXPERTS * ff_here
    whole = pl.BlockSpec(memory_space=pltpu.VMEM)
    part = jax.ShapeDtypeStruct((seq_len, hidden_cols), jnp.bfloat16)
    column = pl.BlockSpec((seq_len, ff_here), lambda e: (0, e))
    flops = 6 * seq_len * width * hidden_cols
    return pl.pallas_call(
        expert_kernel,
        grid=(EXPERTS,),
        out_shape=(part, part, part, jax.ShapeDtypeStruct((seq_len, EXPERTS), jnp.float32)),
        in_specs=[
            whole,
            whole,
            whole,
            pl.BlockSpec((width, ff_here), lambda e: (0, e)),
            pl.BlockSpec((width, ff_here), lambda e: (0, EXPERTS + e)),
            pl.BlockSpec((width, ff_here), lambda e: (0, e)),
        ],
        out_specs=(
            column,
            column,
            column,
            pl.BlockSpec((seq_len, EXPERTS), lambda e: (0, 0)),
        ),
        compiler_params=pltpu.CompilerParams(vmem_limit_bytes=56 * 1024 * 1024),
        cost_estimate=pl.CostEstimate(
            flops=flops, bytes_accessed=weights.size * 2, transcendentals=0
        ),
    )(rows_in, rows_grad, gates, weights, weights, down)


def product_kernel(hg_ref, dg_ref, du_ref, x_ref, c_ref, w_ref, dx_ref, dw_ref):
    cols = hg_ref.shape[1]

    def times_weight(left, which):
        right = w_ref[:, which * cols : (which + 1) * cols]
        return lax.dot_general(
            left, right, (((1,), (1,)), ((), ())), preferred_element_type=jnp.float32
        )

    def weight_grad(rows, grad):
        return lax.dot_general(
            rows, grad, (((0,), (0,)), ((), ())), preferred_element_type=jnp.float32
        ).astype(jnp.bfloat16)

    dx_ref[...] = (times_weight(dg_ref[...], 0) + times_weight(du_ref[...], 1)).astype(
        jnp.bfloat16
    )
    dw_ref[:, :cols] = weight_grad(x_ref[...], dg_ref[...])
    dw_ref[:, cols : 2 * cols] = weight_grad(x_ref[...], du_ref[...])
    dw_ref[:, 2 * cols :] = weight_grad(c_ref[...], hg_ref[...])


def expert_products(hg, dg, du, rows_in, rows_grad, weights):
    seq_len, width = rows_in.shape
    cols = hg.shape[1]
    tile = 256
    whole = pl.BlockSpec(memory_space=pltpu.VMEM)
    column = pl.BlockSpec((seq_len, tile), lambda i: (0, i))
    row = pl.BlockSpec((tile, 3 * cols), lambda i: (i, 0))
    pair = pl.BlockSpec((tile, 2 * cols), lambda i: (i, 0))
    flat = jax.ShapeDtypeStruct((seq_len, width), jnp.bfloat16)
    return pl.pallas_call(
        product_kernel,
        grid=(width // tile,),
        out_shape=(flat, jax.ShapeDtypeStruct((width, 3 * cols), jnp.bfloat16)),
        in_specs=[whole, whole, whole, column, column, pair],
        out_specs=(column, row),
        compiler_params=pltpu.CompilerParams(vmem_limit_bytes=56 * 1024 * 1024),
        cost_estimate=pl.CostEstimate(
            flops=10 * seq_len * width * cols, bytes_accessed=weights.size * 4, transcendentals=0
        ),
    )(hg, dg, du, rows_in, rows_grad, weights)


def output_kernel(hg_ref, w_ref, out_ref):
    out_ref[...] = lax.dot_general(
        hg_ref[...], w_ref[...], (((1,), (1,)), ((), ())), preferred_element_type=jnp.float32
    ).astype(jnp.bfloat16)


def expert_output(hg, weights):
    seq_len, cols = hg.shape
    width = weights.shape[0]
    tile = 256
    return pl.pallas_call(
        output_kernel,
        grid=(width // tile,),
        out_shape=jax.ShapeDtypeStruct((seq_len, width), jnp.bfloat16),
        in_specs=[
            pl.BlockSpec(memory_space=pltpu.VMEM),
            pl.BlockSpec((tile, cols), lambda i: (i, 0)),
        ],
        out_specs=pl.BlockSpec((seq_len, tile), lambda i: (0, i)),
        compiler_params=pltpu.CompilerParams(vmem_limit_bytes=40 * 1024 * 1024),
        cost_estimate=pl.CostEstimate(
            flops=2 * seq_len * width * cols, bytes_accessed=width * cols * 2, transcendentals=0
        ),
    )(hg, weights)


def split_kernel(gate_ref, up_ref, down_ref, gate_out, up_out, down_out):
    gate_out[0] = gate_ref[...].astype(jnp.float32)
    up_out[0] = up_ref[...].astype(jnp.float32)
    down_out[0] = down_ref[...].astype(jnp.float32).T


def split_experts(sums, ff_here):
    width = sums.shape[0]

    def part(which):
        return pl.BlockSpec((width, ff_here), lambda e: (0, which * EXPERTS + e))

    wide = jax.ShapeDtypeStruct((EXPERTS, width, ff_here), jnp.float32)
    tall = jax.ShapeDtypeStruct((EXPERTS, ff_here, width), jnp.float32)
    wide_spec = pl.BlockSpec((1, width, ff_here), lambda e: (e, 0, 0))
    tall_spec = pl.BlockSpec((1, ff_here, width), lambda e: (e, 0, 0))
    return pl.pallas_call(
        split_kernel,
        grid=(EXPERTS,),
        out_shape=(wide, wide, tall),
        in_specs=[part(0), part(1), part(2)],
        out_specs=(wide_spec, wide_spec, tall_spec),
    )(sums, sums, sums)


def scatter_sum(dp_count, count, values, collective_id):
    total_count = dp_count * count

    def kernel(in_ref, out_ref, slots, send_sems, recv_sems):
        me = lax.axis_index("dp") * count + lax.axis_index("tensor")

        def peer(offset):
            other = lax.rem(me + offset, total_count)
            return other, {"dp": other // count, "tensor": lax.rem(other, count)}

        barrier = pltpu.get_barrier_semaphore()

        def greet(offset, carry):
            pl.semaphore_signal(
                barrier, inc=1, device_id=peer(offset)[1], device_id_type=MESH
            )
            return carry

        lax.fori_loop(1, total_count, greet, 0)
        pl.semaphore_wait(barrier, total_count - 1)

        def send(offset):
            other, device = peer(offset)
            return pltpu.make_async_remote_copy(
                src_ref=in_ref.at[other],
                dst_ref=slots.at[offset - 1],
                send_sem=send_sems.at[offset - 1],
                recv_sem=recv_sems.at[offset - 1],
                device_id=device,
                device_id_type=MESH,
            )

        def start(offset, carry):
            send(offset).start()
            return carry

        lax.fori_loop(1, total_count, start, 0)

        def collect(offset, total):
            send(offset).wait_recv()
            return total + slots[offset - 1]

        out_ref[...] = lax.fori_loop(1, total_count, collect, in_ref[me])

        def finish(offset, carry):
            send(offset).wait_send()
            return carry

        lax.fori_loop(1, total_count, finish, 0)

    block = values.shape[1:]
    return pl.pallas_call(
        kernel,
        out_shape=jax.ShapeDtypeStruct(block, jnp.float32),
        in_specs=[pl.BlockSpec(memory_space=pltpu.VMEM)],
        out_specs=pl.BlockSpec(memory_space=pltpu.VMEM),
        scratch_shapes=[
            pltpu.VMEM((total_count - 1,) + block, jnp.float32),
            pltpu.SemaphoreType.DMA((total_count - 1,)),
            pltpu.SemaphoreType.DMA((total_count - 1,)),
        ],
        compiler_params=pltpu.CompilerParams(collective_id=collective_id, has_side_effects=True),
    )(values)


def permute_step(pair, count, step):
    if step == count - 1 and count > 3:
        me = lax.axis_index("tensor")
        block = jnp.where(me == count - 2, pair[0], pair[1])
        block = lax.ppermute(block, "tensor", [(count - 2, count - 1), (1, 0)])
        return block, block
    return (
        lax.ppermute(pair[0], "tensor", [(i, i + 1) for i in range(step - 1, count - 1)]),
        lax.ppermute(pair[1], "tensor", [(i, i - 1) for i in range(1, count - step + 1)]),
    )


def tie(values, *waits):
    def kernel(*refs):
        del refs

    place = pl.BlockSpec(memory_space=pl.ANY)
    return pl.pallas_call(
        kernel,
        out_shape=tuple(jax.ShapeDtypeStruct(value.shape, value.dtype) for value in values),
        in_specs=[place] * (len(values) + len(waits)),
        out_specs=tuple([place] * len(values)),
        input_output_aliases={k: k for k in range(len(values))},
    )(*values, *waits)


def place_blocks(pairs, count):
    me = lax.axis_index("tensor")
    rows, width = pairs[0][0].shape
    full = jnp.zeros((count * rows, width), pairs[0][0].dtype)
    for step in range(count):
        piece = pairs[0][0]
        if step > 0:
            piece = jnp.where(me >= step, pairs[step][0], pairs[count - step][1])
        start = lax.rem(me - step + count, count) * rows
        full = lax.dynamic_update_slice_in_dim(full, piece, start, 0)
    return full


def after(value, *others):
    product = 0.0
    for other in others:
        corner = jnp.clip(other[0, 0].astype(jnp.float32), -1.0, 1.0)
        product = corner if other is others[0] else product * corner
    zero = product * 0.0
    return value + zero.astype(value.dtype)


def local(
    tokens,
    cotangent,
    routes,
    block_ids,
    attn_gain,
    q_gain,
    k_gain,
    w_query,
    w_key,
    w_value,
    w_out,
    ffn_gain,
    w_router,
    w_gate,
    w_up,
    w_down,
):
    shard_width = w_query.shape[0]
    head_cols = w_query.shape[1]
    ff_here = w_gate.shape[2]
    hidden_cols = EXPERTS * ff_here
    small_cols = jnp.concatenate(
        [attn_gain[:, None], q_gain[:, None], k_gain[:, None], ffn_gain[:, None], w_router], axis=1
    )
    small_cols = jnp.pad(small_cols, ((0, 0), (0, 128 - small_cols.shape[1])))
    w_heads = lax.all_gather(
        jnp.concatenate([w_query, w_key, w_value, w_out.T, small_cols], axis=1), "dp", axis=0, tiled=True
    )
    w_qkv = w_heads[:, : 3 * head_cols]
    w_o_t = w_heads[:, 3 * head_cols : 4 * head_cols]
    small = w_heads[:, 4 * head_cols : 4 * head_cols + 4 + EXPERTS]
    full_down = lax.all_gather(
        w_down.transpose(2, 0, 1).reshape(shard_width, hidden_cols), "dp", axis=0, tiled=True
    )
    expert_local = jnp.concatenate(
        [
            w_gate.transpose(1, 0, 2).reshape(shard_width, hidden_cols),
            w_up.transpose(1, 0, 2).reshape(shard_width, hidden_cols),
        ],
        axis=1,
    )
    full_router = small[:, 4:]
    model_width = tokens.shape[1]
    local_rows = tokens.shape[0]
    tensor_rank = lax.axis_index("tensor")
    col_start = tensor_rank * head_cols
    gains = small[:, :4].astype(jnp.float32).T
    attn_scale = gains[0]
    query_scale = lax.dynamic_slice_in_dim(gains[1], col_start, head_cols)
    key_scale = lax.dynamic_slice_in_dim(gains[2], col_start, head_cols)
    ffn_scale = gains[3]
    count = lax.axis_size("tensor")
    unit_rows = start_gather(count, tokens)
    normed = (unit_rows.astype(jnp.float32) * attn_scale[None, :]).astype(jnp.bfloat16)
    pairs = [(cotangent, cotangent)]
    first = after(cotangent, unit_rows)
    pairs.append(permute_step((first, first), count, 1))
    seq_len = normed.shape[0]
    ids_row, ids_col = block_ids, block_ids.T
    tables = rope_constants(seq_len)
    projected = jnp.dot(normed, w_qkv, preferred_element_type=jnp.float32)
    query_proj = projected[:, :head_cols]
    key_proj = projected[:, head_cols : 2 * head_cols]
    squares = jnp.stack(
        [jnp.sum(query_proj * query_proj, axis=1), jnp.sum(key_proj * key_proj, axis=1)]
    )
    squares = small_sum(count, squares, 5)
    full_gate_up = lax.all_gather(
        expert_local, "dp", axis=0, tiled=True
    )
    pairs[1] = tie(pairs[1], squares)
    pairs.append(permute_step(pairs[1], count, 2))
    inverses = lax.rsqrt(squares / model_width + EPSILON).T
    query_row, key_row = query_scale[None, :], key_scale[None, :]
    q_rot, k_rot, value_low, mixed_low, log_totals = attend(
        projected, inverses, query_row, key_row, tables, ids_col, ids_row
    )
    for step in range(3, count):
        if step == 3:
            pairs[-1] = tie(pairs[-1], log_totals)
        pairs.append(permute_step(pairs[-1], count, step))
    branch_part = jnp.einsum(
        "sf,df->sd", mixed_low, w_o_t, preferred_element_type=jnp.float32
    ).astype(jnp.bfloat16)
    normed_two, middle = middle_exchange(
        count, branch_part, tokens, ffn_scale[None, :], ()
    )
    grad_rows = place_blocks(pairs, count)
    logits = jnp.dot(normed_two, full_router, preferred_element_type=jnp.float32)
    router_probs = jax.nn.softmax(logits, axis=-1)
    kept = kept_mask(routes)
    gate_values = router_probs * kept
    hidden_gated, grad_gate_part, grad_up_part, gate_dot = expert_parts(
        normed_two, grad_rows, gate_values, full_gate_up, full_down, ff_here
    )
    combined = expert_output(hidden_gated, full_down)
    grad_two_part, grad_experts_w = expert_products(
        hidden_gated,
        grad_gate_part,
        grad_up_part,
        normed_two,
        grad_rows,
        full_gate_up,
    )
    ffn_branch = lax.psum_scatter(
        combined, "tensor", scatter_dimension=0, tiled=True
    ).astype(jnp.float32)
    output = (middle + ffn_branch).astype(jnp.bfloat16)
    grad_probs = small_sum(count, (gate_dot * kept).T, 6).T
    grad_logits = router_probs * (
        grad_probs - jnp.sum(router_probs * grad_probs, axis=1, keepdims=True)
    )
    logits_low = grad_logits.astype(jnp.bfloat16)
    grad_router = jnp.einsum(
        "sd,se->de", normed_two, logits_low, preferred_element_type=jnp.float32
    )
    own_logits = lax.dynamic_slice_in_dim(logits_low, tensor_rank * local_rows, local_rows)
    sum_experts = lax.psum_scatter(grad_experts_w, "dp", scatter_dimension=0, tiled=True)
    router_part = jnp.einsum(
        "se,de->sd", own_logits, full_router, preferred_element_type=jnp.float32
    )
    grad_attn_rows, grad_middle, grad_ffn_gain = middle_back_exchange(
        count, grad_two_part, router_part, middle, cotangent, ffn_scale[None, :]
    )
    grad_out_w = jnp.einsum(
        "sf,sd->df", mixed_low, grad_attn_rows, preferred_element_type=jnp.float32
    ).astype(jnp.bfloat16)
    grad_mixed = jnp.dot(grad_attn_rows, w_o_t, preferred_element_type=jnp.float32).astype(
        jnp.bfloat16
    )
    query_scaled, key_scaled, grad_value_low, dots, grad_query_gain, grad_key_gain = attend_back(
        q_rot,
        k_rot,
        value_low,
        grad_mixed,
        after(log_totals, ffn_branch),
        projected,
        inverses,
        query_row,
        key_row,
        tables,
        ids_col,
        ids_row,
    )
    dots = small_sum(count, dots.T, 7).T / model_width
    query_inv, key_inv = inverses[:, 0:1], inverses[:, 1:2]
    grad_query_proj = (
        query_inv * (query_scaled - query_proj * query_inv * dots[:, 0:1])
    ).astype(jnp.bfloat16)
    grad_key_proj = (key_inv * (key_scaled - key_proj * key_inv * dots[:, 1:2])).astype(
        jnp.bfloat16
    )
    grad_qkv = jnp.concatenate([grad_query_proj, grad_key_proj, grad_value_low], axis=1)
    grad_qkv_w = (
        jnp.einsum("sd,sf->df", unit_rows, grad_qkv, preferred_element_type=jnp.float32)
        * attn_scale[:, None]
    ).astype(jnp.bfloat16)
    grad_router_wide = jnp.pad(grad_router, ((0, 0), (0, 128 - EXPERTS))).astype(jnp.bfloat16)
    sum_heads = lax.psum_scatter(
        jnp.concatenate([grad_qkv_w, grad_out_w, grad_router_wide], axis=1),
        "dp",
        scatter_dimension=0,
        tiled=True,
    ).astype(jnp.float32)
    grad_normed_part = jnp.einsum(
        "sf,df->sd", grad_qkv, w_qkv, preferred_element_type=jnp.float32
    ).astype(jnp.bfloat16)
    grad_source, grad_attn_gain = end_exchange(
        count, grad_normed_part, grad_middle, tokens, attn_scale[None, :], (sum_experts,)
    )
    zero_cols = jnp.zeros((model_width,), jnp.float32)
    query_gain_full = lax.dynamic_update_slice_in_dim(zero_cols, grad_query_gain[0], col_start, 0)
    key_gain_full = lax.dynamic_update_slice_in_dim(zero_cols, grad_key_gain[0], col_start, 0)
    gain_stack = jnp.stack([grad_attn_gain, query_gain_full, key_gain_full, grad_ffn_gain])
    dp_count = lax.axis_size("dp")
    gain_width = model_width // (dp_count * count)
    gain_blocks = gain_stack.reshape(4, dp_count * count, gain_width).transpose(1, 0, 2)
    gain_blocks = jnp.pad(gain_blocks, ((0, 0), (0, 4), (0, 128 - gain_width)))
    gain_sums = scatter_sum(dp_count, count, gain_blocks, 8)[:4, :gain_width]
    sum_heads = after(sum_heads, grad_attn_gain[None])
    sum_qkv = sum_heads[:, : 3 * head_cols]
    sum_out = sum_heads[:, 3 * head_cols : 4 * head_cols]
    sum_router = sum_heads[:, 4 * head_cols : 4 * head_cols + EXPERTS]
    grad_gate, grad_up, grad_down = split_experts(sum_experts, ff_here)
    return (
        output,
        grad_source,
        gain_sums[0],
        gain_sums[1],
        gain_sums[2],
        sum_qkv[:, :head_cols],
        sum_qkv[:, head_cols : 2 * head_cols],
        sum_qkv[:, 2 * head_cols :],
        sum_out.T.astype(jnp.float32),
        gain_sums[3],
        sum_router,
        grad_gate,
        grad_up,
        grad_down,
    )


def solution(mesh):
    placed = (
        P(("dp", "tensor"), None),
        P(("dp", "tensor"), None),
        P("dp", None),
        P("dp", None),
        P("dp"),
        P("dp"),
        P("dp"),
        P("dp", "tensor"),
        P("dp", "tensor"),
        P("dp", "tensor"),
        P("tensor", "dp"),
        P("dp"),
        P("dp", None),
        P(None, "dp", "tensor"),
        P(None, "dp", "tensor"),
        P(None, "tensor", "dp"),
    )
    return jax.shard_map(
        local,
        mesh=mesh,
        in_specs=placed,
        out_specs=(
            P(("dp", "tensor"), None),
            P(("dp", "tensor"), None),
            P(("dp", "tensor")),
            P(("dp", "tensor")),
            P(("dp", "tensor")),
            P("dp", "tensor"),
            P("dp", "tensor"),
            P("dp", "tensor"),
            P("tensor", "dp"),
            P(("dp", "tensor")),
            P("dp", None),
            P(None, "dp", "tensor"),
            P(None, "dp", "tensor"),
            P(None, "tensor", "dp"),
        ),
        check_vma=False,
    )
```

```python
import math

import jax
import jax.numpy as jnp
import numpy as np
from jax import lax
from jax.experimental import pallas as pl
from jax.experimental.pallas import tpu as pltpu
from jax.sharding import PartitionSpec as P

HEAD_DIM = 128
EXPERTS = 8
TOPK = 2
BLOCK = 256
CAP = 320


EPSILON = 1e-05
MASKED = -1e30
MESH = pl.DeviceIdType.MESH
CHUNK_ROWS = 16


def rms_scale(source):
    return source * lax.rsqrt(jnp.mean(source * source, axis=-1, keepdims=True) + EPSILON)


def rope_constants(seq_len):
    half_dim = HEAD_DIM // 2
    frequency = np.exp(-math.log(10000.0) * 2.0 * np.arange(half_dim) / HEAD_DIM)
    angles = np.arange(seq_len)[:, None] * frequency[None, :]
    cosine = np.concatenate([np.cos(angles)] * 2, axis=1).astype(np.float32)
    sine = np.concatenate([-np.sin(angles), np.sin(angles)], axis=1).astype(np.float32)
    return jnp.asarray(cosine), jnp.asarray(sine)


def masked_scores(q_rows, k_rows, ids_col, ids_row):
    scores = lax.dot_general(
        q_rows, k_rows, (((1,), (1,)), ((), ())), preferred_element_type=jnp.float32
    ) * (HEAD_DIM ** (-0.5))
    return jnp.where(ids_row <= ids_col, scores, MASKED)


def key_limit(start, seq_len):
    return min(seq_len, start + 2 * BLOCK)


def attend_kernel(
    q_ref, k_ref, v_ref, inv_ref, qg_ref, kg_ref, cos_ref, sin_ref, col_ref, row_ref,
    q_out, k_out, v_out, mixed_out, log_out,
):
    head = pl.program_id(0)
    seq_len = q_ref.shape[0]
    cosine, sine = cos_ref[...], sin_ref[...]

    def turn(rows):
        return (rows * cosine + pltpu.roll(rows, HEAD_DIM // 2, 1) * sine).astype(jnp.bfloat16)

    q_out[...] = turn(q_ref[...] * inv_ref[:, 0:1] * qg_ref[...])
    k_out[...] = turn(k_ref[...] * inv_ref[:, 1:2] * kg_ref[...])
    v_out[...] = v_ref[...].astype(jnp.bfloat16)

    @pl.when(head == 0)
    def _():
        log_out[...] = jnp.zeros_like(log_out)

    for start in range(0, seq_len, BLOCK):
        rows = pl.ds(start, BLOCK)
        keys = pl.ds(0, key_limit(start, seq_len))
        scores = masked_scores(q_out[rows, :], k_out[keys, :], col_ref[rows, :], row_ref[:, keys])
        top = jnp.max(scores, axis=-1, keepdims=True)
        powers = jnp.exp(scores - top)
        total = jnp.sum(powers, axis=-1, keepdims=True)
        weights = (powers * (1.0 / total)).astype(jnp.bfloat16)
        mixed_out[rows, :] = jnp.dot(
            weights, v_out[keys, :], preferred_element_type=jnp.float32
        ).astype(jnp.bfloat16)
        lane = lax.broadcasted_iota(jnp.int32, (BLOCK, log_out.shape[1]), 1)
        log_out[rows, :] = log_out[rows, :] + jnp.where(
            lane == head, top + jnp.log(total), 0.0
        )


def attend(projected, inverses, q_gain_row, k_gain_row, tables, ids_col, ids_row):
    seq_len = projected.shape[0]
    heads = projected.shape[1] // (3 * HEAD_DIM)
    cols = heads * HEAD_DIM
    whole = pl.BlockSpec(memory_space=pltpu.VMEM)
    gain = pl.BlockSpec((1, HEAD_DIM), lambda h: (0, h))
    column = pl.BlockSpec((seq_len, HEAD_DIM), lambda h: (0, h))
    flat = jax.ShapeDtypeStruct((seq_len, cols), jnp.bfloat16)
    return pl.pallas_call(
        attend_kernel,
        grid=(heads,),
        out_shape=(flat, flat, flat, flat, jax.ShapeDtypeStruct((seq_len, heads), jnp.float32)),
        in_specs=[
            column,
            pl.BlockSpec((seq_len, HEAD_DIM), lambda h: (0, heads + h)),
            pl.BlockSpec((seq_len, HEAD_DIM), lambda h: (0, 2 * heads + h)),
            whole,
            gain,
            gain,
            whole,
            whole,
            whole,
            whole,
        ],
        out_specs=(
            column,
            column,
            column,
            column,
            pl.BlockSpec((seq_len, heads), lambda h: (0, 0)),
        ),
        compiler_params=pltpu.CompilerParams(vmem_limit_bytes=48 * 1024 * 1024),
        cost_estimate=pl.CostEstimate(
            flops=20 * seq_len * seq_len * cols, bytes_accessed=projected.size * 4, transcendentals=0
        ),
    )(
        projected, projected, projected, inverses, q_gain_row, k_gain_row, tables[0], tables[1],
        ids_col, ids_row,
    )


def attend_back_kernel(
    q_ref, k_ref, v_ref, g_ref, log_ref, qp_ref, kp_ref, inv_ref, qg_ref, kg_ref, cos_ref, sin_ref,
    col_ref, row_ref, gq_out, gk_out, gv_out, dot_out, qgain_out, kgain_out, dq_acc, dk_acc, dv_acc,
):
    head = pl.program_id(0)
    seq_len = q_ref.shape[0]
    scale = HEAD_DIM ** (-0.5)
    dk_acc[...] = jnp.zeros_like(dk_acc)
    dv_acc[...] = jnp.zeros_like(dv_acc)

    def down(left, right):
        return lax.dot_general(
            left, right, (((0,), (0,)), ((), ())), preferred_element_type=jnp.float32
        )

    for start in range(0, seq_len, BLOCK):
        rows = pl.ds(start, BLOCK)
        keys = pl.ds(0, key_limit(start, seq_len))
        scores = masked_scores(q_ref[rows, :], k_ref[keys, :], col_ref[rows, :], row_ref[:, keys])
        lane = lax.broadcasted_iota(jnp.int32, (BLOCK, log_ref.shape[1]), 1)
        log_total = jnp.sum(jnp.where(lane == head, log_ref[rows, :], 0.0), axis=1, keepdims=True)
        weights = jnp.exp(scores - log_total)
        grad_weights = lax.dot_general(
            g_ref[rows, :],
            v_ref[keys, :],
            (((1,), (1,)), ((), ())),
            preferred_element_type=jnp.float32,
        )
        grad_scores = (
            weights * (grad_weights - jnp.sum(weights * grad_weights, axis=-1, keepdims=True))
        ).astype(jnp.bfloat16)
        dq_acc[rows, :] = (
            jnp.dot(grad_scores, k_ref[keys, :], preferred_element_type=jnp.float32) * scale
        )
        dk_acc[keys, :] = dk_acc[keys, :] + down(grad_scores, q_ref[rows, :]) * scale
        dv_acc[keys, :] = dv_acc[keys, :] + down(weights.astype(jnp.bfloat16), g_ref[rows, :])
    gv_out[...] = dv_acc[...].astype(jnp.bfloat16)
    cosine, sine = cos_ref[...], sin_ref[...]

    @pl.when(head == 0)
    def _():
        dot_out[...] = jnp.zeros_like(dot_out)

    def turn_back(rows):
        return rows * cosine - pltpu.roll(rows, HEAD_DIM // 2, 1) * sine

    lane = lax.broadcasted_iota(jnp.int32, dot_out.shape, 1)
    for which, acc, proj, gain, out, gain_out in (
        (0, dq_acc, qp_ref, qg_ref, gq_out, qgain_out),
        (1, dk_acc, kp_ref, kg_ref, gk_out, kgain_out),
    ):
        grad = turn_back(acc[...])
        normed = proj[...] * inv_ref[:, which : which + 1]
        gain_out[...] = jnp.sum(grad * normed, axis=0, keepdims=True)
        scaled = grad * gain[...]
        out[...] = scaled
        dot_out[...] = dot_out[...] + jnp.where(
            lane == which, jnp.sum(scaled * normed, axis=1, keepdims=True), 0.0
        )


def attend_back(
    q_rot, k_rot, value_low, grad_mixed, log_totals, projected, inverses, q_gain_row, k_gain_row,
    tables, ids_col, ids_row,
):
    seq_len, cols = q_rot.shape
    heads = cols // HEAD_DIM
    whole = pl.BlockSpec(memory_space=pltpu.VMEM)
    gain = pl.BlockSpec((1, HEAD_DIM), lambda h: (0, h))
    column = pl.BlockSpec((seq_len, HEAD_DIM), lambda h: (0, h))
    wide = jax.ShapeDtypeStruct((seq_len, cols), jnp.float32)
    gain_shape = jax.ShapeDtypeStruct((1, cols), jnp.float32)
    return pl.pallas_call(
        attend_back_kernel,
        grid=(heads,),
        out_shape=(
            wide,
            wide,
            jax.ShapeDtypeStruct((seq_len, cols), jnp.bfloat16),
            jax.ShapeDtypeStruct((seq_len, 2), jnp.float32),
            gain_shape,
            gain_shape,
        ),
        in_specs=[
            column,
            column,
            column,
            column,
            whole,
            column,
            pl.BlockSpec((seq_len, HEAD_DIM), lambda h: (0, heads + h)),
            whole,
            gain,
            gain,
            whole,
            whole,
            whole,
            whole,
        ],
        out_specs=(
            column,
            column,
            column,
            pl.BlockSpec((seq_len, 2), lambda h: (0, 0)),
            gain,
            gain,
        ),
        scratch_shapes=[pltpu.VMEM((seq_len, HEAD_DIM), jnp.float32)] * 3,
        compiler_params=pltpu.CompilerParams(vmem_limit_bytes=48 * 1024 * 1024),
        cost_estimate=pl.CostEstimate(
            flops=60 * seq_len * seq_len * cols, bytes_accessed=projected.size * 4, transcendentals=0
        ),
    )(
        q_rot, k_rot, value_low, grad_mixed, log_totals, projected, projected, inverses,
        q_gain_row, k_gain_row, tables[0], tables[1], ids_col, ids_row,
    )


def kept_mask(route_rows):
    expert_ids = jnp.arange(EXPERTS, dtype=jnp.int32)
    first = (route_rows[:, 0:1] == expert_ids[None, :]).astype(jnp.int32)
    second = (route_rows[:, 1:2] == expert_ids[None, :]).astype(jnp.int32)
    both = first + second
    earlier = jnp.cumsum(both, axis=0) - both
    return jnp.where((both > 0) & (earlier < CAP), 1.0, 0.0).astype(jnp.float32)


def neighbour_barrier(me, count):
    barrier = pltpu.get_barrier_semaphore()

    @pl.when(me > 0)
    def _():
        pl.semaphore_signal(barrier, inc=1, device_id={"tensor": me - 1}, device_id_type=MESH)

    @pl.when(me < count - 1)
    def _():
        pl.semaphore_signal(barrier, inc=1, device_id={"tensor": me + 1}, device_id_type=MESH)

    pl.semaphore_wait(
        barrier, jnp.minimum(me, 1).astype(jnp.int32) + jnp.minimum(count - 1 - me, 1)
    )


def line_exchange(
    count, chunks, rows, width, part, extras, out_shapes, epilogue, gather, collective_id, prologue=None, waits=()
):
    reduce = part is not None
    n_extra = len(extras)
    n_out = len(out_shapes)
    last = count - 1
    back_lag = last if reduce else 0
    pass_lag = back_lag if reduce else chunks

    def kernel(*refs):
        refs = list(refs)
        part_ref = refs.pop(0) if reduce else None
        extra_refs = [refs.pop(0) for _ in range(n_extra)]
        del refs[: len(waits)]
        full_ref = refs.pop(0) if gather else None
        out_refs = [refs.pop(0) for _ in range(n_out)]
        if reduce:
            sum_right, sum_left, acc = refs.pop(0), refs.pop(0), refs.pop(0)
            rs_send_r, rs_recv_r, rs_send_l, rs_recv_l = [refs.pop(0) for _ in range(4)]
        if gather:
            ag_send_r, ag_recv_r, ag_send_l, ag_recv_l = [refs.pop(0) for _ in range(4)]
        me = lax.axis_index("tensor")
        right, left = jnp.minimum(me + 1, last), jnp.maximum(me - 1, 0)

        def remote(source, target, send_sem, recv_sem, device):
            return pltpu.make_async_remote_copy(
                src_ref=source,
                dst_ref=target,
                send_sem=send_sem,
                recv_sem=recv_sem,
                device_id={"tensor": device},
                device_id_type=MESH,
            )

        def rs_right(block, chunk, source=None):
            here = sum_right.at[block, chunk]
            return remote(
                here if source is None else source,
                here,
                rs_send_r.at[block, chunk],
                rs_recv_r.at[block, chunk],
                right,
            )

        def rs_left(block, chunk, source=None):
            here = sum_left.at[block, chunk]
            return remote(
                here if source is None else source,
                here,
                rs_send_l.at[block, chunk],
                rs_recv_l.at[block, chunk],
                left,
            )

        def ag_right(block, chunk):
            here = full_ref.at[block, chunk]
            return remote(
                here, here, ag_send_r.at[block, chunk], ag_recv_r.at[block, chunk], right
            )

        def ag_left(block, chunk):
            here = full_ref.at[block, chunk]
            return remote(here, here, ag_send_l.at[block, chunk], ag_recv_l.at[block, chunk], left)

        neighbour_barrier(me, count)
        if prologue is not None:
            prologue(extra_refs, out_refs)

        def send_right(chunk):
            for step in range(last):
                far = last - step

                @pl.when(jnp.logical_and(me < far, me == 0))
                def _():
                    rs_right(far, chunk, part_ref.at[far, chunk]).start()

                @pl.when(jnp.logical_and(me < far, me > 0))
                def _():
                    rs_right(far, chunk).wait_recv()
                    sum_right[far, chunk] = sum_right[far, chunk] + part_ref[far, chunk]
                    rs_right(far, chunk).start()

        def send_left(chunk):
            for step in range(last):

                @pl.when(jnp.logical_and(me > step, me == last))
                def _():
                    rs_left(step, chunk, part_ref.at[step, chunk]).start()

                @pl.when(jnp.logical_and(me > step, me < last))
                def _():
                    rs_left(step, chunk).wait_recv()
                    sum_left[step, chunk] = sum_left[step, chunk] + part_ref[step, chunk]
                    rs_left(step, chunk).start()

        def finish(chunk):
            if reduce:
                acc[...] = part_ref[me, chunk].astype(jnp.float32)

                @pl.when(me > 0)
                def _():
                    rs_right(me, chunk).wait_recv()
                    acc[...] = acc[...] + sum_right[me, chunk].astype(jnp.float32)

                @pl.when(me < last)
                def _():
                    rs_left(me, chunk).wait_recv()
                    acc[...] = acc[...] + sum_left[me, chunk].astype(jnp.float32)

                made = epilogue(chunk, acc[...], extra_refs, out_refs)
            else:
                made = epilogue(chunk, None, extra_refs, out_refs)
            if gather:
                full_ref[me, chunk] = made

                @pl.when(me < last)
                def _():
                    ag_right(me, chunk).start()

                @pl.when(me > 0)
                def _():
                    ag_left(me, chunk).start()

        def forward(chunk, step):
            @pl.when(me - step >= 0)
            def _():
                ag_right(jnp.maximum(me - step, 0), chunk).wait_recv()

            @pl.when(jnp.logical_and(me - step >= 0, me < last))
            def _():
                ag_right(jnp.maximum(me - step, 0), chunk).start()

            @pl.when(me + step <= last)
            def _():
                ag_left(jnp.minimum(me + step, last), chunk).wait_recv()

            @pl.when(jnp.logical_and(me + step <= last, me > 0))
            def _():
                ag_left(jnp.minimum(me + step, last), chunk).start()

        def at_chunk(chunk, work):
            @pl.when(jnp.logical_and(chunk >= 0, chunk < chunks))
            def _():
                work(jnp.clip(chunk, 0, chunks - 1))

        def tick(time, carry):
            if reduce:
                at_chunk(time - me, send_right)
                at_chunk(time - (last - me), send_left)
            at_chunk(time - back_lag, finish)
            if gather:
                for step in range(1, count):
                    at_chunk(time - pass_lag - step, lambda chunk: forward(chunk, step))
            return carry

        ticks = chunks + (pass_lag + last if gather else back_lag)
        lax.fori_loop(0, ticks, tick, 0)

        def drain(chunk, carry):
            for block in range(count):
                if reduce:

                    @pl.when(me < block)
                    def _():
                        rs_right(block, chunk).wait_send()

                    @pl.when(me > block)
                    def _():
                        rs_left(block, chunk).wait_send()

                if gather:

                    @pl.when(jnp.logical_and(block <= me, me < last))
                    def _():
                        ag_right(block, chunk).wait_send()

                    @pl.when(jnp.logical_and(block >= me, me > 0))
                    def _():
                        ag_left(block, chunk).wait_send()

            return carry

        lax.fori_loop(0, chunks, drain, 0)

    block = (count, chunks, rows, width)
    shapes = []
    if gather:
        shapes.append(jax.ShapeDtypeStruct(block, jnp.bfloat16))
    shapes.extend(out_shapes)
    scratch = []
    if reduce:
        scratch += [
            pltpu.VMEM(block, jnp.bfloat16),
            pltpu.VMEM(block, jnp.bfloat16),
            pltpu.VMEM((rows, width), jnp.float32),
        ]
        scratch += [pltpu.SemaphoreType.DMA((count, chunks))] * 4
    if gather:
        scratch += [pltpu.SemaphoreType.DMA((count, chunks))] * 4
    operands = ([part] if reduce else []) + list(extras)
    block_bytes = count * chunks * rows * width * 2
    results = pl.pallas_call(
        kernel,
        out_shape=tuple(shapes),
        in_specs=[pl.BlockSpec(memory_space=pltpu.VMEM)] * len(operands)
        + [pl.BlockSpec(memory_space=pl.ANY)] * len(waits),
        out_specs=tuple([pl.BlockSpec(memory_space=pltpu.VMEM)] * len(shapes)),
        scratch_shapes=scratch,
        compiler_params=pltpu.CompilerParams(
            collective_id=collective_id, has_side_effects=True, vmem_limit_bytes=56 * 1024 * 1024
        ),
        cost_estimate=pl.CostEstimate(
            flops=0,
            bytes_accessed=block_bytes * (60 if reduce and gather else 45),
            transcendentals=0,
        ),
    )(*operands, *waits)
    return results


def small_sum(count, values, collective_id, axis="tensor"):
    def kernel(in_ref, out_ref, slots, send_sems, recv_sems):
        me = lax.axis_index(axis)
        barrier = pltpu.get_barrier_semaphore()
        for offset in range(1, count):
            peer = lax.rem(me + offset, count)
            pl.semaphore_signal(barrier, inc=1, device_id={axis: peer}, device_id_type=MESH)
        pl.semaphore_wait(barrier, count - 1)

        def send(offset):
            return pltpu.make_async_remote_copy(
                src_ref=in_ref,
                dst_ref=slots.at[offset - 1],
                send_sem=send_sems.at[offset - 1],
                recv_sem=recv_sems.at[offset - 1],
                device_id={axis: lax.rem(me + offset, count)},
                device_id_type=MESH,
            )

        for offset in range(1, count):
            send(offset).start()
        total = in_ref[...]
        for offset in range(1, count):
            send(offset).wait_recv()
            total = total + slots[offset - 1]
        out_ref[...] = total
        for offset in range(1, count):
            send(offset).wait_send()

    return pl.pallas_call(
        kernel,
        out_shape=jax.ShapeDtypeStruct(values.shape, jnp.float32),
        in_specs=[pl.BlockSpec(memory_space=pltpu.VMEM)],
        out_specs=pl.BlockSpec(memory_space=pltpu.VMEM),
        scratch_shapes=[
            pltpu.VMEM((count - 1,) + values.shape, jnp.float32),
            pltpu.SemaphoreType.DMA((count - 1,)),
            pltpu.SemaphoreType.DMA((count - 1,)),
        ],
        compiler_params=pltpu.CompilerParams(collective_id=collective_id, has_side_effects=True),
    )(values)


def start_gather(count, tokens):
    rows, width = tokens.shape
    step, chunks = CHUNK_ROWS, rows // CHUNK_ROWS

    def epilogue(chunk, total, extra_refs, out_refs):
        value = extra_refs[0][chunk].astype(jnp.float32)
        return rms_scale(value).astype(jnp.bfloat16)

    (full,) = line_exchange(
        count,
        chunks,
        step,
        width,
        None,
        [tokens.reshape(chunks, step, width)],
        [],
        epilogue,
        True,
        1,
    )
    return full.reshape(count * rows, width)


def middle_exchange(count, branch_part, tokens, gain_row, waits):
    rows, width = tokens.shape
    step, chunks = CHUNK_ROWS, rows // CHUNK_ROWS

    def epilogue(chunk, total, extra_refs, out_refs):
        value = extra_refs[0][chunk].astype(jnp.float32) + total
        out_refs[0][chunk] = value
        return (rms_scale(value) * extra_refs[1][...]).astype(jnp.bfloat16)

    full, middle = line_exchange(
        count,
        chunks,
        step,
        width,
        branch_part.reshape(count, chunks, step, width),
        [tokens.reshape(chunks, step, width), gain_row],
        [jax.ShapeDtypeStruct((chunks, step, width), jnp.float32)],
        epilogue,
        True,
        2,
        None,
        waits,
    )
    return full.reshape(count * rows, width), middle.reshape(rows, width)


def norm_back_rows(value, gain_row, grad_out):
    inverse = lax.rsqrt(jnp.mean(value * value, axis=-1, keepdims=True) + EPSILON)
    normed = value * inverse
    scaled = grad_out * gain_row
    grad_in = inverse * (scaled - normed * jnp.mean(scaled * normed, axis=-1, keepdims=True))
    return grad_in, jnp.sum(grad_out * normed, axis=0, keepdims=True)


def zero_gain(extra_refs, out_refs):
    out_refs[1][...] = jnp.zeros_like(out_refs[1])


def middle_back_exchange(count, grad_part, router_part, middle, cotangent, gain_row):
    rows, width = middle.shape
    step, chunks = CHUNK_ROWS, rows // CHUNK_ROWS

    def epilogue(chunk, total, extra_refs, out_refs):
        grad_out = total + extra_refs[0][chunk]
        grad_in, grad_gain = norm_back_rows(extra_refs[1][chunk], extra_refs[3][...], grad_out)
        out_refs[1][...] = out_refs[1][...] + grad_gain
        grad_middle = extra_refs[2][chunk].astype(jnp.float32) + grad_in
        out_refs[0][chunk] = grad_middle
        return grad_middle.astype(jnp.bfloat16)

    full, grad_middle, grad_gain = line_exchange(
        count,
        chunks,
        step,
        width,
        grad_part.reshape(count, chunks, step, width),
        [
            router_part.reshape(chunks, step, width),
            middle.reshape(chunks, step, width),
            cotangent.reshape(chunks, step, width),
            gain_row,
        ],
        [
            jax.ShapeDtypeStruct((chunks, step, width), jnp.float32),
            jax.ShapeDtypeStruct((1, width), jnp.float32),
        ],
        epilogue,
        True,
        3,
        zero_gain,
    )
    return full.reshape(count * rows, width), grad_middle.reshape(rows, width), grad_gain[0]


def end_exchange(count, grad_part, grad_middle, tokens, gain_row, waits):
    rows, width = tokens.shape
    step, chunks = CHUNK_ROWS, rows // CHUNK_ROWS

    def epilogue(chunk, total, extra_refs, out_refs):
        value = extra_refs[1][chunk].astype(jnp.float32)
        grad_in, grad_gain = norm_back_rows(value, extra_refs[2][...], total)
        out_refs[1][...] = out_refs[1][...] + grad_gain
        out_refs[0][chunk] = extra_refs[0][chunk] + grad_in

    grad_source, grad_gain = line_exchange(
        count,
        chunks,
        step,
        width,
        grad_part.reshape(count, chunks, step, width),
        [
            grad_middle.reshape(chunks, step, width),
            tokens.reshape(chunks, step, width),
            gain_row,
        ],
        [
            jax.ShapeDtypeStruct((chunks, step, width), jnp.float32),
            jax.ShapeDtypeStruct((1, width), jnp.float32),
        ],
        epilogue,
        False,
        4,
        zero_gain,
        waits,
    )
    return grad_source.reshape(rows, width), grad_gain[0]


def expert_kernel(x_ref, c_ref, gates_ref, wg_ref, wu_ref, wd_ref, hg_ref, dg_ref, du_ref, gd_ref):
    expert = pl.program_id(0)
    rows_in = x_ref[...]
    gate_part = jnp.dot(rows_in, wg_ref[...], preferred_element_type=jnp.float32)
    up_part = jnp.dot(rows_in, wu_ref[...], preferred_element_type=jnp.float32)
    back_hidden = jnp.dot(c_ref[...], wd_ref[...], preferred_element_type=jnp.float32)
    mine = lax.broadcasted_iota(jnp.int32, gates_ref.shape, 1) == expert
    gates = jnp.sum(jnp.where(mine, gates_ref[...], 0.0), axis=1, keepdims=True)
    sigmoid_gate = jax.nn.sigmoid(gate_part)
    silu_gate = gate_part * sigmoid_gate
    hidden = silu_gate * up_part
    gate_dot = jnp.sum(hidden * back_hidden, axis=1, keepdims=True)

    @pl.when(expert == 0)
    def _():
        gd_ref[...] = jnp.zeros_like(gd_ref)

    gd_ref[...] = gd_ref[...] + jnp.where(mine, gate_dot, 0.0)
    hg_ref[...] = (hidden * gates).astype(jnp.bfloat16)
    grad_hidden = back_hidden * gates
    dg_ref[...] = (
        grad_hidden * up_part * sigmoid_gate * (1.0 + gate_part * (1.0 - sigmoid_gate))
    ).astype(jnp.bfloat16)
    du_ref[...] = (grad_hidden * silu_gate).astype(jnp.bfloat16)


def expert_parts(rows_in, rows_grad, gates, weights, down, ff_here):
    seq_len, width = rows_in.shape
    hidden_cols = EXPERTS * ff_here
    whole = pl.BlockSpec(memory_space=pltpu.VMEM)
    part = jax.ShapeDtypeStruct((seq_len, hidden_cols), jnp.bfloat16)
    column = pl.BlockSpec((seq_len, ff_here), lambda e: (0, e))
    flops = 6 * seq_len * width * hidden_cols
    return pl.pallas_call(
        expert_kernel,
        grid=(EXPERTS,),
        out_shape=(part, part, part, jax.ShapeDtypeStruct((seq_len, EXPERTS), jnp.float32)),
        in_specs=[
            whole,
            whole,
            whole,
            pl.BlockSpec((width, ff_here), lambda e: (0, e)),
            pl.BlockSpec((width, ff_here), lambda e: (0, EXPERTS + e)),
            pl.BlockSpec((width, ff_here), lambda e: (0, e)),
        ],
        out_specs=(
            column,
            column,
            column,
            pl.BlockSpec((seq_len, EXPERTS), lambda e: (0, 0)),
        ),
        compiler_params=pltpu.CompilerParams(vmem_limit_bytes=56 * 1024 * 1024),
        cost_estimate=pl.CostEstimate(
            flops=flops, bytes_accessed=weights.size * 2, transcendentals=0
        ),
    )(rows_in, rows_grad, gates, weights, weights, down)


def product_kernel(hg_ref, dg_ref, du_ref, x_ref, c_ref, w_ref, dx_ref, dw_ref):
    cols = hg_ref.shape[1]

    def times_weight(left, which):
        right = w_ref[:, which * cols : (which + 1) * cols]
        return lax.dot_general(
            left, right, (((1,), (1,)), ((), ())), preferred_element_type=jnp.float32
        )

    def weight_grad(rows, grad):
        return lax.dot_general(
            rows, grad, (((0,), (0,)), ((), ())), preferred_element_type=jnp.float32
        ).astype(jnp.bfloat16)

    dx_ref[...] = (times_weight(dg_ref[...], 0) + times_weight(du_ref[...], 1)).astype(
        jnp.bfloat16
    )
    dw_ref[:, :cols] = weight_grad(x_ref[...], dg_ref[...])
    dw_ref[:, cols : 2 * cols] = weight_grad(x_ref[...], du_ref[...])
    dw_ref[:, 2 * cols :] = weight_grad(c_ref[...], hg_ref[...])


def expert_products(hg, dg, du, rows_in, rows_grad, weights):
    seq_len, width = rows_in.shape
    cols = hg.shape[1]
    tile = 256
    whole = pl.BlockSpec(memory_space=pltpu.VMEM)
    column = pl.BlockSpec((seq_len, tile), lambda i: (0, i))
    row = pl.BlockSpec((tile, 3 * cols), lambda i: (i, 0))
    pair = pl.BlockSpec((tile, 2 * cols), lambda i: (i, 0))
    flat = jax.ShapeDtypeStruct((seq_len, width), jnp.bfloat16)
    return pl.pallas_call(
        product_kernel,
        grid=(width // tile,),
        out_shape=(flat, jax.ShapeDtypeStruct((width, 3 * cols), jnp.bfloat16)),
        in_specs=[whole, whole, whole, column, column, pair],
        out_specs=(column, row),
        compiler_params=pltpu.CompilerParams(vmem_limit_bytes=56 * 1024 * 1024),
        cost_estimate=pl.CostEstimate(
            flops=10 * seq_len * width * cols, bytes_accessed=weights.size * 4, transcendentals=0
        ),
    )(hg, dg, du, rows_in, rows_grad, weights)


def output_kernel(hg_ref, w_ref, out_ref):
    out_ref[...] = lax.dot_general(
        hg_ref[...], w_ref[...], (((1,), (1,)), ((), ())), preferred_element_type=jnp.float32
    ).astype(jnp.bfloat16)


def expert_output(hg, weights):
    seq_len, cols = hg.shape
    width = weights.shape[0]
    tile = 256
    return pl.pallas_call(
        output_kernel,
        grid=(width // tile,),
        out_shape=jax.ShapeDtypeStruct((seq_len, width), jnp.bfloat16),
        in_specs=[
            pl.BlockSpec(memory_space=pltpu.VMEM),
            pl.BlockSpec((tile, cols), lambda i: (i, 0)),
        ],
        out_specs=pl.BlockSpec((seq_len, tile), lambda i: (0, i)),
        compiler_params=pltpu.CompilerParams(vmem_limit_bytes=40 * 1024 * 1024),
        cost_estimate=pl.CostEstimate(
            flops=2 * seq_len * width * cols, bytes_accessed=width * cols * 2, transcendentals=0
        ),
    )(hg, weights)


def split_kernel(gate_ref, up_ref, down_ref, gate_out, up_out, down_out):
    gate_out[0] = gate_ref[...].astype(jnp.float32)
    up_out[0] = up_ref[...].astype(jnp.float32)
    down_out[0] = down_ref[...].astype(jnp.float32).T


def split_experts(sums, ff_here):
    width = sums.shape[0]

    def part(which):
        return pl.BlockSpec((width, ff_here), lambda e: (0, which * EXPERTS + e))

    wide = jax.ShapeDtypeStruct((EXPERTS, width, ff_here), jnp.float32)
    tall = jax.ShapeDtypeStruct((EXPERTS, ff_here, width), jnp.float32)
    wide_spec = pl.BlockSpec((1, width, ff_here), lambda e: (e, 0, 0))
    tall_spec = pl.BlockSpec((1, ff_here, width), lambda e: (e, 0, 0))
    return pl.pallas_call(
        split_kernel,
        grid=(EXPERTS,),
        out_shape=(wide, wide, tall),
        in_specs=[part(0), part(1), part(2)],
        out_specs=(wide_spec, wide_spec, tall_spec),
    )(sums, sums, sums)


def scatter_sum(dp_count, count, values, collective_id):
    total_count = dp_count * count

    def kernel(in_ref, out_ref, slots, send_sems, recv_sems):
        me = lax.axis_index("dp") * count + lax.axis_index("tensor")

        def peer(offset):
            other = lax.rem(me + offset, total_count)
            return other, {"dp": other // count, "tensor": lax.rem(other, count)}

        barrier = pltpu.get_barrier_semaphore()

        def greet(offset, carry):
            pl.semaphore_signal(
                barrier, inc=1, device_id=peer(offset)[1], device_id_type=MESH
            )
            return carry

        lax.fori_loop(1, total_count, greet, 0)
        pl.semaphore_wait(barrier, total_count - 1)

        def send(offset):
            other, device = peer(offset)
            return pltpu.make_async_remote_copy(
                src_ref=in_ref.at[other],
                dst_ref=slots.at[offset - 1],
                send_sem=send_sems.at[offset - 1],
                recv_sem=recv_sems.at[offset - 1],
                device_id=device,
                device_id_type=MESH,
            )

        def start(offset, carry):
            send(offset).start()
            return carry

        lax.fori_loop(1, total_count, start, 0)

        def collect(offset, total):
            send(offset).wait_recv()
            return total + slots[offset - 1]

        out_ref[...] = lax.fori_loop(1, total_count, collect, in_ref[me])

        def finish(offset, carry):
            send(offset).wait_send()
            return carry

        lax.fori_loop(1, total_count, finish, 0)

    block = values.shape[1:]
    return pl.pallas_call(
        kernel,
        out_shape=jax.ShapeDtypeStruct(block, jnp.float32),
        in_specs=[pl.BlockSpec(memory_space=pltpu.VMEM)],
        out_specs=pl.BlockSpec(memory_space=pltpu.VMEM),
        scratch_shapes=[
            pltpu.VMEM((total_count - 1,) + block, jnp.float32),
            pltpu.SemaphoreType.DMA((total_count - 1,)),
            pltpu.SemaphoreType.DMA((total_count - 1,)),
        ],
        compiler_params=pltpu.CompilerParams(collective_id=collective_id, has_side_effects=True),
    )(values)


def permute_step(pair, count, step):
    if step == count - 1 and count > 3:
        me = lax.axis_index("tensor")
        block = jnp.where(me == count - 2, pair[0], pair[1])
        block = lax.ppermute(block, "tensor", [(count - 2, count - 1), (1, 0)])
        return block, block
    return (
        lax.ppermute(pair[0], "tensor", [(i, i + 1) for i in range(step - 1, count - 1)]),
        lax.ppermute(pair[1], "tensor", [(i, i - 1) for i in range(1, count - step + 1)]),
    )


def tie(values, *waits):
    def kernel(*refs):
        del refs

    place = pl.BlockSpec(memory_space=pl.ANY)
    return pl.pallas_call(
        kernel,
        out_shape=tuple(jax.ShapeDtypeStruct(value.shape, value.dtype) for value in values),
        in_specs=[place] * (len(values) + len(waits)),
        out_specs=tuple([place] * len(values)),
        input_output_aliases={k: k for k in range(len(values))},
    )(*values, *waits)


def place_blocks(pairs, count):
    me = lax.axis_index("tensor")
    rows, width = pairs[0][0].shape
    full = jnp.zeros((count * rows, width), pairs[0][0].dtype)
    for step in range(count):
        piece = pairs[0][0]
        if step > 0:
            piece = jnp.where(me >= step, pairs[step][0], pairs[count - step][1])
        start = lax.rem(me - step + count, count) * rows
        full = lax.dynamic_update_slice_in_dim(full, piece, start, 0)
    return full


def after(value, *others):
    product = 0.0
    for other in others:
        corner = jnp.clip(other[0, 0].astype(jnp.float32), -1.0, 1.0)
        product = corner if other is others[0] else product * corner
    zero = product * 0.0
    return value + zero.astype(value.dtype)


def local(
    tokens,
    cotangent,
    routes,
    block_ids,
    attn_gain,
    q_gain,
    k_gain,
    w_query,
    w_key,
    w_value,
    w_out,
    ffn_gain,
    w_router,
    w_gate,
    w_up,
    w_down,
):
    shard_width = w_query.shape[0]
    head_cols = w_query.shape[1]
    ff_here = w_gate.shape[2]
    hidden_cols = EXPERTS * ff_here
    small_cols = jnp.concatenate(
        [attn_gain[:, None], q_gain[:, None], k_gain[:, None], ffn_gain[:, None], w_router], axis=1
    )
    small_cols = jnp.pad(small_cols, ((0, 0), (0, 128 - small_cols.shape[1])))
    w_heads = lax.all_gather(
        jnp.concatenate([w_query, w_key, w_value, w_out.T, small_cols], axis=1), "dp", axis=0, tiled=True
    )
    w_qkv = w_heads[:, : 3 * head_cols]
    w_o_t = w_heads[:, 3 * head_cols : 4 * head_cols]
    small = w_heads[:, 4 * head_cols : 4 * head_cols + 4 + EXPERTS]
    full_down = lax.all_gather(
        w_down.transpose(2, 0, 1).reshape(shard_width, hidden_cols), "dp", axis=0, tiled=True
    )
    expert_local = jnp.concatenate(
        [
            w_gate.transpose(1, 0, 2).reshape(shard_width, hidden_cols),
            w_up.transpose(1, 0, 2).reshape(shard_width, hidden_cols),
        ],
        axis=1,
    )
    full_router = small[:, 4:]
    model_width = tokens.shape[1]
    local_rows = tokens.shape[0]
    tensor_rank = lax.axis_index("tensor")
    col_start = tensor_rank * head_cols
    gains = small[:, :4].astype(jnp.float32).T
    attn_scale = gains[0]
    query_scale = lax.dynamic_slice_in_dim(gains[1], col_start, head_cols)
    key_scale = lax.dynamic_slice_in_dim(gains[2], col_start, head_cols)
    ffn_scale = gains[3]
    count = lax.axis_size("tensor")
    unit_rows = start_gather(count, tokens)
    normed = (unit_rows.astype(jnp.float32) * attn_scale[None, :]).astype(jnp.bfloat16)
    pairs = [(cotangent, cotangent)]
    first = after(cotangent, unit_rows)
    pairs.append(permute_step((first, first), count, 1))
    seq_len = normed.shape[0]
    ids_row, ids_col = block_ids, block_ids.T
    tables = rope_constants(seq_len)
    projected = jnp.dot(normed, w_qkv, preferred_element_type=jnp.float32)
    query_proj = projected[:, :head_cols]
    key_proj = projected[:, head_cols : 2 * head_cols]
    squares = jnp.stack(
        [jnp.sum(query_proj * query_proj, axis=1), jnp.sum(key_proj * key_proj, axis=1)]
    )
    squares = small_sum(count, squares, 5)
    full_gate_up = lax.all_gather(
        expert_local, "dp", axis=0, tiled=True
    )
    pairs[1] = tie(pairs[1], squares)
    pairs.append(permute_step(pairs[1], count, 2))
    inverses = lax.rsqrt(squares / model_width + EPSILON).T
    query_row, key_row = query_scale[None, :], key_scale[None, :]
    q_rot, k_rot, value_low, mixed_low, log_totals = attend(
        projected, inverses, query_row, key_row, tables, ids_col, ids_row
    )
    for step in range(3, count):
        if step == 3:
            pairs[-1] = tie(pairs[-1], log_totals)
        pairs.append(permute_step(pairs[-1], count, step))
    branch_part = jnp.einsum(
        "sf,df->sd", mixed_low, w_o_t, preferred_element_type=jnp.float32
    ).astype(jnp.bfloat16)
    normed_two, middle = middle_exchange(
        count, branch_part, tokens, ffn_scale[None, :], ()
    )
    grad_rows = place_blocks(pairs, count)
    logits = jnp.dot(normed_two, full_router, preferred_element_type=jnp.float32)
    router_probs = jax.nn.softmax(logits, axis=-1)
    kept = kept_mask(routes)
    gate_values = router_probs * kept
    hidden_gated, grad_gate_part, grad_up_part, gate_dot = expert_parts(
        normed_two, grad_rows, gate_values, full_gate_up, full_down, ff_here
    )
    combined = expert_output(hidden_gated, full_down)
    grad_two_part, grad_experts_w = expert_products(
        hidden_gated,
        grad_gate_part,
        grad_up_part,
        normed_two,
        grad_rows,
        full_gate_up,
    )
    ffn_branch = lax.psum_scatter(
        combined, "tensor", scatter_dimension=0, tiled=True
    ).astype(jnp.float32)
    output = (middle + ffn_branch).astype(jnp.bfloat16)
    grad_probs = small_sum(count, (gate_dot * kept).T, 6).T
    grad_logits = router_probs * (
        grad_probs - jnp.sum(router_probs * grad_probs, axis=1, keepdims=True)
    )
    logits_low = grad_logits.astype(jnp.bfloat16)
    grad_router = jnp.einsum(
        "sd,se->de", normed_two, logits_low, preferred_element_type=jnp.float32
    )
    own_logits = lax.dynamic_slice_in_dim(logits_low, tensor_rank * local_rows, local_rows)
    sum_experts = lax.psum_scatter(grad_experts_w, "dp", scatter_dimension=0, tiled=True)
    router_part = jnp.einsum(
        "se,de->sd", own_logits, full_router, preferred_element_type=jnp.float32
    )
    grad_attn_rows, grad_middle, grad_ffn_gain = middle_back_exchange(
        count, grad_two_part, router_part, middle, cotangent, ffn_scale[None, :]
    )
    grad_out_w = jnp.einsum(
        "sf,sd->df", mixed_low, grad_attn_rows, preferred_element_type=jnp.float32
    ).astype(jnp.bfloat16)
    grad_mixed = jnp.dot(grad_attn_rows, w_o_t, preferred_element_type=jnp.float32).astype(
        jnp.bfloat16
    )
    query_scaled, key_scaled, grad_value_low, dots, grad_query_gain, grad_key_gain = attend_back(
        q_rot,
        k_rot,
        value_low,
        grad_mixed,
        after(log_totals, ffn_branch),
        projected,
        inverses,
        query_row,
        key_row,
        tables,
        ids_col,
        ids_row,
    )
    dots = small_sum(count, dots.T, 7).T / model_width
    query_inv, key_inv = inverses[:, 0:1], inverses[:, 1:2]
    grad_query_proj = (
        query_inv * (query_scaled - query_proj * query_inv * dots[:, 0:1])
    ).astype(jnp.bfloat16)
    grad_key_proj = (key_inv * (key_scaled - key_proj * key_inv * dots[:, 1:2])).astype(
        jnp.bfloat16
    )
    grad_qkv = jnp.concatenate([grad_query_proj, grad_key_proj, grad_value_low], axis=1)
    grad_qkv_w = (
        jnp.einsum("sd,sf->df", unit_rows, grad_qkv, preferred_element_type=jnp.float32)
        * attn_scale[:, None]
    ).astype(jnp.bfloat16)
    grad_router_wide = jnp.pad(grad_router, ((0, 0), (0, 128 - EXPERTS))).astype(jnp.bfloat16)
    sum_heads = lax.psum_scatter(
        jnp.concatenate([grad_qkv_w, grad_out_w, grad_router_wide], axis=1),
        "dp",
        scatter_dimension=0,
        tiled=True,
    ).astype(jnp.float32)
    grad_normed_part = jnp.einsum(
        "sf,df->sd", grad_qkv, w_qkv, preferred_element_type=jnp.float32
    ).astype(jnp.bfloat16)
    grad_source, grad_attn_gain = end_exchange(
        count, grad_normed_part, grad_middle, tokens, attn_scale[None, :], (sum_experts,)
    )
    zero_cols = jnp.zeros((model_width,), jnp.float32)
    query_gain_full = lax.dynamic_update_slice_in_dim(zero_cols, grad_query_gain[0], col_start, 0)
    key_gain_full = lax.dynamic_update_slice_in_dim(zero_cols, grad_key_gain[0], col_start, 0)
    gain_stack = jnp.stack([grad_attn_gain, query_gain_full, key_gain_full, grad_ffn_gain])
    dp_count = lax.axis_size("dp")
    gain_width = model_width // (dp_count * count)
    gain_blocks = gain_stack.reshape(4, dp_count * count, gain_width).transpose(1, 0, 2)
    gain_blocks = jnp.pad(gain_blocks, ((0, 0), (0, 4), (0, 128 - gain_width)))
    gain_sums = scatter_sum(dp_count, count, gain_blocks, 8)[:4, :gain_width]
    sum_heads = after(sum_heads, grad_attn_gain[None])
    sum_qkv = sum_heads[:, : 3 * head_cols]
    sum_out = sum_heads[:, 3 * head_cols : 4 * head_cols]
    sum_router = sum_heads[:, 4 * head_cols : 4 * head_cols + EXPERTS]
    grad_gate, grad_up, grad_down = split_experts(sum_experts, ff_here)
    return (
        output,
        grad_source,
        gain_sums[0],
        gain_sums[1],
        gain_sums[2],
        sum_qkv[:, :head_cols],
        sum_qkv[:, head_cols : 2 * head_cols],
        sum_qkv[:, 2 * head_cols :],
        sum_out.T.astype(jnp.float32),
        gain_sums[3],
        sum_router,
        grad_gate,
        grad_up,
        grad_down,
    )


def solution(mesh):
    placed = (
        P(("dp", "tensor"), None),
        P(("dp", "tensor"), None),
        P("dp", None),
        P("dp", None),
        P("dp"),
        P("dp"),
        P("dp"),
        P("dp", "tensor"),
        P("dp", "tensor"),
        P("dp", "tensor"),
        P("tensor", "dp"),
        P("dp"),
        P("dp", None),
        P(None, "dp", "tensor"),
        P(None, "dp", "tensor"),
        P(None, "tensor", "dp"),
    )
    return jax.shard_map(
        local,
        mesh=mesh,
        in_specs=placed,
        out_specs=(
            P(("dp", "tensor"), None),
            P(("dp", "tensor"), None),
            P(("dp", "tensor")),
            P(("dp", "tensor")),
            P(("dp", "tensor")),
            P("dp", "tensor"),
            P("dp", "tensor"),
            P("dp", "tensor"),
            P("tensor", "dp"),
            P(("dp", "tensor")),
            P("dp", None),
            P(None, "dp", "tensor"),
            P(None, "dp", "tensor"),
            P(None, "tensor", "dp"),
        ),
        check_vma=False,
    )
```
